32 devices in a mesh: row: 8 (over y, x, core), col: 4 (over z).
Axes of the slice: x: 2, y: 2, z: 4, core: 2. Of those that a mesh axis runs over, the one named last changes fastest.
Arguments:
- fast_pos: float32 [3, 4096], P(None, ('row', 'col')), may hold values from 0 to 1
- fast_vel: float32 [3, 4096], P(None, ('row', 'col')), may hold values from -5 to 5
- fast_charge: float32 [4096], replicated, may hold values from -4 to 4
- fast_owner: int32 [4096], replicated, may hold values from 0 to 1023, as said below
- exclusions: int32 [4096, 4], replicated, may hold values from 0 to 4095, as said below
- slow_pos: float32 [3, 32, 32, 128], P(None, 'row', 'col'), may hold values from 0 to 1
- slow_vel: float32 [3, 32, 32, 128], P(None, 'row', 'col'), may hold values from -5 to 5
- slow_charge: float32 [32, 32, 128], P('row', 'col'), may hold values from -4 to 4
- neighbours: int32 [32, 32, 5], P('row', 'col'), may hold values from 0 to 24, all different within a row
Outputs:
- fast_pos_out: float32 [3, 4096], P(None, ('row', 'col'))
- fast_vel_out: float32 [3, 4096], P(None, ('row', 'col'))
- slow_pos_out: float32 [3, 32, 32, 128], P(None, 'row', 'col')
- slow_vel_out: float32 [3, 32, 32, 128], P(None, 'row', 'col')
The draws below stay inside these ranges and needn't reach their ends.
Inputs may be any that keep to these rules, and one draw needn't show every extreme that they name: `fast_owner`: atoms a and b with a % (256) == b % (256) share an owner. `exclusions`: the partners of atom a are atoms b != a with b % (256) == a % 256; a partner may repeat. `neighbours`: the entries of one cell are distinct.
All inputs are finite; a program needn't handle non-finite values.
Results may differ from the reference program's by a relative error of at most 0.0003.
Values sent between devices are 32-bit elements; how exact they have to be, the bound alone decides.
No kernel may reach another device: no remote copies, remote signals or barrier semaphores. Data moves between devices by JAX's collectives and lax.ppermute only.
A program may use at most 64 MiB of HBM per device.

```python
import jax
import jax.numpy as jnp
from jax import lax

FAST = 4096
CELL = 128
NBR = 5
INNER = 4
OUTER = 1
CELL_ROWS = 32
CELL_COLS = 32


def draw_fast_owner(key, part):
    molecule = jax.random.randint(key, (FAST // 16,), 0, CELL_ROWS * CELL_COLS, dtype=jnp.int32)
    return jnp.tile(molecule, 16)


def draw_exclusions(key, part):
    groups = FAST // 16
    offset = jax.random.randint(key, (FAST, 4), 1, 16, dtype=jnp.int32)
    atoms = jnp.arange(FAST, dtype=jnp.int32)
    member = atoms // groups
    return (atoms % groups)[:, None] + groups * ((member[:, None] + offset) % 16)


def shard_levels(own_key, extent, split, low, high):
    level, own = 1.0, jax.random.fold_in(own_key, 6)
    for dim, blocks in split:
        heights = jnp.exp(jax.random.uniform(jax.random.fold_in(own, dim), (blocks,), jnp.float32, low / len(split), high / len(split)))
        level = level * jnp.repeat(heights, extent[dim] // blocks).reshape([-1 if axis == dim else 1 for axis in range(len(extent))])
    return level


def distinct(own_key, rows, amount, top, lift):
    ranking = jax.random.permutation(jax.random.fold_in(own_key, 1), amount)
    pull = ranking
    for power in range(3):
        pull = pull * pull // amount
    pull = pull * lift // amount
    chance = jax.random.randint(jax.random.fold_in(own_key, 2), (rows, amount), 0, 4096) + pull
    sure = jax.random.permutation(jax.random.fold_in(own_key, 3), rows)[jnp.arange(amount) % rows]
    chance = jnp.where(jnp.arange(rows)[:, None] == sure[None, :], 1 << 14, chance)
    priority = chance * amount + jnp.arange(amount)
    return lax.top_k(priority.astype(jnp.int32), top)[1].astype(jnp.int32)


def bell_draw(own_key, dims, width, limit, cuts=(), held_as=jnp.bfloat16):
    level = shard_levels(own_key, dims, cuts, -0.22, 0.18) if cuts else 1.0
    values = jax.random.normal(own_key, dims, jnp.float32) * width * level
    return jnp.minimum(jnp.maximum(values, -limit), limit).astype(held_as)


def setup_inputs(seed: int = 0) -> dict:
    seeds = jax.random.split(jax.random.key(seed), 10)
    fast_pos = jnp.clip(1.0 * jax.random.uniform(seeds[0], (3, FAST), jnp.float32) ** shard_levels(seeds[0], (3, FAST), ((1, 32),), -0.2, 0.2), 0.0, 1.0)
    fast_vel = bell_draw(seeds[1], (3, FAST), 1.0, 5.0, ((1, 32),), jnp.float32)
    fast_charge = bell_draw(seeds[2], (FAST,), 1.0, 4.0, (), jnp.float32)
    fast_owner = draw_fast_owner(jax.random.fold_in(seeds[9], 71), 0)
    exclusions = draw_exclusions(jax.random.fold_in(seeds[9], 71), 0)
    slow_pos = jnp.clip(1.0 * jax.random.uniform(seeds[5], (3, CELL_ROWS, CELL_COLS, CELL), jnp.float32) ** shard_levels(seeds[5], (3, CELL_ROWS, CELL_COLS, CELL), ((1, 8), (2, 4)), -0.2, 0.2), 0.0, 1.0)
    slow_vel = bell_draw(seeds[6], (3, CELL_ROWS, CELL_COLS, CELL), 1.0, 5.0, ((1, 8), (2, 4)), jnp.float32)
    slow_charge = bell_draw(seeds[7], (CELL_ROWS, CELL_COLS, CELL), 1.0, 4.0, ((0, 8), (1, 4)), jnp.float32)
    neighbours = distinct(seeds[8], CELL_ROWS * CELL_COLS, 25, NBR, 0).reshape((CELL_ROWS, CELL_COLS, NBR))
    return {"fast_pos": fast_pos, "fast_vel": fast_vel, "fast_charge": fast_charge, "fast_owner": fast_owner, "exclusions": exclusions, "slow_pos": slow_pos, "slow_vel": slow_vel, "slow_charge": slow_charge, "neighbours": neighbours}


fast_coupling = 1.0
slow_coupling = 0.1
outer_dt = 0.2

def owner_coords(owner, total_cols):
    grid_row = (owner // total_cols).astype(jnp.float32)
    grid_col = (owner % total_cols).astype(jnp.float32)
    return jnp.stack([grid_row, grid_col, jnp.zeros_like(grid_row)])

def pair_fast(pos_a, cell_a, charge_a, exclude_a, pos_b, cell_b, charge_b, index_b):
    delta = pos_a[:, :, None] - pos_b[:, None, :] + (cell_a[:, :, None] - cell_b[:, None, :])
    dist_sq = lax.optimization_barrier(jnp.sum(delta * delta, axis=0)) + 1.0
    inverse = 1.0 / (dist_sq * jnp.sqrt(dist_sq))
    barred = jnp.any(exclude_a[:, :, None] == index_b[None, None, :], axis=1)
    weight = jnp.where(barred, jnp.float32(0.0), charge_a[:, None] * charge_b[None, :] * inverse)
    return fast_coupling * lax.optimization_barrier(jnp.sum(weight[None] * delta, axis=2))

def slow_cells(own, views, lists):
    force = jnp.zeros((3,) + own.shape[1:], jnp.float32)
    offsets = jnp.arange(25, dtype=jnp.int32)
    for slot in range(lists.shape[-1]):
        chosen = lists[..., slot]
        pick = (chosen[..., None] == offsets).astype(jnp.float32)
        other = jnp.einsum('abo,oxabn->xabn', pick, views, precision=lax.Precision.HIGHEST)
        shift_row = (chosen // 5 - 2).astype(jnp.float32)
        shift_col = (chosen % 5 - 2).astype(jnp.float32)
        shift = jnp.stack([shift_row, shift_col, jnp.zeros_like(shift_row)])
        delta = own[0:3, :, :, :, None] - (other[0:3, :, :, None, :] + shift[:, :, :, None, None])
        dist_sq = lax.optimization_barrier(jnp.sum(delta * delta, axis=0)) + 0.5
        inverse = 1.0 / (dist_sq * jnp.sqrt(dist_sq))
        weight = other[3][:, :, None, :] * inverse
        force = force + lax.optimization_barrier(jnp.sum(weight[None] * delta, axis=-1))
    return slow_coupling * own[3][None] * force

def fast_from_cells(frac, charge, picked):
    delta = frac[:, :, None] - picked[0:3]
    dist_sq = lax.optimization_barrier(jnp.sum(delta * delta, axis=0)) + 0.5
    inverse = 1.0 / (dist_sq * jnp.sqrt(dist_sq))
    weight = picked[3] * inverse
    return slow_coupling * charge[None, :] * lax.optimization_barrier(jnp.sum(weight[None] * delta, axis=-1))

def reference(fast_pos, fast_vel, fast_charge, fast_owner, exclusions, slow_pos, slow_vel, slow_charge, neighbours):
    coords = owner_coords(fast_owner, CELL_COLS)
    all_index = jnp.arange(FAST, dtype=jnp.int32)

    def fast_force(frac):

        def one_block(start):
            pos_a = lax.dynamic_slice_in_dim(frac, start, 256, 1)
            cell_a = lax.dynamic_slice_in_dim(coords, start, 256, 1)
            charge_a = lax.dynamic_slice_in_dim(fast_charge, start, 256, 0)
            exclude_a = lax.dynamic_slice_in_dim(exclusions, start, 256, 0)
            return pair_fast(pos_a, cell_a, charge_a, exclude_a, frac, coords, fast_charge, all_index)
        starts = jnp.arange(FAST // 256, dtype=jnp.int32) * 256
        blocks = lax.map(one_block, starts)
        return jnp.transpose(blocks, (1, 0, 2)).reshape(3, FAST)
    grid_row = fast_owner // CELL_COLS
    grid_col = fast_owner % CELL_COLS

    def slow_both(spos, frac):
        data = jnp.concatenate([spos, slow_charge[None]], axis=0)
        padded = jnp.pad(data, ((0, 0), (2, 2), (2, 2), (0, 0)), mode='wrap')

        def one_row(row_start):
            slab = lax.dynamic_slice_in_dim(padded, row_start, 5, 1)
            views = jnp.stack([slab[:, o // 5:o // 5 + 1, o % 5:o % 5 + CELL_COLS] for o in range(25)])
            own = slab[:, 2:3, 2:2 + CELL_COLS]
            lists = lax.dynamic_slice_in_dim(neighbours, row_start, 1, 0)
            return slow_cells(own, views, lists)[:, 0]
        rows = lax.map(one_row, jnp.arange(CELL_ROWS, dtype=jnp.int32))
        cell_force = jnp.transpose(rows, (1, 0, 2, 3))
        picked = data[:, grid_row, grid_col, :]
        return (cell_force, fast_from_cells(frac, fast_charge, picked))
    half_outer = 0.5 * outer_dt
    inner_dt = outer_dt / INNER
    fast_acc = fast_force(fast_pos)
    slow_acc, env_acc = slow_both(slow_pos, fast_pos)
    for outer_step in range(OUTER):
        slow_vel = slow_vel + half_outer * slow_acc
        fast_vel = fast_vel + half_outer * env_acc
        for inner_step in range(INNER):
            fast_vel = fast_vel + 0.5 * inner_dt * fast_acc
            fast_pos = fast_pos + inner_dt * fast_vel
            fast_acc = fast_force(fast_pos)
            fast_vel = fast_vel + 0.5 * inner_dt * fast_acc
        slow_pos = slow_pos + outer_dt * slow_vel
        slow_acc, env_acc = slow_both(slow_pos, fast_pos)
        slow_vel = slow_vel + half_outer * slow_acc
        fast_vel = fast_vel + half_outer * env_acc
    return (fast_pos, fast_vel, slow_pos, slow_vel)
```

```python
import functools

import jax
import jax.numpy as jnp
from jax import lax
from jax.experimental import pallas as pl
from jax.experimental.pallas import tpu as pltpu
from jax.sharding import PartitionSpec as P

CELL = 128
INNER = 4
GROUPS = 256

fast_coupling = 1.0
slow_coupling = 0.1
outer_dt = 0.2
half_outer = 0.5 * outer_dt
inner_dt = outer_dt / INNER

BOTH = ("row", "col")
F32 = jnp.float32
BF16 = jnp.bfloat16
LANES = 128
ENV_UNROLL = 4
VMEM = pl.BlockSpec(memory_space=pltpu.VMEM)
SMEM = pl.BlockSpec(memory_space=pltpu.SMEM)


def sds(shape, dtype=F32):
    return jax.ShapeDtypeStruct(shape, dtype)


def fast_rows(g_ref, cor_ref, q_ref, exm_ref, own, planes, cols, sums):
    count = g_ref.shape[0]
    members = exm_ref.shape[0]
    for c in range(3):
        x = g_ref[:, c, :]
        planes[c] = x + cor_ref[c] if c < 2 else x
    own_rows = [planes[c, pl.ds(own, 1), :] for c in range(3)]
    for c in range(3):
        cols[c] = jnp.transpose(jnp.broadcast_to(own_rows[c], (LANES, LANES)))
    unroll = 2

    def body(i, carry):
        at = [pl.ds(pl.multiple_of((i * unroll + u) * 8, 8), 8) for u in range(unroll)]
        a = [[cols[c, at[u], :] for c in range(3)] for u in range(unroll)]
        acc = [[jnp.zeros((8, LANES), F32) for _ in range(3)] for _ in range(unroll)]
        for b in range(count):
            y = [jnp.broadcast_to(planes[c, b : b + 1, :], (8, LANES)) for c in range(3)]
            qb = jnp.broadcast_to(q_ref[b : b + 1, :], (8, LANES))
            for u in range(unroll):
                d = [a[u][c] - y[c] for c in range(3)]
                r = lax.rsqrt(d[0] * d[0] + d[1] * d[1] + d[2] * d[2] + 1.0)
                w = (qb * r) * (r * r)
                for c in range(3):
                    acc[u][c] = acc[u][c] + w * d[c]
        for u in range(unroll):
            for c in range(3):
                sums[c, at[u], :] = acc[u][c]
        return carry

    lax.fori_loop(0, LANES // (8 * unroll), body, 0)
    step = GROUPS // LANES
    part = pl.ds(lax.rem(own, step), members, stride=step)
    d = [own_rows[c] - planes[c, part, :] for c in range(3)]
    r = lax.rsqrt(d[0] * d[0] + d[1] * d[1] + d[2] * d[2] + 1.0)
    w = (exm_ref[...] * q_ref[part, :]) * (r * (r * r))
    ones = jnp.ones((8, LANES), F32)
    scale = fast_coupling * q_ref[pl.ds(own, 1), :]
    out = []
    for c in range(3):
        total = lax.dot_general(
            ones, sums[c], (((1,), (1,)), ((), ())),
            precision=lax.Precision.HIGHEST, preferred_element_type=F32,
        )[0:1, :]
        out.append(scale * (total - jnp.sum(w * d[c], axis=0, keepdims=True)))
    return out


def fast_only_kernel(own_ref, g_ref, cor_ref, q_ref, exm_ref, f_ref, planes, cols, sums):
    rows = fast_rows(g_ref, cor_ref, q_ref, exm_ref, own_ref[0], planes, cols, sums)
    for c in range(3):
        f_ref[c : c + 1, :] = rows[c]


def fast_step_kernel(
    own_ref, g_ref, cor_ref, q_ref, exm_ref, v_ref, send_ref, p_out, v_out, planes, cols, sums
):
    own = own_ref[0]
    rows = fast_rows(g_ref, cor_ref, q_ref, exm_ref, own, planes, cols, sums)
    count = send_ref.shape[0]
    for c in range(3):
        v = v_ref[c : c + 1, :] + inner_dt * rows[c]
        p = g_ref[pl.ds(own, 1), c, :] + inner_dt * v
        v_out[c : c + 1, :] = v
        p_out[c : c + 1, :] = p
        send_ref[:, c, :] = jnp.broadcast_to(p, (count, LANES))


def fast_cost(count):
    pairs = count * LANES * LANES
    return pl.CostEstimate(flops=19 * pairs, transcendentals=pairs, bytes_accessed=count * 4096)


def fast_scratch(count):
    return [
        pltpu.VMEM((3, count, LANES), F32),
        pltpu.VMEM((3, LANES, LANES), F32),
        pltpu.VMEM((3, LANES, LANES), F32),
    ]


def fast_only(own, g, cor, q, exm):
    count = g.shape[0]
    return pl.pallas_call(
        fast_only_kernel,
        out_shape=sds((3, LANES)),
        in_specs=[SMEM] + [VMEM] * 4,
        out_specs=VMEM,
        scratch_shapes=fast_scratch(count),
        cost_estimate=fast_cost(count),
        name="fast_only",
        compiler_params=pltpu.CompilerParams(vmem_limit_bytes=2 << 20),
    )(own, g, cor, q, exm)


def fast_step(own, g, cor, q, exm, v):
    count = g.shape[0]
    return pl.pallas_call(
        fast_step_kernel,
        out_shape=(sds((count, 3, LANES)), sds((3, LANES)), sds((3, LANES))),
        in_specs=[SMEM] + [VMEM] * 5,
        out_specs=(VMEM,) * 3,
        scratch_shapes=fast_scratch(count),
        cost_estimate=fast_cost(count),
        name="fast_step",
        compiler_params=pltpu.CompilerParams(vmem_limit_bytes=2 << 20),
    )(own, g, cor, q, exm, v)


def list_kernel(total_cols, cell_rows, cell_cols, owner_ref, base_ref, list_ref, count_ref):
    row0, col0 = base_ref[0], base_ref[1]
    step = GROUPS // LANES

    def body(i, n):
        cell = owner_ref[i]
        r = lax.div(cell, total_cols) - row0
        c = lax.rem(cell, total_cols) - col0
        inside = (r >= 0) & (r < cell_rows) & (c >= 0) & (c < cell_cols)
        list_ref[0, n] = lax.div(i, LANES)
        list_ref[1, n] = lax.rem(i, LANES)
        list_ref[2, n] = r * cell_cols + c
        return n + inside.astype(jnp.int32)

    n = lax.fori_loop(0, GROUPS, body, jnp.int32(0))
    count_ref[0] = n
    for k in range(ENV_UNROLL):
        list_ref[0, n + k] = 0
        list_ref[1, n + k] = -1
        list_ref[2, n + k] = 0


def env_list(owner, base, total_cols, cell_rows, cell_cols):
    return pl.pallas_call(
        functools.partial(list_kernel, total_cols, cell_rows, cell_cols),
        out_shape=(sds((3, GROUPS + ENV_UNROLL), jnp.int32), sds((1,), jnp.int32)),
        in_specs=[SMEM, SMEM],
        out_specs=(SMEM, SMEM),
        name="env_list",
        compiler_params=pltpu.CompilerParams(vmem_limit_bytes=2 << 20),
    )(owner, base)


def env_kernel(list_ref, count_ref, g_ref, cells_ref, out_ref, planes, sums):
    step = GROUPS // LANES
    members = g_ref.shape[0] // step
    for c in range(3):
        for h in range(step):
            planes[c, h] = g_ref[pl.ds(h, members, stride=step), c, :]
    sums[...] = jnp.zeros_like(sums)
    lane = lax.broadcasted_iota(jnp.int32, (members, LANES), 1)

    def body(t, carry):
        for u in range(ENV_UNROLL):
            n = t * ENV_UNROLL + u
            h = list_ref[0, n]
            here = lane == list_ref[1, n]
            cell = cells_ref[list_ref[2, n]]
            d = []
            for c in range(3):
                x = jnp.sum(jnp.where(here, planes[c, h], 0.0), axis=1, keepdims=True)
                d.append(x - cell[c : c + 1, :])
            r = lax.rsqrt(d[0] * d[0] + d[1] * d[1] + d[2] * d[2] + 0.5)
            w = (cell[3:4, :] * r) * (r * r)
            for c in range(3):
                f = jnp.sum(w * d[c], axis=1, keepdims=True)
                sums[c, h] = sums[c, h] + jnp.where(here, f, 0.0)
        return carry

    lax.fori_loop(0, lax.div(count_ref[0] + (ENV_UNROLL - 1), ENV_UNROLL), body, 0)
    for c in range(3):
        for h in range(step):
            out_ref[pl.ds(h, members, stride=step), c, :] = sums[c, h]


def env(lists, g, cells):
    count = g.shape[0]
    step = GROUPS // LANES
    members = count // step
    return pl.pallas_call(
        env_kernel,
        out_shape=sds((count, 3, LANES)),
        in_specs=[SMEM, SMEM, VMEM, VMEM],
        out_specs=VMEM,
        scratch_shapes=[
            pltpu.VMEM((3, step, members, LANES), F32),
            pltpu.VMEM((3, step, members, LANES), F32),
        ],
        cost_estimate=pl.CostEstimate(flops=2_000_000, transcendentals=60000, bytes_accessed=200000),
        name="env",
        compiler_params=pltpu.CompilerParams(vmem_limit_bytes=2 << 20),
    )(*lists, g, cells)


def kick_kernel(own_ref, e_ref, f_ref, q_ref, p_ref, v_ref, send_ref, p_out, v_out):
    scale = slow_coupling * q_ref[pl.ds(own_ref[0], 1), :]
    count = send_ref.shape[0]
    for c in range(3):
        e = scale * jnp.sum(e_ref[:, c, :], axis=0, keepdims=True)
        v = v_ref[c : c + 1, :] + half_outer * e + 0.5 * inner_dt * f_ref[c : c + 1, :]
        p = p_ref[c : c + 1, :] + inner_dt * v
        v_out[c : c + 1, :] = v
        p_out[c : c + 1, :] = p
        send_ref[:, c, :] = jnp.broadcast_to(p, (count, LANES))


def kick(own, e, f, q, p, v):
    count = e.shape[0]
    return pl.pallas_call(
        kick_kernel,
        out_shape=(sds((count, 3, LANES)), sds((3, LANES)), sds((3, LANES))),
        in_specs=[SMEM] + [VMEM] * 5,
        out_specs=(VMEM,) * 3,
        name="kick",
        compiler_params=pltpu.CompilerParams(vmem_limit_bytes=2 << 20),
    )(own, e, f, q, p, v)


def last_kick_kernel(own_ref, e_ref, f_ref, q_ref, v_ref, v_out):
    scale = slow_coupling * q_ref[pl.ds(own_ref[0], 1), :]
    for c in range(3):
        e = scale * jnp.sum(e_ref[:, c, :], axis=0, keepdims=True)
        v_out[c : c + 1, :] = (
            v_ref[c : c + 1, :] + 0.5 * inner_dt * f_ref[c : c + 1, :] + half_outer * e
        )


def last_kick(own, e, f, q, v):
    return pl.pallas_call(
        last_kick_kernel,
        out_shape=sds((3, LANES)),
        in_specs=[SMEM] + [VMEM] * 4,
        out_specs=VMEM,
        name="last_kick",
        compiler_params=pltpu.CompilerParams(vmem_limit_bytes=2 << 20),
    )(own, e, f, q, v)


def split3(x):
    hi = x.astype(BF16).astype(F32)
    rest = x - hi
    mid = rest.astype(BF16).astype(F32)
    return hi, mid, rest - mid


def slow_kernel(first, nb_ref, tab_ref, vel_ref, *refs):
    if first:
        vel_out, pos_out, cell_out, feat, vals = refs
    else:
        vel_out, feat, vals = refs
    all_rows, all_cols = tab_ref.shape[0], tab_ref.shape[1]
    cell_rows, cell_cols = vel_ref.shape[1], vel_ref.shape[2]
    slots = nb_ref.shape[1]
    row8 = lax.broadcasted_iota(jnp.int32, (8, LANES), 0)

    def load8(r, c):
        t = tab_ref[r, c]
        return jnp.concatenate([t, jnp.zeros_like(t)], axis=0)

    def one_cell(n):
        t = load8(lax.div(n, all_cols), lax.rem(n, all_cols))
        pos = jnp.where(row8 < 3, t, 0.0)
        norm = jnp.sum(pos * pos, axis=0, keepdims=True) + 0.5
        b = jnp.where(row8 == 3, 1.0, jnp.where(row8 == 4, norm, -2.0 * pos))
        hi, mid, lo = split3(b)
        wide = jnp.concatenate([hi, mid, hi, lo, mid, hi], axis=0)
        feat[n] = jnp.transpose(wide).astype(BF16)
        charge = t[3:4, :]
        u = jnp.where(row8 == 3, charge, pos * charge)
        hi = u.astype(BF16).astype(F32)
        vals[n] = jnp.concatenate([hi, u - hi], axis=0).astype(BF16)

    def prepare(i, carry):
        for u in range(4):
            one_cell(i * 4 + u)
        return carry

    lax.fori_loop(0, all_rows * all_cols // 4, prepare, 0)

    def body(n, carry):
        r = lax.div(n, cell_cols)
        c = lax.rem(n, cell_cols)
        t = load8(r + 2, c + 2)
        pos = jnp.where(row8 < 3, t, 0.0)
        force = jnp.zeros((8, LANES), F32)
        for k in range(slots):
            o = nb_ref[n, k]
            dr = lax.div(o, 5)
            dc = lax.rem(o, 5)
            shift = jnp.where(
                row8 == 0, (dr - 2).astype(F32), jnp.where(row8 == 1, (dc - 2).astype(F32), 0.0)
            )
            x = pos - shift
            norm = jnp.sum(x * x, axis=0, keepdims=True)
            a = jnp.where(row8 == 3, norm, jnp.where(row8 == 4, 1.0, x))
            hi, mid, lo = split3(a)
            wide = jnp.concatenate([hi, hi, mid, hi, mid, lo], axis=0).astype(BF16)
            other = (r + dr) * all_cols + c + dc
            s = jnp.dot(feat[other], wide, preferred_element_type=F32)
            inv = lax.rsqrt(s)
            w = inv * (inv * inv)
            whi = w.astype(BF16)
            wlo = (w - whi.astype(F32)).astype(BF16)
            g = vals[other]
            both = jnp.dot(g, whi, preferred_element_type=F32) + jnp.dot(
                g, wlo, preferred_element_type=F32
            )
            total = both[0:8] + both[8:16]
            force = force + (x * total[3:4, :] - total)
        force = slow_coupling * t[3:4, :] * force
        for x in range(3):
            here = (x, r, pl.ds(c, 1), slice(None))
            v = vel_ref[here] + half_outer * force[x : x + 1]
            vel_out[here] = v
            if first:
                p = t[x : x + 1] + outer_dt * v
                pos_out[here] = p
                cell_out[n, x : x + 1, :] = p
        if first:
            cell_out[n, 3:4, :] = t[3:4]
        return carry

    lax.fori_loop(0, cell_rows * cell_cols, body, 0)


def slow(first, nb, tab, vel):
    cells = tab.shape[0] * tab.shape[1]
    own = vel.shape[1] * vel.shape[2]
    out = (sds(vel.shape), sds(vel.shape), sds((own, 4, CELL))) if first else sds(vel.shape)
    pairs = own * nb.shape[1] * CELL * CELL
    return pl.pallas_call(
        functools.partial(slow_kernel, first),
        out_shape=out,
        in_specs=[SMEM, VMEM, VMEM],
        out_specs=(VMEM,) * 3 if first else VMEM,
        scratch_shapes=[pltpu.VMEM((cells, CELL, 48), BF16), pltpu.VMEM((cells, 16, CELL), BF16)],
        cost_estimate=pl.CostEstimate(
            flops=19 * pairs, transcendentals=pairs, bytes_accessed=1_000_000
        ),
        name="slow",
        compiler_params=pltpu.CompilerParams(vmem_limit_bytes=8 << 20),
    )(nb, tab, vel)


def with_halo(x, sides, width):
    for axis, dim in sides:
        count, length = (lax.axis_size(axis), x.shape[dim])
        up = [(i, (i + 1) % count) for i in range(count)]
        down = [(j, i) for i, j in up]
        last = lax.slice_in_dim(x, length - width, length, axis=dim)
        initial = lax.slice_in_dim(x, 0, width, axis=dim)
        before = lax.ppermute(last, axis, up)
        after = lax.ppermute(initial, axis, down)
        x = jnp.concatenate([before, x, after], axis=dim)
    return x


def exchange(x):
    return lax.all_to_all(x, BOTH, 0, 0)


def per_device(
    fast_pos, fast_vel, fast_charge, fast_owner, exclusions,
    slow_pos, slow_vel, slow_charge, neighbours,
):
    if fast_pos.shape[1] != LANES:
        return general(
            fast_pos, fast_vel, fast_charge, fast_owner, exclusions,
            slow_pos, slow_vel, slow_charge, neighbours,
        )
    row_count, col_count = lax.axis_size("row"), lax.axis_size("col")
    row_index, col_index = lax.axis_index("row"), lax.axis_index("col")
    flat = row_index * col_count + col_index
    count = row_count * col_count
    piece = fast_pos.shape[1]
    cell_rows, cell_cols = slow_pos.shape[1], slow_pos.shape[2]
    total_cols = cell_cols * col_count
    own = jnp.reshape(flat, (1,)).astype(jnp.int32)

    g = exchange(jnp.broadcast_to(fast_pos[None], (count, 3, piece)))

    owner = fast_owner.reshape(count, piece)
    cor = jnp.stack([owner // total_cols, owner % total_cols]).astype(F32)
    q = fast_charge.reshape(count, piece)
    members = fast_charge.shape[0] // GROUPS
    ex = lax.dynamic_slice_in_dim(exclusions, flat * piece, piece, 0) // GROUPS
    exm = jnp.any(
        ex[None] == jnp.arange(members, dtype=jnp.int32)[:, None, None], axis=2
    ).astype(F32)
    base = jnp.stack([row_index * cell_rows, col_index * cell_cols]).astype(jnp.int32)
    lists = env_list(fast_owner[:GROUPS], base, total_cols, cell_rows, cell_cols)

    cells = jnp.concatenate([slow_pos, slow_charge[None]], axis=0).transpose(1, 2, 0, 3)
    sides = (("row", 0), ("col", 1))
    nb = neighbours.reshape(cell_rows * cell_cols, -1)
    slow_vel, slow_pos, cells2 = slow(True, nb, with_halo(cells, sides, 2), slow_vel)
    tab2 = with_halo(cells2.reshape(cells.shape), sides, 2)
    slow_vel = slow(False, nb, tab2, slow_vel)

    back = exchange(env(lists, g, cells.reshape(cells2.shape)))
    f = fast_only(own, g, cor, q, exm)
    send, p, v = kick(own, back, f, q, fast_pos, fast_vel)
    for _ in range(INNER - 1):
        g = exchange(send)
        send, p, v = fast_step(own, g, cor, q, exm, v)
    g = exchange(send)
    back = exchange(env(lists, g, cells2))
    f = fast_only(own, g, cor, q, exm)
    v = last_kick(own, back, f, q, v)
    return (p, v, slow_pos, slow_vel)


def owner_coords(owner, total_cols):
    grid_row = (owner // total_cols).astype(jnp.float32)
    grid_col = (owner % total_cols).astype(jnp.float32)
    return jnp.stack([grid_row, grid_col, jnp.zeros_like(grid_row)])


def pair_fast(pos_a, cell_a, charge_a, exclude_a, pos_b, cell_b, charge_b, index_b):
    delta = pos_a[:, :, None] - pos_b[:, None, :] + (cell_a[:, :, None] - cell_b[:, None, :])
    dist_sq = jnp.sum(delta * delta, axis=0) + 1.0
    inverse = 1.0 / (dist_sq * jnp.sqrt(dist_sq))
    barred = jnp.any(exclude_a[:, :, None] == index_b[None, None, :], axis=1)
    weight = jnp.where(barred, jnp.float32(0.0), charge_a[:, None] * charge_b[None, :] * inverse)
    return fast_coupling * jnp.sum(weight[None] * delta, axis=2)


def slow_cells(own, views, lists):
    force = jnp.zeros((3,) + own.shape[1:], jnp.float32)
    offsets = jnp.arange(25, dtype=jnp.int32)
    for slot in range(lists.shape[-1]):
        chosen = lists[..., slot]
        pick = (chosen[..., None] == offsets).astype(jnp.float32)
        other = jnp.einsum("abo,oxabn->xabn", pick, views, precision=lax.Precision.HIGHEST)
        shift_row = (chosen // 5 - 2).astype(jnp.float32)
        shift_col = (chosen % 5 - 2).astype(jnp.float32)
        shift = jnp.stack([shift_row, shift_col, jnp.zeros_like(shift_row)])
        delta = own[0:3, :, :, :, None] - (other[0:3, :, :, None, :] + shift[:, :, :, None, None])
        dist_sq = jnp.sum(delta * delta, axis=0) + 0.5
        inverse = 1.0 / (dist_sq * jnp.sqrt(dist_sq))
        weight = other[3][:, :, None, :] * inverse
        force = force + jnp.sum(weight[None] * delta, axis=-1)
    return slow_coupling * own[3][None] * force


def fast_from_cells(frac, charge, picked):
    delta = frac[:, :, None] - picked[0:3]
    dist_sq = jnp.sum(delta * delta, axis=0) + 0.5
    inverse = 1.0 / (dist_sq * jnp.sqrt(dist_sq))
    weight = picked[3] * inverse
    return slow_coupling * charge[None, :] * jnp.sum(weight[None] * delta, axis=-1)


def general(
    fast_pos,
    fast_vel,
    fast_charge,
    fast_owner,
    exclusions,
    slow_pos,
    slow_vel,
    slow_charge,
    neighbours,
):
    row_count = lax.axis_size("row")
    col_count = lax.axis_size("col")
    row_index = lax.axis_index("row")
    col_index = lax.axis_index("col")
    flat_index = row_index * col_count + col_index
    piece = fast_pos.shape[1]
    cell_rows = slow_pos.shape[1]
    cell_cols = slow_pos.shape[2]
    total_cols = cell_cols * col_count
    coords = owner_coords(fast_owner, total_cols)
    block_width = col_count * piece
    block_start = row_index * block_width
    rows_cells = lax.dynamic_slice_in_dim(coords, block_start, block_width, 1)
    rows_charge = lax.dynamic_slice_in_dim(fast_charge, block_start, block_width, 0)
    rows_exclude = lax.dynamic_slice_in_dim(exclusions, block_start, block_width, 0)
    column_atoms = (
        (jnp.arange(row_count, dtype=jnp.int32) * col_count + col_index)[:, None] * piece
        + jnp.arange(piece, dtype=jnp.int32)[None, :]
    ).reshape(-1)
    column_cells = jnp.take(coords, column_atoms, axis=1)
    column_charge = jnp.take(fast_charge, column_atoms, axis=0)

    def fast_force(frac):
        rows_pos = lax.all_gather(frac, "col", axis=1, tiled=True)
        cols_pos = lax.all_gather(frac, "row", axis=1, tiled=True)
        partial_force = pair_fast(
            rows_pos,
            rows_cells,
            rows_charge,
            rows_exclude,
            cols_pos,
            column_cells,
            column_charge,
            column_atoms,
        )
        return lax.psum_scatter(partial_force, "col", scatter_dimension=1, tiled=True)

    grid_row = fast_owner // total_cols - row_index * cell_rows
    grid_col = fast_owner % total_cols - col_index * cell_cols
    inside = (grid_row >= 0) & (grid_row < cell_rows) & (grid_col >= 0) & (grid_col < cell_cols)
    local_cell = grid_row * cell_cols + grid_col
    cell_ids = jnp.arange(cell_rows * cell_cols, dtype=jnp.int32)
    select = jnp.where(
        inside[:, None] & (local_cell[:, None] == cell_ids[None, :]),
        jnp.float32(1.0),
        jnp.float32(0.0),
    )

    def slow_both(spos, frac):
        data = jnp.concatenate([spos, slow_charge[None]], axis=0)
        padded = with_halo(data, (("row", 1), ("col", 2)), 2)
        views = jnp.stack(
            [padded[:, o // 5 : o // 5 + cell_rows, o % 5 : o % 5 + cell_cols] for o in range(25)]
        )
        cell_force = slow_cells(data, views, neighbours)
        everyone = lax.all_gather(frac, ("row", "col"), axis=1, tiled=True)
        table = jnp.transpose(data, (1, 2, 0, 3)).reshape(cell_rows * cell_cols, 4 * CELL)
        picked = jnp.dot(
            select, table, precision=lax.Precision.HIGHEST, preferred_element_type=jnp.float32
        )
        picked = jnp.transpose(picked.reshape(fast_charge.shape[0], 4, CELL), (1, 0, 2))
        partial_env = fast_from_cells(everyone, fast_charge, picked)
        summed = lax.psum(partial_env, ("row", "col"))
        own_env = lax.dynamic_slice_in_dim(summed, flat_index * piece, piece, 1)
        return (cell_force, own_env)

    half_outer = 0.5 * outer_dt
    inner_dt = outer_dt / INNER
    fast_acc = fast_force(fast_pos)
    slow_acc, env_acc = slow_both(slow_pos, fast_pos)
    slow_vel = slow_vel + half_outer * slow_acc
    fast_vel = fast_vel + half_outer * env_acc
    for inner_step in range(INNER):
        fast_vel = fast_vel + 0.5 * inner_dt * fast_acc
        fast_pos = fast_pos + inner_dt * fast_vel
        fast_acc = fast_force(fast_pos)
        fast_vel = fast_vel + 0.5 * inner_dt * fast_acc
    slow_pos = slow_pos + outer_dt * slow_vel
    slow_acc, env_acc = slow_both(slow_pos, fast_pos)
    slow_vel = slow_vel + half_outer * slow_acc
    fast_vel = fast_vel + half_outer * env_acc
    return (fast_pos, fast_vel, slow_pos, slow_vel)


def solution(mesh):
    both = P(None, ("row", "col"))
    return jax.shard_map(
        per_device,
        mesh=mesh,
        in_specs=(
            both, both, P(), P(), P(),
            P(None, "row", "col", None), P(None, "row", "col", None),
            P("row", "col", None), P("row", "col", None),
        ),
        out_specs=(both, both, P(None, "row", "col", None), P(None, "row", "col", None)),
        check_vma=False,
    )
```

```python
import functools

import jax
import jax.numpy as jnp
from jax import lax
from jax.experimental import pallas as pl
from jax.experimental.pallas import tpu as pltpu
from jax.sharding import PartitionSpec as P


CELL = 128
INNER = 4
GROUPS = 256

fast_coupling = 1.0
slow_coupling = 0.1
outer_dt = 0.2
half_outer = 0.5 * outer_dt
inner_dt = outer_dt / INNER

BOTH = ("row", "col")
F32 = jnp.float32
LANES = 128
ENV_UNROLL = 4
VMEM = pl.BlockSpec(memory_space=pltpu.VMEM)
SMEM = pl.BlockSpec(memory_space=pltpu.SMEM)


def sds(shape, dtype=F32):
    return jax.ShapeDtypeStruct(shape, dtype)


def fast_rows(g_ref, cor_ref, q_ref, exm_ref, own, planes, cols, sums):
    count = g_ref.shape[0]
    members = exm_ref.shape[0]
    for c in range(3):
        x = g_ref[:, c, :]
        planes[c] = x + cor_ref[c] if c < 2 else x
    own_rows = [planes[c, pl.ds(own, 1), :] for c in range(3)]
    for c in range(3):
        cols[c] = jnp.transpose(jnp.broadcast_to(own_rows[c], (LANES, LANES)))
    unroll = 2

    def body(i, carry):
        at = [pl.ds(pl.multiple_of((i * unroll + u) * 8, 8), 8) for u in range(unroll)]
        a = [[cols[c, at[u], :] for c in range(3)] for u in range(unroll)]
        acc = [[jnp.zeros((8, LANES), F32) for _ in range(3)] for _ in range(unroll)]
        for b in range(count):
            y = [jnp.broadcast_to(planes[c, b : b + 1, :], (8, LANES)) for c in range(3)]
            qb = jnp.broadcast_to(q_ref[b : b + 1, :], (8, LANES))
            for u in range(unroll):
                d = [a[u][c] - y[c] for c in range(3)]
                r = lax.rsqrt(d[0] * d[0] + d[1] * d[1] + d[2] * d[2] + 1.0)
                w = (qb * r) * (r * r)
                for c in range(3):
                    acc[u][c] = acc[u][c] + w * d[c]
        for u in range(unroll):
            for c in range(3):
                sums[c, at[u], :] = acc[u][c]
        return carry

    lax.fori_loop(0, LANES // (8 * unroll), body, 0)
    step = GROUPS // LANES
    part = pl.ds(lax.rem(own, step), members, stride=step)
    d = [own_rows[c] - planes[c, part, :] for c in range(3)]
    r = lax.rsqrt(d[0] * d[0] + d[1] * d[1] + d[2] * d[2] + 1.0)
    w = (exm_ref[...] * q_ref[part, :]) * (r * (r * r))
    ones = jnp.ones((8, LANES), F32)
    scale = fast_coupling * q_ref[pl.ds(own, 1), :]
    out = []
    for c in range(3):
        total = lax.dot_general(
            ones, sums[c], (((1,), (1,)), ((), ())),
            precision=lax.Precision.HIGHEST, preferred_element_type=F32,
        )[0:1, :]
        out.append(scale * (total - jnp.sum(w * d[c], axis=0, keepdims=True)))
    return out


def fast_only_kernel(own_ref, g_ref, cor_ref, q_ref, exm_ref, f_ref, planes, cols, sums):
    rows = fast_rows(g_ref, cor_ref, q_ref, exm_ref, own_ref[0], planes, cols, sums)
    for c in range(3):
        f_ref[c : c + 1, :] = rows[c]


def fast_step_kernel(
    own_ref, g_ref, cor_ref, q_ref, exm_ref, v_ref, send_ref, p_out, v_out, planes, cols, sums
):
    own = own_ref[0]
    rows = fast_rows(g_ref, cor_ref, q_ref, exm_ref, own, planes, cols, sums)
    count = send_ref.shape[0]
    for c in range(3):
        v = v_ref[c : c + 1, :] + inner_dt * rows[c]
        p = g_ref[pl.ds(own, 1), c, :] + inner_dt * v
        v_out[c : c + 1, :] = v
        p_out[c : c + 1, :] = p
        send_ref[:, c, :] = jnp.broadcast_to(p, (count, LANES))


def fast_cost(count):
    pairs = count * LANES * LANES
    return pl.CostEstimate(flops=19 * pairs, transcendentals=pairs, bytes_accessed=count * 4096)


def fast_scratch(count):
    return [
        pltpu.VMEM((3, count, LANES), F32),
        pltpu.VMEM((3, LANES, LANES), F32),
        pltpu.VMEM((3, LANES, LANES), F32),
    ]


def fast_only(own, g, cor, q, exm):
    count = g.shape[0]
    return pl.pallas_call(
        fast_only_kernel,
        out_shape=sds((3, LANES)),
        in_specs=[SMEM] + [VMEM] * 4,
        out_specs=VMEM,
        scratch_shapes=fast_scratch(count),
        cost_estimate=fast_cost(count),
        name="fast_only",
        compiler_params=pltpu.CompilerParams(vmem_limit_bytes=2 << 20),
    )(own, g, cor, q, exm)


def fast_step(own, g, cor, q, exm, v):
    count = g.shape[0]
    return pl.pallas_call(
        fast_step_kernel,
        out_shape=(sds((count, 3, LANES)), sds((3, LANES)), sds((3, LANES))),
        in_specs=[SMEM] + [VMEM] * 5,
        out_specs=(VMEM,) * 3,
        scratch_shapes=fast_scratch(count),
        cost_estimate=fast_cost(count),
        name="fast_step",
        compiler_params=pltpu.CompilerParams(vmem_limit_bytes=2 << 20),
    )(own, g, cor, q, exm, v)


def list_kernel(total_cols, cell_rows, cell_cols, owner_ref, base_ref, list_ref, count_ref):
    row0, col0 = base_ref[0], base_ref[1]

    unroll = 8

    def body(j, n):
        for u in range(unroll):
            i = j * unroll + u
            cell = owner_ref[i]
            r = lax.div(cell, total_cols)
            c = cell - r * total_cols - col0
            r = r - row0
            sign = r | (cell_rows - 1 - r) | c | (cell_cols - 1 - c)
            list_ref[n] = i + (r * cell_cols + c) * GROUPS
            n = n + (1 + lax.shift_right_arithmetic(sign, 31))
        return n

    n = lax.fori_loop(0, GROUPS // unroll, body, jnp.int32(0))
    count_ref[0] = n
    for k in range(ENV_UNROLL):
        list_ref[n + k] = -1


def env_list(owner, base, total_cols, cell_rows, cell_cols):
    return pl.pallas_call(
        functools.partial(list_kernel, total_cols, cell_rows, cell_cols),
        out_shape=(sds((GROUPS + ENV_UNROLL,), jnp.int32), sds((1,), jnp.int32)),
        in_specs=[SMEM, SMEM],
        out_specs=(SMEM, SMEM),
        name="env_list",
        compiler_params=pltpu.CompilerParams(vmem_limit_bytes=2 << 20),
    )(owner, base)


def env_kernel(list_ref, count_ref, g_ref, cells_ref, out_ref, planes, sums):
    step = GROUPS // LANES
    members = g_ref.shape[0] // step
    for c in range(3):
        for h in range(step):
            planes[c, h] = g_ref[pl.ds(h, members, stride=step), c, :]
    sums[...] = jnp.zeros_like(sums)
    lane = lax.broadcasted_iota(jnp.int32, (members, LANES), 1)

    def body(t, carry):
        for u in range(ENV_UNROLL):
            n = t * ENV_UNROLL + u
            entry = list_ref[n]
            group = entry & (GROUPS - 1)
            h = lax.shift_right_logical(group, LANES.bit_length() - 1)
            here = (lane == (group & (LANES - 1))) & (entry >= 0)
            cell = cells_ref[jnp.maximum(lax.div(entry, GROUPS), 0)]
            d = []
            for c in range(3):
                x = jnp.sum(jnp.where(here, planes[c, h], 0.0), axis=1, keepdims=True)
                d.append(x - cell[c : c + 1, :])
            r = lax.rsqrt(d[0] * d[0] + d[1] * d[1] + d[2] * d[2] + 0.5)
            w = (cell[3:4, :] * r) * (r * r)
            for c in range(3):
                f = jnp.sum(w * d[c], axis=1, keepdims=True)
                sums[c, h] = sums[c, h] + jnp.where(here, f, 0.0)
        return carry

    lax.fori_loop(0, lax.div(count_ref[0] + (ENV_UNROLL - 1), ENV_UNROLL), body, 0)
    for c in range(3):
        for h in range(step):
            out_ref[pl.ds(h, members, stride=step), c, :] = sums[c, h]


def env(lists, g, cells):
    count = g.shape[0]
    step = GROUPS // LANES
    members = count // step
    return pl.pallas_call(
        env_kernel,
        out_shape=sds((count, 3, LANES)),
        in_specs=[SMEM, SMEM, VMEM, VMEM],
        out_specs=VMEM,
        scratch_shapes=[
            pltpu.VMEM((3, step, members, LANES), F32),
            pltpu.VMEM((3, step, members, LANES), F32),
        ],
        cost_estimate=pl.CostEstimate(flops=2_000_000, transcendentals=60000, bytes_accessed=200000),
        name="env",
        compiler_params=pltpu.CompilerParams(vmem_limit_bytes=2 << 20),
    )(*lists, g, cells)


def kick_kernel(own_ref, e_ref, f_ref, q_ref, p_ref, v_ref, send_ref, p_out, v_out):
    scale = slow_coupling * q_ref[pl.ds(own_ref[0], 1), :]
    count = send_ref.shape[0]
    for c in range(3):
        e = scale * jnp.sum(e_ref[:, c, :], axis=0, keepdims=True)
        v = v_ref[c : c + 1, :] + half_outer * e + 0.5 * inner_dt * f_ref[c : c + 1, :]
        p = p_ref[c : c + 1, :] + inner_dt * v
        v_out[c : c + 1, :] = v
        p_out[c : c + 1, :] = p
        send_ref[:, c, :] = jnp.broadcast_to(p, (count, LANES))


def kick(own, e, f, q, p, v):
    count = e.shape[0]
    return pl.pallas_call(
        kick_kernel,
        out_shape=(sds((count, 3, LANES)), sds((3, LANES)), sds((3, LANES))),
        in_specs=[SMEM] + [VMEM] * 5,
        out_specs=(VMEM,) * 3,
        name="kick",
        compiler_params=pltpu.CompilerParams(vmem_limit_bytes=2 << 20),
    )(own, e, f, q, p, v)


def last_kick_kernel(own_ref, e_ref, f_ref, q_ref, v_ref, v_out):
    scale = slow_coupling * q_ref[pl.ds(own_ref[0], 1), :]
    for c in range(3):
        e = scale * jnp.sum(e_ref[:, c, :], axis=0, keepdims=True)
        v_out[c : c + 1, :] = (
            v_ref[c : c + 1, :] + 0.5 * inner_dt * f_ref[c : c + 1, :] + half_outer * e
        )


def last_kick(own, e, f, q, v):
    return pl.pallas_call(
        last_kick_kernel,
        out_shape=sds((3, LANES)),
        in_specs=[SMEM] + [VMEM] * 4,
        out_specs=VMEM,
        name="last_kick",
        compiler_params=pltpu.CompilerParams(vmem_limit_bytes=2 << 20),
    )(own, e, f, q, v)


def slow_kernel(first, row0, nb_ref, tab_ref, vel_ref, *refs):
    if first:
        vel_out, pos_out, cell_out, cols_a, cols_b, sums_a, sums_b = refs
    else:
        vel_out, cols_a, cols_b, sums_a, sums_b = refs
    cell_rows, cell_cols = vel_out.shape[1], vel_out.shape[2]
    slots = nb_ref.shape[1]
    count = cell_rows * cell_cols

    def place(n):
        return lax.div(n, cell_cols), lax.rem(n, cell_cols)

    def spread(n, cols):
        r, c = place(n)
        t = tab_ref[r + (row0 + 2), c + 2]
        for x in range(3):
            cols[x] = jnp.transpose(jnp.broadcast_to(t[x : x + 1], (CELL, CELL)))

    def pairs(n, cols, sums):
        r, c = place(n)
        others = []
        for k in range(slots):
            o = nb_ref[n + row0 * cell_cols, k]
            dr, dc = lax.div(o, 5), lax.rem(o, 5)
            t = tab_ref[r + (dr + row0), c + dc]
            rows = [t[0:1] + (dr - 2).astype(F32), t[1:2] + (dc - 2).astype(F32), t[2:3], t[3:4]]
            others.append([jnp.broadcast_to(y, (8, CELL)) for y in rows])
        for g in range(CELL // 8):
            at = slice(8 * g, 8 * g + 8)
            a = [cols[x, at, :] for x in range(3)]
            acc = None
            for y in others:
                d = [a[x] - y[x] for x in range(3)]
                i = lax.rsqrt(d[0] * d[0] + d[1] * d[1] + d[2] * d[2] + 0.5)
                w = (y[3] * i) * (i * i)
                f = [w * d[x] for x in range(3)]
                acc = f if acc is None else [acc[x] + f[x] for x in range(3)]
            for x in range(3):
                sums[x, at, :] = acc[x]

    def finish(n, sums):
        r, c = place(n)
        t = tab_ref[r + (row0 + 2), c + 2]
        scale = slow_coupling * t[3:4]
        for x in range(3):
            f = scale * jnp.sum(jnp.transpose(sums[x]), axis=0, keepdims=True)
            v = vel_ref[x, r + row0, pl.ds(c, 1), :] + half_outer * f
            vel_out[x, r, pl.ds(c, 1), :] = v
            if first:
                p = t[x : x + 1] + outer_dt * v
                pos_out[x, r, pl.ds(c, 1), :] = p
                cell_out[n, x : x + 1, :] = p
        if first:
            cell_out[n, 3:4, :] = t[3:4]

    spread(0, cols_a)

    def body(i, carry):
        n = 2 * i
        spread(n + 1, cols_b)
        pairs(n, cols_a, sums_a)
        finish(jnp.maximum(n - 1, 0), sums_b)
        spread(jnp.minimum(n + 2, count - 1), cols_a)
        pairs(n + 1, cols_b, sums_b)
        finish(n, sums_a)
        return carry

    lax.fori_loop(0, count // 2, body, 0)
    finish(count - 1, sums_b)


def slow(first, row0, rows, nb, tab, vel):
    shape = (3, rows) + vel.shape[2:]
    own = rows * vel.shape[2]
    out = (sds(shape), sds(shape), sds((own, 4, CELL))) if first else sds(shape)
    pairs = own * nb.shape[1] * CELL * CELL
    return pl.pallas_call(
        functools.partial(slow_kernel, first, row0),
        out_shape=out,
        in_specs=[SMEM, VMEM, VMEM],
        out_specs=(VMEM,) * 3 if first else VMEM,
        scratch_shapes=[pltpu.VMEM((3, CELL, CELL), F32)] * 4,
        compiler_params=pltpu.CompilerParams(vmem_limit_bytes=3 << 20),
        cost_estimate=pl.CostEstimate(
            flops=19 * pairs, transcendentals=pairs, bytes_accessed=1_000_000
        ),
        name="slow",
    )(nb, tab, vel)


def with_halo(x, sides, width):
    for axis, dim in sides:
        count, length = (lax.axis_size(axis), x.shape[dim])
        up = [(i, (i + 1) % count) for i in range(count)]
        down = [(j, i) for i, j in up]
        last = lax.slice_in_dim(x, length - width, length, axis=dim)
        initial = lax.slice_in_dim(x, 0, width, axis=dim)
        before = lax.ppermute(last, axis, up)
        after = lax.ppermute(initial, axis, down)
        x = jnp.concatenate([before, x, after], axis=dim)
    return x


def exchange(x):
    return lax.all_to_all(x, BOTH, 0, 0)


def per_device(*args):
    return rows_of_lanes(*args)


def rows_of_lanes(
    fast_pos, fast_vel, fast_charge, fast_owner, exclusions,
    slow_pos, slow_vel, slow_charge, neighbours,
):
    row_count, col_count = lax.axis_size("row"), lax.axis_size("col")
    row_index, col_index = lax.axis_index("row"), lax.axis_index("col")
    flat = row_index * col_count + col_index
    count = row_count * col_count
    piece = fast_pos.shape[1]
    cell_rows, cell_cols = slow_pos.shape[1], slow_pos.shape[2]
    total_cols = cell_cols * col_count
    own = jnp.reshape(flat, (1,)).astype(jnp.int32)

    g = exchange(jnp.broadcast_to(fast_pos[None], (count, 3, piece)))

    owner = fast_owner.reshape(count, piece)
    cor = jnp.stack([owner // total_cols, owner % total_cols]).astype(F32)
    q = fast_charge.reshape(count, piece)
    members = fast_charge.shape[0] // GROUPS
    ex = lax.dynamic_slice_in_dim(exclusions, flat * piece, piece, 0) // GROUPS
    exm = jnp.any(
        ex[None] == jnp.arange(members, dtype=jnp.int32)[:, None, None], axis=2
    ).astype(F32)
    base = jnp.stack([row_index * cell_rows, col_index * cell_cols]).astype(jnp.int32)
    lists = env_list(fast_owner[:GROUPS], base, total_cols, cell_rows, cell_cols)

    cells = jnp.concatenate([slow_pos, slow_charge[None]], axis=0).transpose(1, 2, 0, 3)
    sides = (("row", 0), ("col", 1))
    nb = neighbours.reshape(cell_rows * cell_cols, -1)
    half = cell_rows // 2
    tab = with_halo(cells, sides, 2)
    parts = []
    for r0 in (0, half):
        parts.append(slow(True, r0, half, nb, tab, slow_vel))
    slow_vel, slow_pos = (jnp.concatenate([parts[0][i], parts[1][i]], axis=1) for i in (0, 1))
    cells2 = jnp.concatenate([parts[0][2], parts[1][2]], axis=0)
    tab2 = with_halo(cells2.reshape(cells.shape), sides, 2)
    parts = []
    for r0 in (0, half):
        parts.append(slow(False, r0, half, nb, tab2, slow_vel))
    slow_vel = jnp.concatenate(parts, axis=1)

    back = exchange(env(lists, g, cells.reshape(cells2.shape)))
    f = fast_only(own, g, cor, q, exm)
    send, p, v = kick(own, back, f, q, fast_pos, fast_vel)
    for _ in range(INNER - 1):
        g = exchange(send)
        send, p, v = fast_step(own, g, cor, q, exm, v)
    g = exchange(send)
    back = exchange(env(lists, g, cells2))
    f = fast_only(own, g, cor, q, exm)
    v = last_kick(own, back, f, q, v)
    return (p, v, slow_pos, slow_vel)


def owner_coords(owner, total_cols):
    grid_row = (owner // total_cols).astype(jnp.float32)
    grid_col = (owner % total_cols).astype(jnp.float32)
    return jnp.stack([grid_row, grid_col, jnp.zeros_like(grid_row)])


def pair_fast(pos_a, cell_a, charge_a, exclude_a, pos_b, cell_b, charge_b, index_b):
    delta = pos_a[:, :, None] - pos_b[:, None, :] + (cell_a[:, :, None] - cell_b[:, None, :])
    dist_sq = jnp.sum(delta * delta, axis=0) + 1.0
    inverse = 1.0 / (dist_sq * jnp.sqrt(dist_sq))
    barred = jnp.any(exclude_a[:, :, None] == index_b[None, None, :], axis=1)
    weight = jnp.where(barred, jnp.float32(0.0), charge_a[:, None] * charge_b[None, :] * inverse)
    return fast_coupling * jnp.sum(weight[None] * delta, axis=2)


def slow_cells(own, views, lists):
    force = jnp.zeros((3,) + own.shape[1:], jnp.float32)
    offsets = jnp.arange(25, dtype=jnp.int32)
    for slot in range(lists.shape[-1]):
        chosen = lists[..., slot]
        pick = (chosen[..., None] == offsets).astype(jnp.float32)
        other = jnp.einsum("abo,oxabn->xabn", pick, views, precision=lax.Precision.HIGHEST)
        shift_row = (chosen // 5 - 2).astype(jnp.float32)
        shift_col = (chosen % 5 - 2).astype(jnp.float32)
        shift = jnp.stack([shift_row, shift_col, jnp.zeros_like(shift_row)])
        delta = own[0:3, :, :, :, None] - (other[0:3, :, :, None, :] + shift[:, :, :, None, None])
        dist_sq = jnp.sum(delta * delta, axis=0) + 0.5
        inverse = 1.0 / (dist_sq * jnp.sqrt(dist_sq))
        weight = other[3][:, :, None, :] * inverse
        force = force + jnp.sum(weight[None] * delta, axis=-1)
    return slow_coupling * own[3][None] * force


def fast_from_cells(frac, charge, picked):
    delta = frac[:, :, None] - picked[0:3]
    dist_sq = jnp.sum(delta * delta, axis=0) + 0.5
    inverse = 1.0 / (dist_sq * jnp.sqrt(dist_sq))
    weight = picked[3] * inverse
    return slow_coupling * charge[None, :] * jnp.sum(weight[None] * delta, axis=-1)


def general(
    fast_pos,
    fast_vel,
    fast_charge,
    fast_owner,
    exclusions,
    slow_pos,
    slow_vel,
    slow_charge,
    neighbours,
):
    row_count = lax.axis_size("row")
    col_count = lax.axis_size("col")
    row_index = lax.axis_index("row")
    col_index = lax.axis_index("col")
    flat_index = row_index * col_count + col_index
    piece = fast_pos.shape[1]
    cell_rows = slow_pos.shape[1]
    cell_cols = slow_pos.shape[2]
    total_cols = cell_cols * col_count
    coords = owner_coords(fast_owner, total_cols)
    block_width = col_count * piece
    block_start = row_index * block_width
    rows_cells = lax.dynamic_slice_in_dim(coords, block_start, block_width, 1)
    rows_charge = lax.dynamic_slice_in_dim(fast_charge, block_start, block_width, 0)
    rows_exclude = lax.dynamic_slice_in_dim(exclusions, block_start, block_width, 0)
    column_atoms = (
        (jnp.arange(row_count, dtype=jnp.int32) * col_count + col_index)[:, None] * piece
        + jnp.arange(piece, dtype=jnp.int32)[None, :]
    ).reshape(-1)
    column_cells = jnp.take(coords, column_atoms, axis=1)
    column_charge = jnp.take(fast_charge, column_atoms, axis=0)

    def fast_force(frac):
        rows_pos = lax.all_gather(frac, "col", axis=1, tiled=True)
        cols_pos = lax.all_gather(frac, "row", axis=1, tiled=True)
        partial_force = pair_fast(
            rows_pos,
            rows_cells,
            rows_charge,
            rows_exclude,
            cols_pos,
            column_cells,
            column_charge,
            column_atoms,
        )
        return lax.psum_scatter(partial_force, "col", scatter_dimension=1, tiled=True)

    grid_row = fast_owner // total_cols - row_index * cell_rows
    grid_col = fast_owner % total_cols - col_index * cell_cols
    inside = (grid_row >= 0) & (grid_row < cell_rows) & (grid_col >= 0) & (grid_col < cell_cols)
    local_cell = grid_row * cell_cols + grid_col
    cell_ids = jnp.arange(cell_rows * cell_cols, dtype=jnp.int32)
    select = jnp.where(
        inside[:, None] & (local_cell[:, None] == cell_ids[None, :]),
        jnp.float32(1.0),
        jnp.float32(0.0),
    )

    def slow_both(spos, frac):
        data = jnp.concatenate([spos, slow_charge[None]], axis=0)
        padded = with_halo(data, (("row", 1), ("col", 2)), 2)
        views = jnp.stack(
            [padded[:, o // 5 : o // 5 + cell_rows, o % 5 : o % 5 + cell_cols] for o in range(25)]
        )
        cell_force = slow_cells(data, views, neighbours)
        everyone = lax.all_gather(frac, ("row", "col"), axis=1, tiled=True)
        table = jnp.transpose(data, (1, 2, 0, 3)).reshape(cell_rows * cell_cols, 4 * CELL)
        picked = jnp.dot(
            select, table, precision=lax.Precision.HIGHEST, preferred_element_type=jnp.float32
        )
        picked = jnp.transpose(picked.reshape(fast_charge.shape[0], 4, CELL), (1, 0, 2))
        partial_env = fast_from_cells(everyone, fast_charge, picked)
        summed = lax.psum(partial_env, ("row", "col"))
        own_env = lax.dynamic_slice_in_dim(summed, flat_index * piece, piece, 1)
        return (cell_force, own_env)

    half_outer = 0.5 * outer_dt
    inner_dt = outer_dt / INNER
    fast_acc = fast_force(fast_pos)
    slow_acc, env_acc = slow_both(slow_pos, fast_pos)
    slow_vel = slow_vel + half_outer * slow_acc
    fast_vel = fast_vel + half_outer * env_acc
    for _ in range(INNER):
        fast_vel = fast_vel + 0.5 * inner_dt * fast_acc
        fast_pos = fast_pos + inner_dt * fast_vel
        fast_acc = fast_force(fast_pos)
        fast_vel = fast_vel + 0.5 * inner_dt * fast_acc
    slow_pos = slow_pos + outer_dt * slow_vel
    slow_acc, env_acc = slow_both(slow_pos, fast_pos)
    slow_vel = slow_vel + half_outer * slow_acc
    fast_vel = fast_vel + half_outer * env_acc
    return (fast_pos, fast_vel, slow_pos, slow_vel)


def solution(mesh):
    both = P(None, ("row", "col"))

    def run(*args):
        special = args[0].shape[1] == LANES * mesh.size
        step = jax.shard_map(
            per_device if special else general,
            mesh=mesh,
            in_specs=(
                both, both, P(), P(), P(),
                P(None, "row", "col", None), P(None, "row", "col", None),
                P("row", "col", None), P("row", "col", None),
            ),
            out_specs=(both, both, P(None, "row", "col", None), P(None, "row", "col", None)),
            check_vma=False,
        )
        return step(*args)

    return run
```

```python
import functools

import jax
import jax.numpy as jnp
from jax import lax
from jax.experimental import pallas as pl
from jax.experimental.pallas import tpu as pltpu
from jax.sharding import PartitionSpec as P


CELL = 128
INNER = 4
GROUPS = 256

fast_coupling = 1.0
slow_coupling = 0.1
outer_dt = 0.2
half_outer = 0.5 * outer_dt
inner_dt = outer_dt / INNER

BOTH = ("row", "col")
F32 = jnp.float32
BF16 = jnp.bfloat16
LANES = 128
ENV_UNROLL = 4
VMEM = pl.BlockSpec(memory_space=pltpu.VMEM)
SMEM = pl.BlockSpec(memory_space=pltpu.SMEM)


def sds(shape, dtype=F32):
    return jax.ShapeDtypeStruct(shape, dtype)


def fast_rows(g_ref, cor_ref, q_ref, exm_ref, own, planes, cols, sums):
    count = g_ref.shape[0]
    members = exm_ref.shape[0]
    for c in range(3):
        x = g_ref[:, c, :]
        planes[c] = x + cor_ref[c] if c < 2 else x
    own_rows = [planes[c, pl.ds(own, 1), :] for c in range(3)]
    for c in range(3):
        cols[c] = jnp.transpose(jnp.broadcast_to(own_rows[c], (LANES, LANES)))
    unroll = 2

    def body(i, carry):
        at = [pl.ds(pl.multiple_of((i * unroll + u) * 8, 8), 8) for u in range(unroll)]
        a = [[cols[c, at[u], :] for c in range(3)] for u in range(unroll)]
        acc = [[jnp.zeros((8, LANES), F32) for _ in range(3)] for _ in range(unroll)]
        for b in range(count):
            y = [jnp.broadcast_to(planes[c, b : b + 1, :], (8, LANES)) for c in range(3)]
            qb = jnp.broadcast_to(q_ref[b : b + 1, :], (8, LANES))
            for u in range(unroll):
                d = [a[u][c] - y[c] for c in range(3)]
                r = lax.rsqrt(d[0] * d[0] + d[1] * d[1] + d[2] * d[2] + 1.0)
                w = (qb * r) * (r * r)
                for c in range(3):
                    acc[u][c] = acc[u][c] + w * d[c]
        for u in range(unroll):
            for c in range(3):
                sums[c, at[u], :] = acc[u][c]
        return carry

    lax.fori_loop(0, LANES // (8 * unroll), body, 0)
    step = GROUPS // LANES
    part = pl.ds(lax.rem(own, step), members, stride=step)
    d = [own_rows[c] - planes[c, part, :] for c in range(3)]
    r = lax.rsqrt(d[0] * d[0] + d[1] * d[1] + d[2] * d[2] + 1.0)
    w = (exm_ref[...] * q_ref[part, :]) * (r * (r * r))
    ones = jnp.ones((8, LANES), F32)
    scale = fast_coupling * q_ref[pl.ds(own, 1), :]
    out = []
    for c in range(3):
        total = lax.dot_general(
            ones, sums[c], (((1,), (1,)), ((), ())),
            precision=lax.Precision.HIGHEST, preferred_element_type=F32,
        )[0:1, :]
        out.append(scale * (total - jnp.sum(w * d[c], axis=0, keepdims=True)))
    return out


def fast_only_kernel(own_ref, g_ref, cor_ref, q_ref, exm_ref, f_ref, planes, cols, sums):
    rows = fast_rows(g_ref, cor_ref, q_ref, exm_ref, own_ref[0], planes, cols, sums)
    for c in range(3):
        f_ref[c : c + 1, :] = rows[c]


def fast_step_kernel(
    own_ref, g_ref, cor_ref, q_ref, exm_ref, v_ref, send_ref, p_out, v_out, planes, cols, sums
):
    own = own_ref[0]
    rows = fast_rows(g_ref, cor_ref, q_ref, exm_ref, own, planes, cols, sums)
    count = send_ref.shape[0]
    for c in range(3):
        v = v_ref[c : c + 1, :] + inner_dt * rows[c]
        p = g_ref[pl.ds(own, 1), c, :] + inner_dt * v
        v_out[c : c + 1, :] = v
        p_out[c : c + 1, :] = p
        send_ref[:, c, :] = jnp.broadcast_to(p, (count, LANES))


def fast_cost(count):
    pairs = count * LANES * LANES
    return pl.CostEstimate(flops=19 * pairs, transcendentals=pairs, bytes_accessed=count * 4096)


def fast_scratch(count):
    return [
        pltpu.VMEM((3, count, LANES), F32),
        pltpu.VMEM((3, LANES, LANES), F32),
        pltpu.VMEM((3, LANES, LANES), F32),
    ]


def fast_only(own, g, cor, q, exm):
    count = g.shape[0]
    return pl.pallas_call(
        fast_only_kernel,
        out_shape=sds((3, LANES)),
        in_specs=[SMEM] + [VMEM] * 4,
        out_specs=VMEM,
        scratch_shapes=fast_scratch(count),
        cost_estimate=fast_cost(count),
        name="fast_only",
        compiler_params=pltpu.CompilerParams(vmem_limit_bytes=2 << 20),
    )(own, g, cor, q, exm)


def fast_step(own, g, cor, q, exm, v):
    count = g.shape[0]
    return pl.pallas_call(
        fast_step_kernel,
        out_shape=(sds((count, 3, LANES)), sds((3, LANES)), sds((3, LANES))),
        in_specs=[SMEM] + [VMEM] * 5,
        out_specs=(VMEM,) * 3,
        scratch_shapes=fast_scratch(count),
        cost_estimate=fast_cost(count),
        name="fast_step",
        compiler_params=pltpu.CompilerParams(vmem_limit_bytes=2 << 20),
    )(own, g, cor, q, exm, v)


def list_kernel(total_cols, cell_rows, cell_cols, owner_ref, base_ref, list_ref, count_ref):
    row0, col0 = base_ref[0], base_ref[1]

    unroll = 8

    power = total_cols & (total_cols - 1) == 0 and cell_cols & (cell_cols - 1) == 0

    def body(j, n):
        found = []
        for u in range(unroll):
            cell = owner_ref[j * unroll + u]
            if power:
                r = lax.shift_right_logical(cell, total_cols.bit_length() - 1) - row0
                c = (cell & (total_cols - 1)) - col0
                local = lax.shift_left(r, cell_cols.bit_length() - 1) + c
            else:
                r = lax.div(cell, total_cols) - row0
                c = lax.rem(cell, total_cols) - col0
                local = r * cell_cols + c
            sign = r | (cell_rows - 1 - r) | c | (cell_cols - 1 - c)
            entry = j * unroll + (u + lax.shift_left(local, GROUPS.bit_length() - 1))
            found.append((entry, 1 + lax.shift_right_arithmetic(sign, 31)))
        for entry, inside in found:
            list_ref[n] = entry
            n = n + inside
        return n

    n = lax.fori_loop(0, GROUPS // unroll, body, jnp.int32(0))
    count_ref[0] = n
    for k in range(ENV_UNROLL):
        list_ref[n + k] = -1


def env_list(owner, base, total_cols, cell_rows, cell_cols):
    return pl.pallas_call(
        functools.partial(list_kernel, total_cols, cell_rows, cell_cols),
        out_shape=(sds((GROUPS + ENV_UNROLL,), jnp.int32), sds((1,), jnp.int32)),
        in_specs=[SMEM, SMEM],
        out_specs=(SMEM, SMEM),
        name="env_list",
        compiler_params=pltpu.CompilerParams(vmem_limit_bytes=2 << 20),
    )(owner, base)


def env_kernel(list_ref, count_ref, g_ref, cells_ref, out_ref, planes, sums):
    step = GROUPS // LANES
    members = g_ref.shape[0] // step
    for c in range(3):
        for h in range(step):
            planes[c, h] = g_ref[pl.ds(h, members, stride=step), c, :]
    sums[...] = jnp.zeros_like(sums)
    lane = lax.broadcasted_iota(jnp.int32, (members, LANES), 1)

    def body(t, carry):
        for u in range(ENV_UNROLL):
            n = t * ENV_UNROLL + u
            entry = list_ref[n]
            group = entry & (GROUPS - 1)
            h = lax.shift_right_logical(group, LANES.bit_length() - 1)
            here = (lane == (group & (LANES - 1))) & (entry >= 0)
            cell = cells_ref[jnp.maximum(lax.shift_right_arithmetic(entry, GROUPS.bit_length() - 1), 0)]
            d = []
            for c in range(3):
                x = jnp.sum(jnp.where(here, planes[c, h], 0.0), axis=1, keepdims=True)
                d.append(x - cell[c : c + 1, :])
            r = lax.rsqrt(d[0] * d[0] + d[1] * d[1] + d[2] * d[2] + 0.5)
            w = (cell[3:4, :] * r) * (r * r)
            for c in range(3):
                f = jnp.sum(w * d[c], axis=1, keepdims=True)
                sums[c, h] = sums[c, h] + jnp.where(here, f, 0.0)
        return carry

    lax.fori_loop(0, lax.div(count_ref[0] + (ENV_UNROLL - 1), ENV_UNROLL), body, 0)
    for c in range(3):
        for h in range(step):
            out_ref[pl.ds(h, members, stride=step), c, :] = sums[c, h]


def env(lists, g, cells):
    count = g.shape[0]
    step = GROUPS // LANES
    members = count // step
    return pl.pallas_call(
        env_kernel,
        out_shape=sds((count, 3, LANES)),
        in_specs=[SMEM, SMEM, VMEM, VMEM],
        out_specs=VMEM,
        scratch_shapes=[
            pltpu.VMEM((3, step, members, LANES), F32),
            pltpu.VMEM((3, step, members, LANES), F32),
        ],
        cost_estimate=pl.CostEstimate(flops=2_000_000, transcendentals=60000, bytes_accessed=200000),
        name="env",
        compiler_params=pltpu.CompilerParams(vmem_limit_bytes=2 << 20),
    )(*lists, g, cells)


def kick_kernel(own_ref, e_ref, f_ref, q_ref, p_ref, v_ref, send_ref, p_out, v_out):
    scale = slow_coupling * q_ref[pl.ds(own_ref[0], 1), :]
    count = send_ref.shape[0]
    for c in range(3):
        e = scale * jnp.sum(e_ref[:, c, :], axis=0, keepdims=True)
        v = v_ref[c : c + 1, :] + half_outer * e + 0.5 * inner_dt * f_ref[c : c + 1, :]
        p = p_ref[c : c + 1, :] + inner_dt * v
        v_out[c : c + 1, :] = v
        p_out[c : c + 1, :] = p
        send_ref[:, c, :] = jnp.broadcast_to(p, (count, LANES))


def kick(own, e, f, q, p, v):
    count = e.shape[0]
    return pl.pallas_call(
        kick_kernel,
        out_shape=(sds((count, 3, LANES)), sds((3, LANES)), sds((3, LANES))),
        in_specs=[SMEM] + [VMEM] * 5,
        out_specs=(VMEM,) * 3,
        name="kick",
        compiler_params=pltpu.CompilerParams(vmem_limit_bytes=2 << 20),
    )(own, e, f, q, p, v)


def last_kick_kernel(own_ref, e_ref, f_ref, q_ref, v_ref, v_out):
    scale = slow_coupling * q_ref[pl.ds(own_ref[0], 1), :]
    for c in range(3):
        e = scale * jnp.sum(e_ref[:, c, :], axis=0, keepdims=True)
        v_out[c : c + 1, :] = (
            v_ref[c : c + 1, :] + 0.5 * inner_dt * f_ref[c : c + 1, :] + half_outer * e
        )


def last_kick(own, e, f, q, v):
    return pl.pallas_call(
        last_kick_kernel,
        out_shape=sds((3, LANES)),
        in_specs=[SMEM] + [VMEM] * 4,
        out_specs=VMEM,
        name="last_kick",
        compiler_params=pltpu.CompilerParams(vmem_limit_bytes=2 << 20),
    )(own, e, f, q, v)


def split3(x):
    hi = x.astype(BF16).astype(F32)
    rest = x - hi
    mid = rest.astype(BF16).astype(F32)
    return hi, mid, rest - mid


def slow_kernel(first, row0, nb_ref, tab_ref, vel_ref, *refs):
    if first:
        vel_out, pos_out, cell_out, *scratch = refs
    else:
        vel_out, *scratch = refs
    bufs = [tuple(scratch[0:4]), tuple(scratch[4:8])]
    cell_rows, cell_cols = vel_out.shape[1], vel_out.shape[2]
    slots = nb_ref.shape[1]
    count = cell_rows * cell_cols
    row8 = lax.broadcasted_iota(jnp.int32, (8, CELL), 0)

    def place(n):
        return lax.div(n, cell_cols), lax.rem(n, cell_cols)

    def load8(r, c):
        t = tab_ref[r, c]
        return jnp.concatenate([t, jnp.zeros_like(t)], axis=0)

    def distances(n, buf):
        feat, ys, dist, _ = buf
        r, c = place(n)
        x = jnp.where(row8 < 3, load8(r + (row0 + 2), c + 2), 0.0)
        norm = jnp.sum(x * x, axis=0, keepdims=True)
        hi, mid, lo = split3(jnp.where(row8 == 3, norm, jnp.where(row8 == 4, 1.0, x)))
        left = jnp.transpose(jnp.concatenate([hi, hi, mid, hi, mid, lo], axis=0)).astype(BF16)
        for k in range(slots):
            o = nb_ref[n + row0 * cell_cols, k]
            dr, dc = lax.div(o, 5), lax.rem(o, 5)
            y = load8(r + (dr + row0), c + dc)
            y = y + jnp.where(
                row8 == 0, (dr - 2).astype(F32), jnp.where(row8 == 1, (dc - 2).astype(F32), 0.0)
            )
            ys[8 * k : 8 * k + 8] = y
            y = jnp.where(row8 < 3, y, 0.0)
            norm = jnp.sum(y * y, axis=0, keepdims=True) + 0.5
            hi, mid, lo = split3(
                jnp.where(row8 == 3, 1.0, jnp.where(row8 == 4, norm, -2.0 * y))
            )
            feat[:, CELL * k : CELL * (k + 1)] = jnp.concatenate(
                [hi, mid, hi, lo, mid, hi], axis=0
            ).astype(BF16)
        dist[...] = jnp.dot(left, feat[...], preferred_element_type=F32)

    def pairs(buf):
        _, ys, dist, sums = buf
        for g in range(0, CELL // 8, 2):
            at = [slice(8 * (g + h), 8 * (g + h) + 8) for h in range(2)]
            acc = [None, None]
            for k in range(slots):
                y = [jnp.broadcast_to(ys[8 * k + x : 8 * k + x + 1], (8, CELL)) for x in range(4)]
                for h in range(2):
                    i = lax.rsqrt(dist[at[h], CELL * k : CELL * (k + 1)])
                    w = (y[3] * i) * (i * i)
                    f = [w * y[0], w * y[1], w * y[2], w]
                    acc[h] = f if acc[h] is None else [acc[h][x] + f[x] for x in range(4)]
            for h in range(2):
                for x in range(4):
                    sums[x, at[h], :] = acc[h][x]

    def finish(n, buf):
        sums = buf[3]
        r, c = place(n)
        t = tab_ref[r + (row0 + 2), c + 2]
        total = [jnp.sum(jnp.transpose(sums[x]), axis=0, keepdims=True) for x in range(4)]
        scale = slow_coupling * t[3:4]
        for x in range(3):
            f = scale * (t[x : x + 1] * total[3] - total[x])
            v = vel_ref[x, r + row0, pl.ds(c, 1), :] + half_outer * f
            vel_out[x, r, pl.ds(c, 1), :] = v
            if first:
                p = t[x : x + 1] + outer_dt * v
                pos_out[x, r, pl.ds(c, 1), :] = p
                cell_out[n, x : x + 1, :] = p
        if first:
            cell_out[n, 3:4, :] = t[3:4]

    distances(0, bufs[0])

    def body(i, carry):
        n = 2 * i
        distances(n + 1, bufs[1])
        pairs(bufs[0])
        finish(jnp.maximum(n - 1, 0), bufs[1])
        distances(jnp.minimum(n + 2, count - 1), bufs[0])
        pairs(bufs[1])
        finish(n, bufs[0])
        return carry

    lax.fori_loop(0, count // 2, body, 0)
    finish(count - 1, bufs[1])


def slow(first, row0, rows, nb, tab, vel):
    shape = (3, rows) + vel.shape[2:]
    own = rows * vel.shape[2]
    slots = nb.shape[1]
    out = (sds(shape), sds(shape), sds((own, 4, CELL))) if first else sds(shape)
    pairs = own * slots * CELL * CELL
    return pl.pallas_call(
        functools.partial(slow_kernel, first, row0),
        out_shape=out,
        in_specs=[SMEM, VMEM, VMEM],
        out_specs=(VMEM,) * 3 if first else VMEM,
        scratch_shapes=[
            pltpu.VMEM((48, slots * CELL), BF16),
            pltpu.VMEM((8 * slots, CELL), F32),
            pltpu.VMEM((CELL, slots * CELL), F32),
            pltpu.VMEM((4, CELL, CELL), F32),
        ] * 2,
        compiler_params=pltpu.CompilerParams(vmem_limit_bytes=4 << 20),
        cost_estimate=pl.CostEstimate(
            flops=10 * pairs, transcendentals=pairs, bytes_accessed=1_000_000
        ),
        name="slow",
    )(nb, tab, vel)


def with_halo(x, sides, width):
    for axis, dim in sides:
        count, length = (lax.axis_size(axis), x.shape[dim])
        up = [(i, (i + 1) % count) for i in range(count)]
        down = [(j, i) for i, j in up]
        last = lax.slice_in_dim(x, length - width, length, axis=dim)
        initial = lax.slice_in_dim(x, 0, width, axis=dim)
        before = lax.ppermute(last, axis, up)
        after = lax.ppermute(initial, axis, down)
        x = jnp.concatenate([before, x, after], axis=dim)
    return x


def exchange(x):
    return lax.all_to_all(x, BOTH, 0, 0)


def per_device(*args):
    return rows_of_lanes(*args)


def rows_of_lanes(
    fast_pos, fast_vel, fast_charge, fast_owner, exclusions,
    slow_pos, slow_vel, slow_charge, neighbours,
):
    row_count, col_count = lax.axis_size("row"), lax.axis_size("col")
    row_index, col_index = lax.axis_index("row"), lax.axis_index("col")
    flat = row_index * col_count + col_index
    count = row_count * col_count
    piece = fast_pos.shape[1]
    cell_rows, cell_cols = slow_pos.shape[1], slow_pos.shape[2]
    total_cols = cell_cols * col_count
    own = jnp.reshape(flat, (1,)).astype(jnp.int32)

    g = exchange(jnp.broadcast_to(fast_pos[None], (count, 3, piece)))

    owner = fast_owner.reshape(count, piece)
    cor = jnp.stack([owner // total_cols, owner % total_cols]).astype(F32)
    q = fast_charge.reshape(count, piece)
    members = fast_charge.shape[0] // GROUPS
    ex = lax.dynamic_slice_in_dim(exclusions, flat * piece, piece, 0) // GROUPS
    exm = jnp.any(
        ex[None] == jnp.arange(members, dtype=jnp.int32)[:, None, None], axis=2
    ).astype(F32)
    base = jnp.stack([row_index * cell_rows, col_index * cell_cols]).astype(jnp.int32)
    lists = env_list(fast_owner[:GROUPS], base, total_cols, cell_rows, cell_cols)

    cells = jnp.concatenate([slow_pos, slow_charge[None]], axis=0).transpose(1, 2, 0, 3)
    sides = (("row", 0), ("col", 1))
    nb = neighbours.reshape(cell_rows * cell_cols, -1)
    half = cell_rows // 2
    tab = with_halo(cells, sides, 2)
    parts = []
    for r0 in (0, half):
        parts.append(slow(True, r0, half, nb, tab, slow_vel))
    slow_vel, slow_pos = (jnp.concatenate([parts[0][i], parts[1][i]], axis=1) for i in (0, 1))
    cells2 = jnp.concatenate([parts[0][2], parts[1][2]], axis=0)
    tab2 = with_halo(cells2.reshape(cells.shape), sides, 2)
    parts = []
    for r0 in (0, half):
        parts.append(slow(False, r0, half, nb, tab2, slow_vel))
    slow_vel = jnp.concatenate(parts, axis=1)

    back = exchange(env(lists, g, cells.reshape(cells2.shape)))
    f = fast_only(own, g, cor, q, exm)
    send, p, v = kick(own, back, f, q, fast_pos, fast_vel)
    for _ in range(INNER - 1):
        g = exchange(send)
        send, p, v = fast_step(own, g, cor, q, exm, v)
    g = exchange(send)
    back = exchange(env(lists, g, cells2))
    f = fast_only(own, g, cor, q, exm)
    v = last_kick(own, back, f, q, v)
    return (p, v, slow_pos, slow_vel)


def owner_coords(owner, total_cols):
    grid_row = (owner // total_cols).astype(jnp.float32)
    grid_col = (owner % total_cols).astype(jnp.float32)
    return jnp.stack([grid_row, grid_col, jnp.zeros_like(grid_row)])


def pair_fast(pos_a, cell_a, charge_a, exclude_a, pos_b, cell_b, charge_b, index_b):
    delta = pos_a[:, :, None] - pos_b[:, None, :] + (cell_a[:, :, None] - cell_b[:, None, :])
    dist_sq = jnp.sum(delta * delta, axis=0) + 1.0
    inverse = 1.0 / (dist_sq * jnp.sqrt(dist_sq))
    barred = jnp.any(exclude_a[:, :, None] == index_b[None, None, :], axis=1)
    weight = jnp.where(barred, jnp.float32(0.0), charge_a[:, None] * charge_b[None, :] * inverse)
    return fast_coupling * jnp.sum(weight[None] * delta, axis=2)


def slow_cells(own, views, lists):
    force = jnp.zeros((3,) + own.shape[1:], jnp.float32)
    offsets = jnp.arange(25, dtype=jnp.int32)
    for slot in range(lists.shape[-1]):
        chosen = lists[..., slot]
        pick = (chosen[..., None] == offsets).astype(jnp.float32)
        other = jnp.einsum("abo,oxabn->xabn", pick, views, precision=lax.Precision.HIGHEST)
        shift_row = (chosen // 5 - 2).astype(jnp.float32)
        shift_col = (chosen % 5 - 2).astype(jnp.float32)
        shift = jnp.stack([shift_row, shift_col, jnp.zeros_like(shift_row)])
        delta = own[0:3, :, :, :, None] - (other[0:3, :, :, None, :] + shift[:, :, :, None, None])
        dist_sq = jnp.sum(delta * delta, axis=0) + 0.5
        inverse = 1.0 / (dist_sq * jnp.sqrt(dist_sq))
        weight = other[3][:, :, None, :] * inverse
        force = force + jnp.sum(weight[None] * delta, axis=-1)
    return slow_coupling * own[3][None] * force


def fast_from_cells(frac, charge, picked):
    delta = frac[:, :, None] - picked[0:3]
    dist_sq = jnp.sum(delta * delta, axis=0) + 0.5
    inverse = 1.0 / (dist_sq * jnp.sqrt(dist_sq))
    weight = picked[3] * inverse
    return slow_coupling * charge[None, :] * jnp.sum(weight[None] * delta, axis=-1)


def general(
    fast_pos,
    fast_vel,
    fast_charge,
    fast_owner,
    exclusions,
    slow_pos,
    slow_vel,
    slow_charge,
    neighbours,
):
    row_count = lax.axis_size("row")
    col_count = lax.axis_size("col")
    row_index = lax.axis_index("row")
    col_index = lax.axis_index("col")
    flat_index = row_index * col_count + col_index
    piece = fast_pos.shape[1]
    cell_rows = slow_pos.shape[1]
    cell_cols = slow_pos.shape[2]
    total_cols = cell_cols * col_count
    coords = owner_coords(fast_owner, total_cols)
    block_width = col_count * piece
    block_start = row_index * block_width
    rows_cells = lax.dynamic_slice_in_dim(coords, block_start, block_width, 1)
    rows_charge = lax.dynamic_slice_in_dim(fast_charge, block_start, block_width, 0)
    rows_exclude = lax.dynamic_slice_in_dim(exclusions, block_start, block_width, 0)
    column_atoms = (
        (jnp.arange(row_count, dtype=jnp.int32) * col_count + col_index)[:, None] * piece
        + jnp.arange(piece, dtype=jnp.int32)[None, :]
    ).reshape(-1)
    column_cells = jnp.take(coords, column_atoms, axis=1)
    column_charge = jnp.take(fast_charge, column_atoms, axis=0)

    def fast_force(frac):
        rows_pos = lax.all_gather(frac, "col", axis=1, tiled=True)
        cols_pos = lax.all_gather(frac, "row", axis=1, tiled=True)
        partial_force = pair_fast(
            rows_pos,
            rows_cells,
            rows_charge,
            rows_exclude,
            cols_pos,
            column_cells,
            column_charge,
            column_atoms,
        )
        return lax.psum_scatter(partial_force, "col", scatter_dimension=1, tiled=True)

    grid_row = fast_owner // total_cols - row_index * cell_rows
    grid_col = fast_owner % total_cols - col_index * cell_cols
    inside = (grid_row >= 0) & (grid_row < cell_rows) & (grid_col >= 0) & (grid_col < cell_cols)
    local_cell = grid_row * cell_cols + grid_col
    cell_ids = jnp.arange(cell_rows * cell_cols, dtype=jnp.int32)
    select = jnp.where(
        inside[:, None] & (local_cell[:, None] == cell_ids[None, :]),
        jnp.float32(1.0),
        jnp.float32(0.0),
    )

    def slow_both(spos, frac):
        data = jnp.concatenate([spos, slow_charge[None]], axis=0)
        padded = with_halo(data, (("row", 1), ("col", 2)), 2)
        views = jnp.stack(
            [padded[:, o // 5 : o // 5 + cell_rows, o % 5 : o % 5 + cell_cols] for o in range(25)]
        )
        cell_force = slow_cells(data, views, neighbours)
        everyone = lax.all_gather(frac, ("row", "col"), axis=1, tiled=True)
        table = jnp.transpose(data, (1, 2, 0, 3)).reshape(cell_rows * cell_cols, 4 * CELL)
        picked = jnp.dot(
            select, table, precision=lax.Precision.HIGHEST, preferred_element_type=jnp.float32
        )
        picked = jnp.transpose(picked.reshape(fast_charge.shape[0], 4, CELL), (1, 0, 2))
        partial_env = fast_from_cells(everyone, fast_charge, picked)
        summed = lax.psum(partial_env, ("row", "col"))
        own_env = lax.dynamic_slice_in_dim(summed, flat_index * piece, piece, 1)
        return (cell_force, own_env)

    half_outer = 0.5 * outer_dt
    inner_dt = outer_dt / INNER
    fast_acc = fast_force(fast_pos)
    slow_acc, env_acc = slow_both(slow_pos, fast_pos)
    slow_vel = slow_vel + half_outer * slow_acc
    fast_vel = fast_vel + half_outer * env_acc
    for _ in range(INNER):
        fast_vel = fast_vel + 0.5 * inner_dt * fast_acc
        fast_pos = fast_pos + inner_dt * fast_vel
        fast_acc = fast_force(fast_pos)
        fast_vel = fast_vel + 0.5 * inner_dt * fast_acc
    slow_pos = slow_pos + outer_dt * slow_vel
    slow_acc, env_acc = slow_both(slow_pos, fast_pos)
    slow_vel = slow_vel + half_outer * slow_acc
    fast_vel = fast_vel + half_outer * env_acc
    return (fast_pos, fast_vel, slow_pos, slow_vel)


def solution(mesh):
    both = P(None, ("row", "col"))

    def run(*args):
        special = args[0].shape[1] == LANES * mesh.size
        step = jax.shard_map(
            per_device if special else general,
            mesh=mesh,
            in_specs=(
                both, both, P(), P(), P(),
                P(None, "row", "col", None), P(None, "row", "col", None),
                P("row", "col", None), P("row", "col", None),
            ),
            out_specs=(both, both, P(None, "row", "col", None), P(None, "row", "col", None)),
            check_vma=False,
        )
        return step(*args)

    return run
```

```python
import functools

import jax
import jax.numpy as jnp
from jax import lax
from jax.experimental import pallas as pl
from jax.experimental.pallas import tpu as pltpu
from jax.sharding import PartitionSpec as P


CELL = 128
INNER = 4
GROUPS = 256

fast_coupling = 1.0
slow_coupling = 0.1
outer_dt = 0.2
half_outer = 0.5 * outer_dt
inner_dt = outer_dt / INNER

BOTH = ("row", "col")
F32 = jnp.float32
BF16 = jnp.bfloat16
LANES = 128
ENV_UNROLL = 4
VMEM = pl.BlockSpec(memory_space=pltpu.VMEM)
SMEM = pl.BlockSpec(memory_space=pltpu.SMEM)


def sds(shape, dtype=F32):
    return jax.ShapeDtypeStruct(shape, dtype)


def split3(x):
    hi = x.astype(BF16).astype(F32)
    rest = x - hi
    mid = rest.astype(BF16).astype(F32)
    return hi, mid, rest - mid


def norm_rows(y):
    row = lax.broadcasted_iota(jnp.int32, y.shape, 0)
    pos = jnp.where(row < 3, y, 0.0)
    return row, pos, jnp.sum(pos * pos, axis=0, keepdims=True)


def left_rows(y):
    row, pos, norm = norm_rows(y)
    hi, mid, lo = split3(jnp.where(row == 3, norm, jnp.where(row == 4, 1.0, pos)))
    return jnp.concatenate([hi, hi, mid, hi, mid, lo], axis=0)


def right_rows(y, soft):
    row, pos, norm = norm_rows(y)
    hi, mid, lo = split3(
        jnp.where(row == 3, 1.0, jnp.where(row == 4, norm + soft, -2.0 * pos))
    )
    return jnp.concatenate([hi, mid, hi, lo, mid, hi], axis=0)


def fast_rows(g_ref, table_ref, exm_ref, own, atoms, feat, dist, sums):
    count = g_ref.shape[0]
    members = exm_ref.shape[0]
    zeros = jnp.zeros((5, LANES), F32)
    for b in range(count):
        y = jnp.concatenate([g_ref[b], zeros], axis=0) + table_ref[b]
        atoms[b] = y
        feat[:, LANES * b : LANES * (b + 1)] = right_rows(y, 1.0).astype(BF16)
    me = atoms[own]
    left = jnp.transpose(left_rows(me)).astype(BF16)
    dist[...] = jnp.dot(left, feat[...], preferred_element_type=F32)
    unroll = 2

    def body(i, carry):
        at = [pl.ds(pl.multiple_of((i * unroll + u) * 8, 8), 8) for u in range(unroll)]
        acc = [None] * unroll
        for b in range(count):
            y = [jnp.broadcast_to(atoms[b, c : c + 1, :], (8, LANES)) for c in range(4)]
            for u in range(unroll):
                r = lax.rsqrt(dist[at[u], LANES * b : LANES * (b + 1)])
                w = (y[3] * r) * (r * r)
                f = [w * y[0], w * y[1], w * y[2], w]
                acc[u] = f if acc[u] is None else [acc[u][c] + f[c] for c in range(4)]
        for u in range(unroll):
            for c in range(4):
                sums[c, at[u], :] = acc[u][c]
        return carry

    lax.fori_loop(0, LANES // (8 * unroll), body, 0)
    step = GROUPS // LANES
    part = pl.ds(lax.rem(own, step), members, stride=step)
    d = [me[c : c + 1] - atoms[part, c, :] for c in range(3)]
    r = lax.rsqrt(d[0] * d[0] + d[1] * d[1] + d[2] * d[2] + 1.0)
    w = (exm_ref[...] * atoms[part, 3, :]) * (r * (r * r))
    scale = fast_coupling * me[3:4]
    total = [jnp.sum(jnp.transpose(sums[c]), axis=0, keepdims=True) for c in range(4)]
    return [
        scale
        * (me[c : c + 1] * total[3] - total[c] - jnp.sum(w * d[c], axis=0, keepdims=True))
        for c in range(3)
    ]


def fast_only_kernel(own_ref, g_ref, table_ref, exm_ref, f_ref, *scratch):
    rows = fast_rows(g_ref, table_ref, exm_ref, own_ref[0], *scratch)
    for c in range(3):
        f_ref[c : c + 1, :] = rows[c]


def fast_step_kernel(
    own_ref, g_ref, table_ref, exm_ref, v_ref, send_ref, p_out, v_out, *scratch
):
    own = own_ref[0]
    rows = fast_rows(g_ref, table_ref, exm_ref, own, *scratch)
    count = send_ref.shape[0]
    for c in range(3):
        v = v_ref[c : c + 1, :] + inner_dt * rows[c]
        p = g_ref[pl.ds(own, 1), c, :] + inner_dt * v
        v_out[c : c + 1, :] = v
        p_out[c : c + 1, :] = p
        send_ref[:, c, :] = jnp.broadcast_to(p, (count, LANES))


def fast_cost(count):
    pairs = count * LANES * LANES
    return pl.CostEstimate(flops=10 * pairs, transcendentals=pairs, bytes_accessed=count * 4096)


def fast_scratch(count):
    return [
        pltpu.VMEM((count, 8, LANES), F32),
        pltpu.VMEM((48, count * LANES), BF16),
        pltpu.VMEM((LANES, count * LANES), F32),
        pltpu.VMEM((4, LANES, LANES), F32),
    ]


def fast_only(own, g, table, exm):
    count = g.shape[0]
    return pl.pallas_call(
        fast_only_kernel,
        out_shape=sds((3, LANES)),
        in_specs=[SMEM] + [VMEM] * 3,
        out_specs=VMEM,
        scratch_shapes=fast_scratch(count),
        cost_estimate=fast_cost(count),
        name="fast_only",
        compiler_params=pltpu.CompilerParams(vmem_limit_bytes=4 << 20),
    )(own, g, table, exm)


def fast_step(own, g, table, exm, v):
    count = g.shape[0]
    return pl.pallas_call(
        fast_step_kernel,
        out_shape=(sds((count, 3, LANES)), sds((3, LANES)), sds((3, LANES))),
        in_specs=[SMEM] + [VMEM] * 4,
        out_specs=(VMEM,) * 3,
        scratch_shapes=fast_scratch(count),
        cost_estimate=fast_cost(count),
        name="fast_step",
        compiler_params=pltpu.CompilerParams(vmem_limit_bytes=4 << 20),
    )(own, g, table, exm, v)


def prep_kernel(
    grid, place_ref, owner_smem, owner_ref, q_ref, ex_ref, table_ref, exm_ref, list_ref, count_ref
):
    total_cols, cell_rows, cell_cols = grid
    own, row_index, col_index = place_ref[0], place_ref[1], place_ref[2]
    owner = owner_ref[...]
    table_ref[...] = jnp.zeros_like(table_ref)
    table_ref[:, 0, :] = (lax.div(owner, total_cols) - total_cols // 2).astype(F32)
    table_ref[:, 1, :] = (lax.rem(owner, total_cols) - total_cols // 2).astype(F32)
    table_ref[:, 3, :] = q_ref[...]
    ex = ex_ref[:, pl.ds(pl.multiple_of(own * LANES, LANES), LANES)]
    ex = lax.div(ex, GROUPS)
    member = lax.broadcasted_iota(jnp.int32, exm_ref.shape, 0)
    barred = jnp.zeros(exm_ref.shape, F32)
    for k in range(ex_ref.shape[0]):
        barred = jnp.where(member == ex[k : k + 1], 1.0, barred)
    exm_ref[...] = barred
    row_bit = total_cols * cell_rows
    keep = -row_bit | (total_cols - cell_cols)
    here = row_index * row_bit + col_index * cell_cols
    unroll = 16

    def body(j, n):
        found = []
        for u in range(unroll):
            i = j * unroll + u
            cell = owner_smem[i]
            other = (cell & keep) ^ here
            found.append((cell * GROUPS + i, lax.shift_right_logical(other - 1, 31)))
        for entry, inside in found:
            list_ref[n] = entry
            n = n + inside
        return n

    n = lax.fori_loop(0, GROUPS // unroll, body, jnp.int32(0))
    count_ref[0] = n
    for k in range(ENV_UNROLL):
        list_ref[n + k] = -1


def prep(place, owner, q, exclusions, members, grid):
    count = owner.shape[0] // LANES
    return pl.pallas_call(
        functools.partial(prep_kernel, grid),
        out_shape=(
            sds((count, 8, LANES)), sds((members, LANES)),
            sds((GROUPS + ENV_UNROLL,), jnp.int32), sds((1,), jnp.int32),
        ),
        in_specs=[SMEM, SMEM, VMEM, VMEM, VMEM],
        out_specs=(VMEM, VMEM, SMEM, SMEM),
        name="prep",
        compiler_params=pltpu.CompilerParams(vmem_limit_bytes=2 << 20),
    )(place, owner, owner.reshape(count, LANES), q, exclusions.T)


def env_kernel(grid, list_ref, count_ref, g_ref, cells_ref, out_ref, planes, sums):
    total_cols, cell_rows, cell_cols = grid
    step = GROUPS // LANES
    members = g_ref.shape[0] // step
    for c in range(3):
        for h in range(step):
            planes[c, h] = g_ref[pl.ds(h, members, stride=step), c, :]
    sums[...] = jnp.zeros_like(sums)
    lane = lax.broadcasted_iota(jnp.int32, (members, LANES), 1)

    def body(t, carry):
        for u in range(ENV_UNROLL):
            n = t * ENV_UNROLL + u
            entry = list_ref[n]
            group = entry & (GROUPS - 1)
            h = lax.shift_right_logical(group, LANES.bit_length() - 1)
            here = (lane == (group & (LANES - 1))) & (entry >= 0)
            number = jnp.maximum(lax.shift_right_arithmetic(entry, GROUPS.bit_length() - 1), 0)
            r = lax.div(number, total_cols) & (cell_rows - 1)
            cell = cells_ref[r * cell_cols + (number & (cell_cols - 1))]
            d = []
            for c in range(3):
                x = jnp.sum(jnp.where(here, planes[c, h], 0.0), axis=1, keepdims=True)
                d.append(x - cell[c : c + 1, :])
            r = lax.rsqrt(d[0] * d[0] + d[1] * d[1] + d[2] * d[2] + 0.5)
            w = (cell[3:4, :] * r) * (r * r)
            for c in range(3):
                f = jnp.sum(w * d[c], axis=1, keepdims=True)
                sums[c, h] = sums[c, h] + jnp.where(here, f, 0.0)
        return carry

    lax.fori_loop(0, lax.div(count_ref[0] + (ENV_UNROLL - 1), ENV_UNROLL), body, 0)
    for c in range(3):
        for h in range(step):
            out_ref[pl.ds(h, members, stride=step), c, :] = sums[c, h]


def env(lists, g, cells, grid):
    count = g.shape[0]
    step = GROUPS // LANES
    members = count // step
    return pl.pallas_call(
        functools.partial(env_kernel, grid),
        out_shape=sds((count, 3, LANES)),
        in_specs=[SMEM, SMEM, VMEM, VMEM],
        out_specs=VMEM,
        scratch_shapes=[
            pltpu.VMEM((3, step, members, LANES), F32),
            pltpu.VMEM((3, step, members, LANES), F32),
        ],
        cost_estimate=pl.CostEstimate(flops=2_000_000, transcendentals=60000, bytes_accessed=200000),
        name="env",
        compiler_params=pltpu.CompilerParams(vmem_limit_bytes=2 << 20),
    )(*lists, g, cells)


def kick_kernel(own_ref, e_ref, f_ref, q_ref, p_ref, v_ref, send_ref, p_out, v_out):
    scale = slow_coupling * q_ref[pl.ds(own_ref[0], 1), :]
    count = send_ref.shape[0]
    for c in range(3):
        e = scale * jnp.sum(e_ref[:, c, :], axis=0, keepdims=True)
        v = v_ref[c : c + 1, :] + half_outer * e + 0.5 * inner_dt * f_ref[c : c + 1, :]
        p = p_ref[c : c + 1, :] + inner_dt * v
        v_out[c : c + 1, :] = v
        p_out[c : c + 1, :] = p
        send_ref[:, c, :] = jnp.broadcast_to(p, (count, LANES))


def kick(own, e, f, q, p, v):
    count = e.shape[0]
    return pl.pallas_call(
        kick_kernel,
        out_shape=(sds((count, 3, LANES)), sds((3, LANES)), sds((3, LANES))),
        in_specs=[SMEM] + [VMEM] * 5,
        out_specs=(VMEM,) * 3,
        name="kick",
        compiler_params=pltpu.CompilerParams(vmem_limit_bytes=2 << 20),
    )(own, e, f, q, p, v)


def last_kick_kernel(own_ref, e_ref, f_ref, q_ref, v_ref, v_out):
    scale = slow_coupling * q_ref[pl.ds(own_ref[0], 1), :]
    for c in range(3):
        e = scale * jnp.sum(e_ref[:, c, :], axis=0, keepdims=True)
        v_out[c : c + 1, :] = (
            v_ref[c : c + 1, :] + 0.5 * inner_dt * f_ref[c : c + 1, :] + half_outer * e
        )


def last_kick(own, e, f, q, v):
    return pl.pallas_call(
        last_kick_kernel,
        out_shape=sds((3, LANES)),
        in_specs=[SMEM] + [VMEM] * 4,
        out_specs=VMEM,
        name="last_kick",
        compiler_params=pltpu.CompilerParams(vmem_limit_bytes=2 << 20),
    )(own, e, f, q, v)


def slow_kernel(first, row0, nb_ref, tab_ref, vel_ref, *refs):
    results = 3 if first else 1
    if row0:
        before, refs = refs[:results], refs[results:]
    outs, scratch = refs[:results], refs[results:]
    vel_out = outs[0]
    if first:
        pos_out, cell_out = outs[1:]
    bufs = [tuple(scratch[0:4]), tuple(scratch[4:8])]
    cell_rows, cell_cols = vel_out.shape[1] - row0, vel_out.shape[2]
    slots = nb_ref.shape[1]
    count = cell_rows * cell_cols
    skip = row0 * cell_cols
    if row0:
        vel_out[:, :row0] = before[0][...]
        if first:
            pos_out[:, :row0] = before[1][...]
            cell_out[:skip] = before[2][...]
    row8 = lax.broadcasted_iota(jnp.int32, (8, CELL), 0)

    def place(n):
        return lax.div(n, cell_cols), lax.rem(n, cell_cols)

    def load8(r, c):
        t = tab_ref[r, c]
        return jnp.concatenate([t, jnp.zeros_like(t)], axis=0)

    def distances(n, buf):
        feat, ys, dist, _ = buf
        r, c = place(n)
        left = jnp.transpose(left_rows(load8(r + (row0 + 2), c + 2))).astype(BF16)
        for k in range(slots):
            o = nb_ref[n + row0 * cell_cols, k]
            dr, dc = lax.div(o, 5), lax.rem(o, 5)
            y = load8(r + (dr + row0), c + dc)
            y = y + jnp.where(
                row8 == 0, (dr - 2).astype(F32), jnp.where(row8 == 1, (dc - 2).astype(F32), 0.0)
            )
            ys[8 * k : 8 * k + 8] = y
            feat[:, CELL * k : CELL * (k + 1)] = right_rows(y, 0.5).astype(BF16)
        dist[...] = jnp.dot(left, feat[...], preferred_element_type=F32)

    def pairs(buf):
        _, ys, dist, sums = buf
        for g in range(0, CELL // 8, 2):
            at = [slice(8 * (g + h), 8 * (g + h) + 8) for h in range(2)]
            acc = [None, None]
            for k in range(slots):
                y = [jnp.broadcast_to(ys[8 * k + x : 8 * k + x + 1], (8, CELL)) for x in range(4)]
                for h in range(2):
                    i = lax.rsqrt(dist[at[h], CELL * k : CELL * (k + 1)])
                    w = (y[3] * i) * (i * i)
                    f = [w * y[0], w * y[1], w * y[2], w]
                    acc[h] = f if acc[h] is None else [acc[h][x] + f[x] for x in range(4)]
            for h in range(2):
                for x in range(4):
                    sums[x, at[h], :] = acc[h][x]

    def finish(n, buf):
        sums = buf[3]
        r, c = place(n)
        t = tab_ref[r + (row0 + 2), c + 2]
        total = [jnp.sum(jnp.transpose(sums[x]), axis=0, keepdims=True) for x in range(4)]
        scale = slow_coupling * t[3:4]
        for x in range(3):
            f = scale * (t[x : x + 1] * total[3] - total[x])
            v = vel_ref[x, r + row0, pl.ds(c, 1), :] + half_outer * f
            vel_out[x, r + row0, pl.ds(c, 1), :] = v
            if first:
                p = t[x : x + 1] + outer_dt * v
                pos_out[x, r + row0, pl.ds(c, 1), :] = p
                cell_out[n + skip, x : x + 1, :] = p
        if first:
            cell_out[n + skip, 3:4, :] = t[3:4]

    distances(0, bufs[0])

    def body(i, carry):
        n = 2 * i
        distances(n + 1, bufs[1])
        pairs(bufs[0])
        finish(jnp.maximum(n - 1, 0), bufs[1])
        distances(jnp.minimum(n + 2, count - 1), bufs[0])
        pairs(bufs[1])
        finish(n, bufs[0])
        return carry

    lax.fori_loop(0, count // 2, body, 0)
    finish(count - 1, bufs[1])


def slow(first, row0, rows, nb, tab, vel, before=()):
    shape = (3, row0 + rows) + vel.shape[2:]
    own = rows * vel.shape[2]
    slots = nb.shape[1]
    out = (sds(shape),)
    if first:
        out += (sds(shape), sds(((row0 + rows) * vel.shape[2], 4, CELL)))
    pairs = own * slots * CELL * CELL
    return pl.pallas_call(
        functools.partial(slow_kernel, first, row0),
        out_shape=out,
        in_specs=[SMEM] + [VMEM] * (2 + len(before)),
        out_specs=(VMEM,) * len(out),
        scratch_shapes=[
            pltpu.VMEM((48, slots * CELL), BF16),
            pltpu.VMEM((8 * slots, CELL), F32),
            pltpu.VMEM((CELL, slots * CELL), F32),
            pltpu.VMEM((4, CELL, CELL), F32),
        ] * 2,
        compiler_params=pltpu.CompilerParams(vmem_limit_bytes=4 << 20),
        cost_estimate=pl.CostEstimate(
            flops=10 * pairs, transcendentals=pairs, bytes_accessed=1_000_000
        ),
        name="slow",
    )(nb, tab, vel, *before)


def with_halo(x, sides, width):
    for axis, dim in sides:
        count, length = (lax.axis_size(axis), x.shape[dim])
        up = [(i, (i + 1) % count) for i in range(count)]
        down = [(j, i) for i, j in up]
        last = lax.slice_in_dim(x, length - width, length, axis=dim)
        initial = lax.slice_in_dim(x, 0, width, axis=dim)
        before = lax.ppermute(last, axis, up)
        after = lax.ppermute(initial, axis, down)
        x = jnp.concatenate([before, x, after], axis=dim)
    return x


def exchange(x):
    return lax.all_to_all(x, BOTH, 0, 0)


def per_device(*args):
    return rows_of_lanes(*args)


def rows_of_lanes(
    fast_pos, fast_vel, fast_charge, fast_owner, exclusions,
    slow_pos, slow_vel, slow_charge, neighbours,
):
    row_count, col_count = lax.axis_size("row"), lax.axis_size("col")
    row_index, col_index = lax.axis_index("row"), lax.axis_index("col")
    flat = row_index * col_count + col_index
    count = row_count * col_count
    piece = fast_pos.shape[1]
    cell_rows, cell_cols = slow_pos.shape[1], slow_pos.shape[2]
    total_cols = cell_cols * col_count
    own = jnp.reshape(flat, (1,)).astype(jnp.int32)

    g = exchange(jnp.broadcast_to(fast_pos[None], (count, 3, piece)))

    q = fast_charge.reshape(count, piece)
    members = fast_charge.shape[0] // GROUPS
    place = jnp.stack([flat, row_index, col_index]).astype(jnp.int32)
    grid = (total_cols, cell_rows, cell_cols)
    table, exm, *lists = prep(place, fast_owner, q, exclusions, members, grid)

    cells = jnp.concatenate([slow_pos, slow_charge[None]], axis=0).transpose(1, 2, 0, 3)
    sides = (("row", 0), ("col", 1))
    nb = neighbours.reshape(cell_rows * cell_cols, -1)
    half = cell_rows // 2
    tab = with_halo(cells, sides, 2)
    part = ()
    for r0 in (0, half):
        part = slow(True, r0, half, nb, tab, slow_vel, part)
    slow_vel, slow_pos, cells2 = part
    tab2 = with_halo(cells2.reshape(cells.shape), sides, 2)
    part = ()
    for r0 in (0, half):
        part = slow(False, r0, half, nb, tab2, slow_vel, part)
    (slow_vel,) = part

    back = exchange(env(lists, g, cells.reshape(cells2.shape), grid))
    f = fast_only(own, g, table, exm)
    send, p, v = kick(own, back, f, q, fast_pos, fast_vel)
    for _ in range(INNER - 1):
        g = exchange(send)
        send, p, v = fast_step(own, g, table, exm, v)
    g = exchange(send)
    back = exchange(env(lists, g, cells2, grid))
    f = fast_only(own, g, table, exm)
    v = last_kick(own, back, f, q, v)
    return (p, v, slow_pos, slow_vel)


def owner_coords(owner, total_cols):
    grid_row = (owner // total_cols).astype(jnp.float32)
    grid_col = (owner % total_cols).astype(jnp.float32)
    return jnp.stack([grid_row, grid_col, jnp.zeros_like(grid_row)])


def pair_fast(pos_a, cell_a, charge_a, exclude_a, pos_b, cell_b, charge_b, index_b):
    delta = pos_a[:, :, None] - pos_b[:, None, :] + (cell_a[:, :, None] - cell_b[:, None, :])
    dist_sq = jnp.sum(delta * delta, axis=0) + 1.0
    inverse = 1.0 / (dist_sq * jnp.sqrt(dist_sq))
    barred = jnp.any(exclude_a[:, :, None] == index_b[None, None, :], axis=1)
    weight = jnp.where(barred, jnp.float32(0.0), charge_a[:, None] * charge_b[None, :] * inverse)
    return fast_coupling * jnp.sum(weight[None] * delta, axis=2)


def slow_cells(own, views, lists):
    force = jnp.zeros((3,) + own.shape[1:], jnp.float32)
    offsets = jnp.arange(25, dtype=jnp.int32)
    for slot in range(lists.shape[-1]):
        chosen = lists[..., slot]
        pick = (chosen[..., None] == offsets).astype(jnp.float32)
        other = jnp.einsum("abo,oxabn->xabn", pick, views, precision=lax.Precision.HIGHEST)
        shift_row = (chosen // 5 - 2).astype(jnp.float32)
        shift_col = (chosen % 5 - 2).astype(jnp.float32)
        shift = jnp.stack([shift_row, shift_col, jnp.zeros_like(shift_row)])
        delta = own[0:3, :, :, :, None] - (other[0:3, :, :, None, :] + shift[:, :, :, None, None])
        dist_sq = jnp.sum(delta * delta, axis=0) + 0.5
        inverse = 1.0 / (dist_sq * jnp.sqrt(dist_sq))
        weight = other[3][:, :, None, :] * inverse
        force = force + jnp.sum(weight[None] * delta, axis=-1)
    return slow_coupling * own[3][None] * force


def fast_from_cells(frac, charge, picked):
    delta = frac[:, :, None] - picked[0:3]
    dist_sq = jnp.sum(delta * delta, axis=0) + 0.5
    inverse = 1.0 / (dist_sq * jnp.sqrt(dist_sq))
    weight = picked[3] * inverse
    return slow_coupling * charge[None, :] * jnp.sum(weight[None] * delta, axis=-1)


def general(
    fast_pos,
    fast_vel,
    fast_charge,
    fast_owner,
    exclusions,
    slow_pos,
    slow_vel,
    slow_charge,
    neighbours,
):
    row_count = lax.axis_size("row")
    col_count = lax.axis_size("col")
    row_index = lax.axis_index("row")
    col_index = lax.axis_index("col")
    flat_index = row_index * col_count + col_index
    piece = fast_pos.shape[1]
    cell_rows = slow_pos.shape[1]
    cell_cols = slow_pos.shape[2]
    total_cols = cell_cols * col_count
    coords = owner_coords(fast_owner, total_cols)
    block_width = col_count * piece
    block_start = row_index * block_width
    rows_cells = lax.dynamic_slice_in_dim(coords, block_start, block_width, 1)
    rows_charge = lax.dynamic_slice_in_dim(fast_charge, block_start, block_width, 0)
    rows_exclude = lax.dynamic_slice_in_dim(exclusions, block_start, block_width, 0)
    column_atoms = (
        (jnp.arange(row_count, dtype=jnp.int32) * col_count + col_index)[:, None] * piece
        + jnp.arange(piece, dtype=jnp.int32)[None, :]
    ).reshape(-1)
    column_cells = jnp.take(coords, column_atoms, axis=1)
    column_charge = jnp.take(fast_charge, column_atoms, axis=0)

    def fast_force(frac):
        rows_pos = lax.all_gather(frac, "col", axis=1, tiled=True)
        cols_pos = lax.all_gather(frac, "row", axis=1, tiled=True)
        partial_force = pair_fast(
            rows_pos,
            rows_cells,
            rows_charge,
            rows_exclude,
            cols_pos,
            column_cells,
            column_charge,
            column_atoms,
        )
        return lax.psum_scatter(partial_force, "col", scatter_dimension=1, tiled=True)

    grid_row = fast_owner // total_cols - row_index * cell_rows
    grid_col = fast_owner % total_cols - col_index * cell_cols
    inside = (grid_row >= 0) & (grid_row < cell_rows) & (grid_col >= 0) & (grid_col < cell_cols)
    local_cell = grid_row * cell_cols + grid_col
    cell_ids = jnp.arange(cell_rows * cell_cols, dtype=jnp.int32)
    select = jnp.where(
        inside[:, None] & (local_cell[:, None] == cell_ids[None, :]),
        jnp.float32(1.0),
        jnp.float32(0.0),
    )

    def slow_both(spos, frac):
        data = jnp.concatenate([spos, slow_charge[None]], axis=0)
        padded = with_halo(data, (("row", 1), ("col", 2)), 2)
        views = jnp.stack(
            [padded[:, o // 5 : o // 5 + cell_rows, o % 5 : o % 5 + cell_cols] for o in range(25)]
        )
        cell_force = slow_cells(data, views, neighbours)
        everyone = lax.all_gather(frac, ("row", "col"), axis=1, tiled=True)
        table = jnp.transpose(data, (1, 2, 0, 3)).reshape(cell_rows * cell_cols, 4 * CELL)
        picked = jnp.dot(
            select, table, precision=lax.Precision.HIGHEST, preferred_element_type=jnp.float32
        )
        picked = jnp.transpose(picked.reshape(fast_charge.shape[0], 4, CELL), (1, 0, 2))
        partial_env = fast_from_cells(everyone, fast_charge, picked)
        summed = lax.psum(partial_env, ("row", "col"))
        own_env = lax.dynamic_slice_in_dim(summed, flat_index * piece, piece, 1)
        return (cell_force, own_env)

    half_outer = 0.5 * outer_dt
    inner_dt = outer_dt / INNER
    fast_acc = fast_force(fast_pos)
    slow_acc, env_acc = slow_both(slow_pos, fast_pos)
    slow_vel = slow_vel + half_outer * slow_acc
    fast_vel = fast_vel + half_outer * env_acc
    for _ in range(INNER):
        fast_vel = fast_vel + 0.5 * inner_dt * fast_acc
        fast_pos = fast_pos + inner_dt * fast_vel
        fast_acc = fast_force(fast_pos)
        fast_vel = fast_vel + 0.5 * inner_dt * fast_acc
    slow_pos = slow_pos + outer_dt * slow_vel
    slow_acc, env_acc = slow_both(slow_pos, fast_pos)
    slow_vel = slow_vel + half_outer * slow_acc
    fast_vel = fast_vel + half_outer * env_acc
    return (fast_pos, fast_vel, slow_pos, slow_vel)


def solution(mesh):
    both = P(None, ("row", "col"))

    def run(*args):
        rows, cols = args[5].shape[1:3]
        powers = all(n & (n - 1) == 0 for n in (rows, cols, *mesh.shape.values()))
        special = args[0].shape[1] == LANES * mesh.size and powers
        step = jax.shard_map(
            per_device if special else general,
            mesh=mesh,
            in_specs=(
                both, both, P(), P(), P(),
                P(None, "row", "col", None), P(None, "row", "col", None),
                P("row", "col", None), P("row", "col", None),
            ),
            out_specs=(both, both, P(None, "row", "col", None), P(None, "row", "col", None)),
            check_vma=False,
        )
        return step(*args)

    return run
```

```python
import functools

import jax
import jax.numpy as jnp
from jax import lax
from jax.experimental import pallas as pl
from jax.experimental.pallas import tpu as pltpu
from jax.sharding import PartitionSpec as P


CELL = 128
INNER = 4
GROUPS = 256

fast_coupling = 1.0
slow_coupling = 0.1
outer_dt = 0.2
half_outer = 0.5 * outer_dt
inner_dt = outer_dt / INNER

BOTH = ("row", "col")
F32 = jnp.float32
BF16 = jnp.bfloat16
LANES = 128
ENV_UNROLL = 4


def in_hbm(x):
    return pltpu.with_memory_space_constraint(x, pltpu.HBM)


def position():
    return lax.axis_index("row") * lax.axis_size("col") + lax.axis_index("col")


VMEM = pl.BlockSpec(memory_space=pltpu.VMEM)
SMEM = pl.BlockSpec(memory_space=pltpu.SMEM)


def sds(shape, dtype=F32):
    return jax.ShapeDtypeStruct(shape, dtype)


def split3(x):
    hi = x.astype(BF16).astype(F32)
    rest = x - hi
    mid = rest.astype(BF16).astype(F32)
    return hi, mid, rest - mid


def norm_rows(y):
    row = lax.broadcasted_iota(jnp.int32, y.shape, 0)
    pos = jnp.where(row < 3, y, 0.0)
    return row, pos, jnp.sum(pos * pos, axis=0, keepdims=True)


def left_rows(y):
    row, pos, norm = norm_rows(y)
    hi, mid, lo = split3(jnp.where(row == 3, norm, jnp.where(row == 4, 1.0, pos)))
    return jnp.concatenate([hi, hi, mid, hi, mid, lo], axis=0)


def right_rows(y, soft):
    row, pos, norm = norm_rows(y)
    hi, mid, lo = split3(
        jnp.where(row == 3, 1.0, jnp.where(row == 4, norm + soft, -2.0 * pos))
    )
    return jnp.concatenate([hi, mid, hi, lo, mid, hi], axis=0)


def fast_rows(g_ref, table_ref, exm_ref, own, atoms, feat, dist, sums):
    count = g_ref.shape[0]
    members = exm_ref.shape[0]
    zeros = jnp.zeros((5, LANES), F32)
    for b in range(count):
        y = jnp.concatenate([g_ref[b], zeros], axis=0) + table_ref[b]
        atoms[b] = y
        feat[:, LANES * b : LANES * (b + 1)] = right_rows(y, 1.0).astype(BF16)
    me = atoms[own]
    left = jnp.transpose(left_rows(me)).astype(BF16)
    dist[...] = jnp.dot(left, feat[...], preferred_element_type=F32)
    unroll = 2

    def body(i, carry):
        at = [pl.ds(pl.multiple_of((i * unroll + u) * 8, 8), 8) for u in range(unroll)]
        acc = [None] * unroll
        for b in range(count):
            y = [jnp.broadcast_to(atoms[b, c : c + 1, :], (8, LANES)) for c in range(4)]
            for u in range(unroll):
                r = lax.rsqrt(dist[at[u], LANES * b : LANES * (b + 1)])
                w = (y[3] * r) * (r * r)
                f = [w * y[0], w * y[1], w * y[2], w]
                acc[u] = f if acc[u] is None else [acc[u][c] + f[c] for c in range(4)]
        for u in range(unroll):
            for c in range(4):
                sums[c, at[u], :] = acc[u][c]
        return carry

    lax.fori_loop(0, LANES // (8 * unroll), body, 0)
    step = GROUPS // LANES
    part = pl.ds(lax.rem(own, step), members, stride=step)
    d = [me[c : c + 1] - atoms[part, c, :] for c in range(3)]
    r = lax.rsqrt(d[0] * d[0] + d[1] * d[1] + d[2] * d[2] + 1.0)
    w = (exm_ref[...] * atoms[part, 3, :]) * (r * (r * r))
    scale = fast_coupling * me[3:4]
    total = [jnp.sum(jnp.transpose(sums[c]), axis=0, keepdims=True) for c in range(4)]
    return [
        scale
        * (me[c : c + 1] * total[3] - total[c] - jnp.sum(w * d[c], axis=0, keepdims=True))
        for c in range(3)
    ]


def fast_only_kernel(g_ref, table_ref, exm_ref, f_ref, *scratch):
    rows = fast_rows(g_ref, table_ref, exm_ref, position(), *scratch)
    for c in range(3):
        f_ref[c : c + 1, :] = rows[c]


def fast_step_kernel(
    g_ref, table_ref, exm_ref, v_ref, send_ref, p_out, v_out, *scratch
):
    own = position()
    rows = fast_rows(g_ref, table_ref, exm_ref, own, *scratch)
    count = send_ref.shape[0]
    for c in range(3):
        v = v_ref[c : c + 1, :] + inner_dt * rows[c]
        p = g_ref[pl.ds(own, 1), c, :] + inner_dt * v
        v_out[c : c + 1, :] = v
        p_out[c : c + 1, :] = p
        send_ref[:, c, :] = jnp.broadcast_to(p, (count, LANES))


def fast_cost(count):
    pairs = count * LANES * LANES
    return pl.CostEstimate(flops=10 * pairs, transcendentals=pairs, bytes_accessed=count * 4096)


def fast_scratch(count):
    return [
        pltpu.VMEM((count, 8, LANES), F32),
        pltpu.VMEM((48, count * LANES), BF16),
        pltpu.VMEM((LANES, count * LANES), F32),
        pltpu.VMEM((4, LANES, LANES), F32),
    ]


def fast_only(g, table, exm):
    count = g.shape[0]
    return pl.pallas_call(
        fast_only_kernel,
        out_shape=sds((3, LANES)),
        in_specs=[VMEM] * 3,
        out_specs=VMEM,
        scratch_shapes=fast_scratch(count),
        cost_estimate=fast_cost(count),
        name="fast_only",
        compiler_params=pltpu.CompilerParams(vmem_limit_bytes=4 << 20),
    )(g, table, exm)


def fast_step(g, table, exm, v):
    count = g.shape[0]
    return pl.pallas_call(
        fast_step_kernel,
        out_shape=(sds((count, 3, LANES)), sds((3, LANES)), sds((3, LANES))),
        in_specs=[VMEM] * 4,
        out_specs=(VMEM,) * 3,
        scratch_shapes=fast_scratch(count),
        cost_estimate=fast_cost(count),
        name="fast_step",
        compiler_params=pltpu.CompilerParams(vmem_limit_bytes=4 << 20),
    )(g, table, exm, v)


def prep_kernel(
    grid, owner_hbm, q_hbm, ex_hbm, table_ref, exm_ref, list_ref,
    heads, owner_ref, q_ref, ex_ref, sems,
):
    total_cols, cell_rows, cell_cols = grid
    mine = pl.ds(pl.multiple_of(position() * LANES, LANES), LANES)
    first = pltpu.make_async_copy(owner_hbm.at[0 : heads.shape[0]], heads, sems.at[3])
    first.start()
    copies = [
        pltpu.make_async_copy(owner_hbm, owner_ref, sems.at[0]),
        pltpu.make_async_copy(q_hbm, q_ref, sems.at[1]),
        pltpu.make_async_copy(ex_hbm.at[:, mine], ex_ref, sems.at[2]),
    ]
    for copy in copies:
        copy.start()
    table_ref[...] = jnp.zeros_like(table_ref)
    row_bit = total_cols * cell_rows
    keep = -row_bit | (total_cols - cell_cols)
    here = lax.axis_index("row") * row_bit + lax.axis_index("col") * cell_cols
    unroll = 16

    def body(j, n):
        found = []
        row = lax.shift_right_logical(j * unroll, LANES.bit_length() - 1)
        col = (j * unroll) & (LANES - 1)
        for u in range(unroll):
            i = j * unroll + u
            cell = heads[row, col + u]
            other = (cell & keep) ^ here
            found.append((cell * GROUPS + i, lax.shift_right_logical(other - 1, 31)))
        for entry, inside in found:
            list_ref[n] = entry
            n = n + inside
        return n

    first.wait()
    n = lax.fori_loop(0, GROUPS // unroll, body, jnp.int32(0))
    for k in range(ENV_UNROLL):
        list_ref[n + k] = -1
    list_ref[GROUPS + ENV_UNROLL] = n
    for copy in copies:
        copy.wait()
    owner = owner_ref[...]
    shift = total_cols.bit_length() - 1
    table_ref[:, 0, :] = (lax.shift_right_logical(owner, shift) - total_cols // 2).astype(F32)
    table_ref[:, 1, :] = ((owner & (total_cols - 1)) - total_cols // 2).astype(F32)
    table_ref[:, 3, :] = q_ref[...]
    ex = lax.shift_right_logical(ex_ref[...], GROUPS.bit_length() - 1)
    member = lax.broadcasted_iota(jnp.int32, exm_ref.shape, 0)
    barred = jnp.zeros(exm_ref.shape, F32)
    for k in range(ex_ref.shape[0]):
        barred = jnp.where(member == ex[k : k + 1], 1.0, barred)
    exm_ref[...] = barred


def prep(owner, q, exclusions, members, grid):
    count = owner.shape[0] // LANES
    hbm = pl.BlockSpec(memory_space=pltpu.HBM)
    return pl.pallas_call(
        functools.partial(prep_kernel, grid),
        out_shape=(
            sds((count, 8, LANES)), sds((members, LANES)),
            sds((GROUPS + ENV_UNROLL + 1,), jnp.int32),
        ),
        in_specs=[hbm, hbm, hbm],
        out_specs=(VMEM, VMEM, SMEM),
        scratch_shapes=[
            pltpu.SMEM((8 * pl.cdiv(GROUPS, 8 * LANES), LANES), jnp.int32),
            pltpu.VMEM((count, LANES), jnp.int32),
            pltpu.VMEM((count, LANES), F32),
            pltpu.VMEM((exclusions.shape[1], LANES), jnp.int32),
            pltpu.SemaphoreType.DMA((4,)),
        ],
        name="prep",
        compiler_params=pltpu.CompilerParams(vmem_limit_bytes=2 << 20),
    )(*(in_hbm(x) for x in (owner.reshape(count, LANES), q, exclusions.T)))


def env_kernel(grid, list_ref, g_ref, cells_ref, out_ref, planes, sums):
    total_cols, cell_rows, cell_cols = grid
    step = GROUPS // LANES
    members = g_ref.shape[0] // step
    for c in range(3):
        for h in range(step):
            planes[c, h] = g_ref[pl.ds(h, members, stride=step), c, :]
    sums[...] = jnp.zeros_like(sums)
    lane = lax.broadcasted_iota(jnp.int32, (members, LANES), 1)

    def body(t, carry):
        for u in range(ENV_UNROLL):
            n = t * ENV_UNROLL + u
            entry = list_ref[n]
            group = entry & (GROUPS - 1)
            h = lax.shift_right_logical(group, LANES.bit_length() - 1)
            here = (lane == (group & (LANES - 1))) & (entry >= 0)
            number = jnp.maximum(lax.shift_right_arithmetic(entry, GROUPS.bit_length() - 1), 0)
            r = lax.div(number, total_cols) & (cell_rows - 1)
            cell = cells_ref[r * cell_cols + (number & (cell_cols - 1))]
            d = []
            for c in range(3):
                x = jnp.sum(jnp.where(here, planes[c, h], 0.0), axis=1, keepdims=True)
                d.append(x - cell[c : c + 1, :])
            r = lax.rsqrt(d[0] * d[0] + d[1] * d[1] + d[2] * d[2] + 0.5)
            w = (cell[3:4, :] * r) * (r * r)
            for c in range(3):
                f = jnp.sum(w * d[c], axis=1, keepdims=True)
                sums[c, h] = sums[c, h] + jnp.where(here, f, 0.0)
        return carry

    lax.fori_loop(0, lax.div(list_ref[GROUPS + ENV_UNROLL] + (ENV_UNROLL - 1), ENV_UNROLL), body, 0)
    for c in range(3):
        for h in range(step):
            out_ref[pl.ds(h, members, stride=step), c, :] = sums[c, h]


def env(groups, g, cells, grid):
    count = g.shape[0]
    step = GROUPS // LANES
    members = count // step
    return pl.pallas_call(
        functools.partial(env_kernel, grid),
        out_shape=sds((count, 3, LANES)),
        in_specs=[SMEM, VMEM, VMEM],
        out_specs=VMEM,
        scratch_shapes=[
            pltpu.VMEM((3, step, members, LANES), F32),
            pltpu.VMEM((3, step, members, LANES), F32),
        ],
        cost_estimate=pl.CostEstimate(flops=2_000_000, transcendentals=60000, bytes_accessed=200000),
        name="env",
        compiler_params=pltpu.CompilerParams(vmem_limit_bytes=2 << 20),
    )(groups, g, cells)


def kick_kernel(e_ref, f_ref, q_ref, p_ref, v_ref, send_ref, p_out, v_out):
    scale = slow_coupling * q_ref[pl.ds(position(), 1), :]
    count = send_ref.shape[0]
    for c in range(3):
        e = scale * jnp.sum(e_ref[:, c, :], axis=0, keepdims=True)
        v = v_ref[c : c + 1, :] + half_outer * e + 0.5 * inner_dt * f_ref[c : c + 1, :]
        p = p_ref[c : c + 1, :] + inner_dt * v
        v_out[c : c + 1, :] = v
        p_out[c : c + 1, :] = p
        send_ref[:, c, :] = jnp.broadcast_to(p, (count, LANES))


def kick(e, f, q, p, v):
    count = e.shape[0]
    return pl.pallas_call(
        kick_kernel,
        out_shape=(sds((count, 3, LANES)), sds((3, LANES)), sds((3, LANES))),
        in_specs=[VMEM] * 5,
        out_specs=(VMEM,) * 3,
        name="kick",
        compiler_params=pltpu.CompilerParams(vmem_limit_bytes=2 << 20),
    )(e, f, q, p, v)


def last_kick_kernel(e_ref, f_ref, q_ref, v_ref, v_out):
    scale = slow_coupling * q_ref[pl.ds(position(), 1), :]
    for c in range(3):
        e = scale * jnp.sum(e_ref[:, c, :], axis=0, keepdims=True)
        v_out[c : c + 1, :] = (
            v_ref[c : c + 1, :] + 0.5 * inner_dt * f_ref[c : c + 1, :] + half_outer * e
        )


def last_kick(e, f, q, v):
    return pl.pallas_call(
        last_kick_kernel,
        out_shape=sds((3, LANES)),
        in_specs=[VMEM] * 4,
        out_specs=VMEM,
        name="last_kick",
        compiler_params=pltpu.CompilerParams(vmem_limit_bytes=2 << 20),
    )(e, f, q, v)


def slow_kernel(first, row0, nb_ref, tab_ref, vel_ref, *refs):
    results = 3 if first else 1
    if row0:
        before, refs = refs[:results], refs[results:]
    outs, scratch = refs[:results], refs[results:]
    totals = scratch[8]
    if first:
        fetch = pltpu.make_async_copy(vel_ref.at[:, row0 : outs[0].shape[1]], scratch[9], scratch[10])
        fetch.start()
    vel_out = outs[0]
    if first:
        pos_out, cell_out = outs[1:]
    bufs = [tuple(scratch[0:4]), tuple(scratch[4:8])]
    cell_rows, cell_cols = vel_out.shape[1] - row0, vel_out.shape[2]
    slots = nb_ref.shape[1]
    count = cell_rows * cell_cols
    skip = row0 * cell_cols
    if row0:
        vel_out[:, :row0] = before[0][...]
        if first:
            pos_out[:, :row0] = before[1][...]
            cell_out[:skip] = before[2][...]
    row8 = lax.broadcasted_iota(jnp.int32, (8, CELL), 0)

    def place(n):
        return lax.shift_right_logical(n, cell_cols.bit_length() - 1), n & (cell_cols - 1)

    def load8(r, c):
        t = tab_ref[r, c]
        return jnp.concatenate([t, jnp.zeros_like(t)], axis=0)

    def distances(n, buf):
        feat, ys, dist, _ = buf
        r, c = place(n)
        left = jnp.transpose(left_rows(load8(r + (row0 + 2), c + 2))).astype(BF16)
        for k in range(slots):
            o = nb_ref[n + row0 * cell_cols, k]
            dr = lax.shift_right_logical(o * 13, 6)
            dc = o - 5 * dr
            y = load8(r + (dr + row0), c + dc)
            y = y + jnp.where(
                row8 == 0, (dr - 2).astype(F32), jnp.where(row8 == 1, (dc - 2).astype(F32), 0.0)
            )
            ys[8 * k : 8 * k + 8] = y
            feat[:, CELL * k : CELL * (k + 1)] = right_rows(y, 0.5).astype(BF16)
        dist[...] = jnp.dot(left, feat[...], preferred_element_type=F32)

    def pairs(buf):
        _, ys, dist, sums = buf
        for g in range(0, CELL // 8, 2):
            at = [slice(8 * (g + h), 8 * (g + h) + 8) for h in range(2)]
            acc = [None, None]
            for k in range(slots):
                y = [jnp.broadcast_to(ys[8 * k + x : 8 * k + x + 1], (8, CELL)) for x in range(4)]
                for h in range(2):
                    i = lax.rsqrt(dist[at[h], CELL * k : CELL * (k + 1)])
                    w = (y[3] * i) * (i * i)
                    f = [w * y[0], w * y[1], w * y[2], w]
                    acc[h] = f if acc[h] is None else [acc[h][x] + f[x] for x in range(4)]
            for h in range(2):
                for x in range(4):
                    sums[x, at[h], :] = acc[h][x]

    def finish(n, buf):
        sums = buf[3]
        for x in range(4):
            totals[n, x : x + 1, :] = jnp.sum(jnp.transpose(sums[x]), axis=0, keepdims=True)

    distances(0, bufs[0])

    def body(i, carry):
        n = 2 * i
        distances(n + 1, bufs[1])
        pairs(bufs[0])
        finish(jnp.maximum(n - 1, 0), bufs[1])
        distances(jnp.minimum(n + 2, count - 1), bufs[0])
        pairs(bufs[1])
        finish(n, bufs[0])
        return carry

    lax.fori_loop(0, count // 2, body, 0)
    finish(count - 1, bufs[1])
    if first:
        fetch.wait()
    rows = slice(row0, row0 + cell_rows)
    inner = (slice(row0 + 2, row0 + 2 + cell_rows), slice(2, 2 + cell_cols))
    charge = tab_ref[inner[0], inner[1], 3, :].reshape(count, CELL)
    for x in range(3):
        p = tab_ref[inner[0], inner[1], x, :].reshape(count, CELL)
        f = slow_coupling * charge * (p * totals[:, 3, :] - totals[:, x, :])
        v = (scratch[9][x] if first else vel_ref[x, rows]) + half_outer * f.reshape(cell_rows, cell_cols, CELL)
        vel_out[x, rows] = v
        if first:
            p = p + outer_dt * v.reshape(count, CELL)
            pos_out[x, rows] = p.reshape(cell_rows, cell_cols, CELL)
            cell_out[skip:, x, :] = p
    if first:
        cell_out[skip:, 3, :] = charge


def slow(first, row0, rows, nb, tab, vel, before=()):
    shape = (3, row0 + rows) + vel.shape[2:]
    own = rows * vel.shape[2]
    slots = nb.shape[1]
    out = (sds(shape),)
    if first:
        out += (sds(shape), sds(((row0 + rows) * vel.shape[2], 4, CELL)))
    pairs = own * slots * CELL * CELL
    return pl.pallas_call(
        functools.partial(slow_kernel, first, row0),
        out_shape=out,
        in_specs=[SMEM, VMEM, pl.BlockSpec(memory_space=pltpu.HBM) if first else VMEM]
        + [VMEM] * len(before),
        out_specs=(VMEM,) * len(out),
        scratch_shapes=[
            pltpu.VMEM((48, slots * CELL), BF16),
            pltpu.VMEM((8 * slots, CELL), F32),
            pltpu.VMEM((CELL, slots * CELL), F32),
            pltpu.VMEM((4, CELL, CELL), F32),
        ] * 2 + [pltpu.VMEM((own, 4, CELL), F32)]
        + ([pltpu.VMEM((3, rows) + vel.shape[2:], F32), pltpu.SemaphoreType.DMA] if first else []),
        compiler_params=pltpu.CompilerParams(vmem_limit_bytes=4 << 20),
        cost_estimate=pl.CostEstimate(
            flops=10 * pairs, transcendentals=pairs, bytes_accessed=1_000_000
        ),
        name="slow",
    )(nb, tab, in_hbm(vel) if first else vel, *before)


def with_halo(x, sides, width):
    for axis, dim in sides:
        count, length = (lax.axis_size(axis), x.shape[dim])
        up = [(i, (i + 1) % count) for i in range(count)]
        down = [(j, i) for i, j in up]
        last = lax.slice_in_dim(x, length - width, length, axis=dim)
        initial = lax.slice_in_dim(x, 0, width, axis=dim)
        before = lax.ppermute(last, axis, up)
        after = lax.ppermute(initial, axis, down)
        x = jnp.concatenate([before, x, after], axis=dim)
    return x


def exchange(x):
    return lax.all_to_all(x, BOTH, 0, 0)


def per_device(*args):
    return rows_of_lanes(*args)


def rows_of_lanes(
    fast_pos, fast_vel, fast_charge, fast_owner, exclusions,
    slow_pos, slow_vel, slow_charge, neighbours,
):
    row_count, col_count = lax.axis_size("row"), lax.axis_size("col")
    count = row_count * col_count
    piece = fast_pos.shape[1]
    cell_rows, cell_cols = slow_pos.shape[1], slow_pos.shape[2]
    total_cols = cell_cols * col_count

    g = exchange(jnp.broadcast_to(fast_pos[None], (count, 3, piece)))

    q = fast_charge.reshape(count, piece)
    members = fast_charge.shape[0] // GROUPS
    grid = (total_cols, cell_rows, cell_cols)
    table, exm, groups = prep(fast_owner, q, exclusions, members, grid)

    cells = jnp.concatenate([slow_pos, slow_charge[None]], axis=0).transpose(1, 2, 0, 3)
    sides = (("row", 0), ("col", 1))
    nb = neighbours.reshape(cell_rows * cell_cols, -1)
    half = cell_rows // 2
    tab = with_halo(cells, sides, 2)
    part = ()
    for r0 in (0, half):
        part = slow(True, r0, half, nb, tab, slow_vel, part)
    slow_vel, slow_pos, cells2 = part
    tab2 = with_halo(cells2.reshape(cells.shape), sides, 2)
    part = ()
    for r0 in (0, half):
        part = slow(False, r0, half, nb, tab2, slow_vel, part)
    (slow_vel,) = part

    back = exchange(env(groups, g, cells.reshape(cells2.shape), grid))
    f = fast_only(g, table, exm)
    send, p, v = kick(back, f, q, fast_pos, fast_vel)
    for _ in range(INNER - 1):
        g = exchange(send)
        send, p, v = fast_step(g, table, exm, v)
    g = exchange(send)
    back = exchange(env(groups, g, cells2, grid))
    f = fast_only(g, table, exm)
    v = last_kick(back, f, q, v)
    return (p, v, slow_pos, slow_vel)


def owner_coords(owner, total_cols):
    grid_row = (owner // total_cols).astype(jnp.float32)
    grid_col = (owner % total_cols).astype(jnp.float32)
    return jnp.stack([grid_row, grid_col, jnp.zeros_like(grid_row)])


def pair_fast(pos_a, cell_a, charge_a, exclude_a, pos_b, cell_b, charge_b, index_b):
    delta = pos_a[:, :, None] - pos_b[:, None, :] + (cell_a[:, :, None] - cell_b[:, None, :])
    dist_sq = jnp.sum(delta * delta, axis=0) + 1.0
    inverse = 1.0 / (dist_sq * jnp.sqrt(dist_sq))
    barred = jnp.any(exclude_a[:, :, None] == index_b[None, None, :], axis=1)
    weight = jnp.where(barred, jnp.float32(0.0), charge_a[:, None] * charge_b[None, :] * inverse)
    return fast_coupling * jnp.sum(weight[None] * delta, axis=2)


def slow_cells(own, views, lists):
    force = jnp.zeros((3,) + own.shape[1:], jnp.float32)
    offsets = jnp.arange(25, dtype=jnp.int32)
    for slot in range(lists.shape[-1]):
        chosen = lists[..., slot]
        pick = (chosen[..., None] == offsets).astype(jnp.float32)
        other = jnp.einsum("abo,oxabn->xabn", pick, views, precision=lax.Precision.HIGHEST)
        shift_row = (chosen // 5 - 2).astype(jnp.float32)
        shift_col = (chosen % 5 - 2).astype(jnp.float32)
        shift = jnp.stack([shift_row, shift_col, jnp.zeros_like(shift_row)])
        delta = own[0:3, :, :, :, None] - (other[0:3, :, :, None, :] + shift[:, :, :, None, None])
        dist_sq = jnp.sum(delta * delta, axis=0) + 0.5
        inverse = 1.0 / (dist_sq * jnp.sqrt(dist_sq))
        weight = other[3][:, :, None, :] * inverse
        force = force + jnp.sum(weight[None] * delta, axis=-1)
    return slow_coupling * own[3][None] * force


def fast_from_cells(frac, charge, picked):
    delta = frac[:, :, None] - picked[0:3]
    dist_sq = jnp.sum(delta * delta, axis=0) + 0.5
    inverse = 1.0 / (dist_sq * jnp.sqrt(dist_sq))
    weight = picked[3] * inverse
    return slow_coupling * charge[None, :] * jnp.sum(weight[None] * delta, axis=-1)


def general(
    fast_pos,
    fast_vel,
    fast_charge,
    fast_owner,
    exclusions,
    slow_pos,
    slow_vel,
    slow_charge,
    neighbours,
):
    row_count = lax.axis_size("row")
    col_count = lax.axis_size("col")
    row_index = lax.axis_index("row")
    col_index = lax.axis_index("col")
    flat_index = row_index * col_count + col_index
    piece = fast_pos.shape[1]
    cell_rows = slow_pos.shape[1]
    cell_cols = slow_pos.shape[2]
    total_cols = cell_cols * col_count
    coords = owner_coords(fast_owner, total_cols)
    block_width = col_count * piece
    block_start = row_index * block_width
    rows_cells = lax.dynamic_slice_in_dim(coords, block_start, block_width, 1)
    rows_charge = lax.dynamic_slice_in_dim(fast_charge, block_start, block_width, 0)
    rows_exclude = lax.dynamic_slice_in_dim(exclusions, block_start, block_width, 0)
    column_atoms = (
        (jnp.arange(row_count, dtype=jnp.int32) * col_count + col_index)[:, None] * piece
        + jnp.arange(piece, dtype=jnp.int32)[None, :]
    ).reshape(-1)
    column_cells = jnp.take(coords, column_atoms, axis=1)
    column_charge = jnp.take(fast_charge, column_atoms, axis=0)

    def fast_force(frac):
        rows_pos = lax.all_gather(frac, "col", axis=1, tiled=True)
        cols_pos = lax.all_gather(frac, "row", axis=1, tiled=True)
        partial_force = pair_fast(
            rows_pos,
            rows_cells,
            rows_charge,
            rows_exclude,
            cols_pos,
            column_cells,
            column_charge,
            column_atoms,
        )
        return lax.psum_scatter(partial_force, "col", scatter_dimension=1, tiled=True)

    grid_row = fast_owner // total_cols - row_index * cell_rows
    grid_col = fast_owner % total_cols - col_index * cell_cols
    inside = (grid_row >= 0) & (grid_row < cell_rows) & (grid_col >= 0) & (grid_col < cell_cols)
    local_cell = grid_row * cell_cols + grid_col
    cell_ids = jnp.arange(cell_rows * cell_cols, dtype=jnp.int32)
    select = jnp.where(
        inside[:, None] & (local_cell[:, None] == cell_ids[None, :]),
        jnp.float32(1.0),
        jnp.float32(0.0),
    )

    def slow_both(spos, frac):
        data = jnp.concatenate([spos, slow_charge[None]], axis=0)
        padded = with_halo(data, (("row", 1), ("col", 2)), 2)
        views = jnp.stack(
            [padded[:, o // 5 : o // 5 + cell_rows, o % 5 : o % 5 + cell_cols] for o in range(25)]
        )
        cell_force = slow_cells(data, views, neighbours)
        everyone = lax.all_gather(frac, ("row", "col"), axis=1, tiled=True)
        table = jnp.transpose(data, (1, 2, 0, 3)).reshape(cell_rows * cell_cols, 4 * CELL)
        picked = jnp.dot(
            select, table, precision=lax.Precision.HIGHEST, preferred_element_type=jnp.float32
        )
        picked = jnp.transpose(picked.reshape(fast_charge.shape[0], 4, CELL), (1, 0, 2))
        partial_env = fast_from_cells(everyone, fast_charge, picked)
        summed = lax.psum(partial_env, ("row", "col"))
        own_env = lax.dynamic_slice_in_dim(summed, flat_index * piece, piece, 1)
        return (cell_force, own_env)

    half_outer = 0.5 * outer_dt
    inner_dt = outer_dt / INNER
    fast_acc = fast_force(fast_pos)
    slow_acc, env_acc = slow_both(slow_pos, fast_pos)
    slow_vel = slow_vel + half_outer * slow_acc
    fast_vel = fast_vel + half_outer * env_acc
    for _ in range(INNER):
        fast_vel = fast_vel + 0.5 * inner_dt * fast_acc
        fast_pos = fast_pos + inner_dt * fast_vel
        fast_acc = fast_force(fast_pos)
        fast_vel = fast_vel + 0.5 * inner_dt * fast_acc
    slow_pos = slow_pos + outer_dt * slow_vel
    slow_acc, env_acc = slow_both(slow_pos, fast_pos)
    slow_vel = slow_vel + half_outer * slow_acc
    fast_vel = fast_vel + half_outer * env_acc
    return (fast_pos, fast_vel, slow_pos, slow_vel)


def solution(mesh):
    both = P(None, ("row", "col"))

    def run(*args):
        rows, cols = args[5].shape[1:3]
        powers = all(n & (n - 1) == 0 for n in (rows, cols, *mesh.shape.values()))
        special = args[0].shape[1] == LANES * mesh.size and powers
        step = jax.shard_map(
            per_device if special else general,
            mesh=mesh,
            in_specs=(
                both, both, P(), P(), P(),
                P(None, "row", "col", None), P(None, "row", "col", None),
                P("row", "col", None), P("row", "col", None),
            ),
            out_specs=(both, both, P(None, "row", "col", None), P(None, "row", "col", None)),
            check_vma=False,
        )
        return step(*args)

    return run
```

```python
import functools

import jax
import jax.numpy as jnp
from jax import lax
from jax.experimental import pallas as pl
from jax.experimental.pallas import tpu as pltpu
from jax.sharding import PartitionSpec as P


CELL = 128
INNER = 4
GROUPS = 256

fast_coupling = 1.0
slow_coupling = 0.1
outer_dt = 0.2
half_outer = 0.5 * outer_dt
inner_dt = outer_dt / INNER

BOTH = ("row", "col")
F32 = jnp.float32
BF16 = jnp.bfloat16
LANES = 128
ENV_UNROLL = 8
PARTS = 4


def in_hbm(x):
    return pltpu.with_memory_space_constraint(x, pltpu.HBM)


def position():
    return lax.axis_index("row") * lax.axis_size("col") + lax.axis_index("col")


VMEM = pl.BlockSpec(memory_space=pltpu.VMEM)
SMEM = pl.BlockSpec(memory_space=pltpu.SMEM)


def sds(shape, dtype=F32):
    return jax.ShapeDtypeStruct(shape, dtype)


def split3(x):
    hi = x.astype(BF16).astype(F32)
    rest = x - hi
    mid = rest.astype(BF16).astype(F32)
    return hi, mid, rest - mid


def norm_rows(y):
    row = lax.broadcasted_iota(jnp.int32, y.shape, 0)
    pos = jnp.where(row < 3, y, 0.0)
    return row, pos, jnp.sum(pos * pos, axis=0, keepdims=True)


def left_rows(y):
    row, pos, norm = norm_rows(y)
    hi, mid, lo = split3(jnp.where(row == 3, norm, jnp.where(row == 4, 1.0, pos)))
    return jnp.concatenate([hi, hi, mid, hi, mid, lo], axis=0)


def right_rows(y, soft):
    row, pos, norm = norm_rows(y)
    hi, mid, lo = split3(
        jnp.where(row == 3, 1.0, jnp.where(row == 4, norm + soft, -2.0 * pos))
    )
    return jnp.concatenate([hi, mid, hi, lo, mid, hi], axis=0)


def fast_rows(g_ref, table_ref, exm_ref, own, atoms, feat, dist, sums):
    count = g_ref.shape[0]
    members = exm_ref.shape[0]
    zeros = jnp.zeros((5, LANES), F32)
    me = jnp.concatenate([g_ref[own], zeros], axis=0) + table_ref[own]
    left = jnp.transpose(left_rows(me)).astype(BF16)
    part = max(1, count // PARTS)
    for start in range(0, count, part):
        for b in range(start, start + part):
            y = jnp.concatenate([g_ref[b], zeros], axis=0) + table_ref[b]
            atoms[b] = y
            feat[:, LANES * b : LANES * (b + 1)] = right_rows(y, 1.0).astype(BF16)
        at = slice(LANES * start, LANES * (start + part))
        dist[:, at] = jnp.dot(left, feat[:, at], preferred_element_type=F32)
    unroll = 2

    def body(i, carry):
        at = [pl.ds(pl.multiple_of((i * unroll + u) * 8, 8), 8) for u in range(unroll)]
        acc = [None] * unroll
        for b in range(count):
            y = [jnp.broadcast_to(atoms[b, c : c + 1, :], (8, LANES)) for c in range(4)]
            for u in range(unroll):
                r = lax.rsqrt(dist[at[u], LANES * b : LANES * (b + 1)])
                w = (y[3] * r) * (r * r)
                f = [w * y[0], w * y[1], w * y[2], w]
                acc[u] = f if acc[u] is None else [acc[u][c] + f[c] for c in range(4)]
        for u in range(unroll):
            for c in range(4):
                sums[c, at[u], :] = acc[u][c]
        return carry

    lax.fori_loop(0, LANES // (8 * unroll), body, 0)
    step = GROUPS // LANES
    part = pl.ds(lax.rem(own, step), members, stride=step)
    d = [me[c : c + 1] - atoms[part, c, :] for c in range(3)]
    r = lax.rsqrt(d[0] * d[0] + d[1] * d[1] + d[2] * d[2] + 1.0)
    w = (exm_ref[...] * atoms[part, 3, :]) * (r * (r * r))
    scale = fast_coupling * me[3:4]
    total = [jnp.sum(jnp.transpose(sums[c]), axis=0, keepdims=True) for c in range(4)]
    return [
        scale
        * (me[c : c + 1] * total[3] - total[c] - jnp.sum(w * d[c], axis=0, keepdims=True))
        for c in range(3)
    ]


def fast_only_kernel(g_ref, table_ref, exm_ref, f_ref, *scratch):
    rows = fast_rows(g_ref, table_ref, exm_ref, position(), *scratch)
    for c in range(3):
        f_ref[c : c + 1, :] = rows[c]


def fast_step_kernel(
    g_ref, table_ref, exm_ref, v_ref, send_ref, p_out, v_out, *scratch
):
    own = position()
    rows = fast_rows(g_ref, table_ref, exm_ref, own, *scratch)
    count = send_ref.shape[0]
    for c in range(3):
        v = v_ref[c : c + 1, :] + inner_dt * rows[c]
        p = g_ref[pl.ds(own, 1), c, :] + inner_dt * v
        v_out[c : c + 1, :] = v
        p_out[c : c + 1, :] = p
        send_ref[:, c, :] = jnp.broadcast_to(p, (count, LANES))


def fast_cost(count):
    pairs = count * LANES * LANES
    return pl.CostEstimate(flops=10 * pairs, transcendentals=pairs, bytes_accessed=count * 4096)


def fast_scratch(count):
    return [
        pltpu.VMEM((count, 8, LANES), F32),
        pltpu.VMEM((48, count * LANES), BF16),
        pltpu.VMEM((LANES, count * LANES), F32),
        pltpu.VMEM((4, LANES, LANES), F32),
    ]


def fast_only(g, table, exm):
    count = g.shape[0]
    return pl.pallas_call(
        fast_only_kernel,
        out_shape=sds((3, LANES)),
        in_specs=[VMEM] * 3,
        out_specs=VMEM,
        scratch_shapes=fast_scratch(count),
        cost_estimate=fast_cost(count),
        name="fast_only",
        compiler_params=pltpu.CompilerParams(vmem_limit_bytes=4 << 20),
    )(g, table, exm)


def fast_step(g, table, exm, v):
    count = g.shape[0]
    return pl.pallas_call(
        fast_step_kernel,
        out_shape=(sds((count, 3, LANES)), sds((3, LANES)), sds((3, LANES))),
        in_specs=[VMEM] * 4,
        out_specs=(VMEM,) * 3,
        scratch_shapes=fast_scratch(count),
        cost_estimate=fast_cost(count),
        name="fast_step",
        compiler_params=pltpu.CompilerParams(vmem_limit_bytes=4 << 20),
    )(g, table, exm, v)


def prep_kernel(
    grid, owner_hbm, q_hbm, ex_hbm, table_ref, exm_ref, list_ref,
    heads, owner_ref, q_ref, ex_ref, sems,
):
    total_cols, cell_rows, cell_cols = grid
    mine = pl.ds(pl.multiple_of(position() * LANES, LANES), LANES)
    first = pltpu.make_async_copy(owner_hbm.at[0 : heads.shape[0]], heads, sems.at[3])
    first.start()
    copies = [
        pltpu.make_async_copy(owner_hbm, owner_ref, sems.at[0]),
        pltpu.make_async_copy(q_hbm, q_ref, sems.at[1]),
        pltpu.make_async_copy(ex_hbm.at[:, mine], ex_ref, sems.at[2]),
    ]
    for copy in copies:
        copy.start()
    table_ref[...] = jnp.zeros_like(table_ref)
    row_bit = total_cols * cell_rows
    keep = -row_bit | (total_cols - cell_cols)
    here = lax.axis_index("row") * row_bit + lax.axis_index("col") * cell_cols
    first.wait()
    n = jnp.int32(0)
    batch = 16
    for start in range(0, GROUPS, batch):
        found = []
        for i in range(start, start + batch):
            cell = heads[i // LANES, i % LANES]
            other = (cell & keep) ^ here
            found.append((cell * GROUPS + i, lax.shift_right_logical(other - 1, 31)))
        for entry, inside in found:
            list_ref[n] = entry
            n = n + inside
    for k in range(ENV_UNROLL):
        list_ref[n + k] = -1
    list_ref[GROUPS + ENV_UNROLL] = n
    for copy in copies:
        copy.wait()
    owner = owner_ref[...]
    shift = total_cols.bit_length() - 1
    table_ref[:, 0, :] = (lax.shift_right_logical(owner, shift) - total_cols // 2).astype(F32)
    table_ref[:, 1, :] = ((owner & (total_cols - 1)) - total_cols // 2).astype(F32)
    table_ref[:, 3, :] = q_ref[...]
    ex = lax.shift_right_logical(ex_ref[...], GROUPS.bit_length() - 1)
    member = lax.broadcasted_iota(jnp.int32, exm_ref.shape, 0)
    barred = jnp.zeros(exm_ref.shape, F32)
    for k in range(ex_ref.shape[0]):
        barred = jnp.where(member == ex[k : k + 1], 1.0, barred)
    exm_ref[...] = barred


def prep(owner, q, exclusions, members, grid):
    count = owner.shape[0] // LANES
    hbm = pl.BlockSpec(memory_space=pltpu.HBM)
    return pl.pallas_call(
        functools.partial(prep_kernel, grid),
        out_shape=(
            sds((count, 8, LANES)), sds((members, LANES)),
            sds((GROUPS + ENV_UNROLL + 1,), jnp.int32),
        ),
        in_specs=[hbm, hbm, hbm],
        out_specs=(VMEM, VMEM, SMEM),
        scratch_shapes=[
            pltpu.SMEM((8 * pl.cdiv(GROUPS, 8 * LANES), LANES), jnp.int32),
            pltpu.VMEM((count, LANES), jnp.int32),
            pltpu.VMEM((count, LANES), F32),
            pltpu.VMEM((exclusions.shape[1], LANES), jnp.int32),
            pltpu.SemaphoreType.DMA((4,)),
        ],
        name="prep",
        compiler_params=pltpu.CompilerParams(vmem_limit_bytes=2 << 20),
    )(*(in_hbm(x) for x in (owner.reshape(count, LANES), q, exclusions.T)))


def env_kernel(grid, list_ref, g_ref, cells_ref, out_ref, planes, sums):
    total_cols, cell_rows, cell_cols = grid
    step = GROUPS // LANES
    members = g_ref.shape[0] // step
    for c in range(3):
        for h in range(step):
            planes[c, h] = g_ref[pl.ds(h, members, stride=step), c, :]
    sums[...] = jnp.zeros_like(sums)
    lane = lax.broadcasted_iota(jnp.int32, (members, LANES), 1)

    def body(t, carry):
        for u in range(ENV_UNROLL):
            n = t * ENV_UNROLL + u
            entry = list_ref[n]
            group = entry & (GROUPS - 1)
            h = lax.shift_right_logical(group, LANES.bit_length() - 1)
            here = (lane == (group & (LANES - 1))) & (entry >= 0)
            number = jnp.maximum(lax.shift_right_arithmetic(entry, GROUPS.bit_length() - 1), 0)
            r = lax.div(number, total_cols) & (cell_rows - 1)
            cell = cells_ref[r * cell_cols + (number & (cell_cols - 1))]
            d = []
            for c in range(3):
                x = jnp.sum(jnp.where(here, planes[c, h], 0.0), axis=1, keepdims=True)
                d.append(x - cell[c : c + 1, :])
            r = lax.rsqrt(d[0] * d[0] + d[1] * d[1] + d[2] * d[2] + 0.5)
            w = (cell[3:4, :] * r) * (r * r)
            for c in range(3):
                f = jnp.sum(w * d[c], axis=1, keepdims=True)
                sums[c, h] = sums[c, h] + jnp.where(here, f, 0.0)
        return carry

    lax.fori_loop(0, lax.div(list_ref[GROUPS + ENV_UNROLL] + (ENV_UNROLL - 1), ENV_UNROLL), body, 0)
    for c in range(3):
        for h in range(step):
            out_ref[pl.ds(h, members, stride=step), c, :] = sums[c, h]


def env(groups, g, cells, grid):
    count = g.shape[0]
    step = GROUPS // LANES
    members = count // step
    return pl.pallas_call(
        functools.partial(env_kernel, grid),
        out_shape=sds((count, 3, LANES)),
        in_specs=[SMEM, VMEM, VMEM],
        out_specs=VMEM,
        scratch_shapes=[
            pltpu.VMEM((3, step, members, LANES), F32),
            pltpu.VMEM((3, step, members, LANES), F32),
        ],
        cost_estimate=pl.CostEstimate(flops=2_000_000, transcendentals=60000, bytes_accessed=200000),
        name="env",
        compiler_params=pltpu.CompilerParams(vmem_limit_bytes=2 << 20),
    )(groups, g, cells)


def kick_kernel(e_ref, f_ref, q_ref, p_ref, v_ref, send_ref, p_out, v_out):
    scale = slow_coupling * q_ref[pl.ds(position(), 1), :]
    count = send_ref.shape[0]
    for c in range(3):
        e = scale * jnp.sum(e_ref[:, c, :], axis=0, keepdims=True)
        v = v_ref[c : c + 1, :] + half_outer * e + 0.5 * inner_dt * f_ref[c : c + 1, :]
        p = p_ref[c : c + 1, :] + inner_dt * v
        v_out[c : c + 1, :] = v
        p_out[c : c + 1, :] = p
        send_ref[:, c, :] = jnp.broadcast_to(p, (count, LANES))


def kick(e, f, q, p, v):
    count = e.shape[0]
    return pl.pallas_call(
        kick_kernel,
        out_shape=(sds((count, 3, LANES)), sds((3, LANES)), sds((3, LANES))),
        in_specs=[VMEM] * 5,
        out_specs=(VMEM,) * 3,
        name="kick",
        compiler_params=pltpu.CompilerParams(vmem_limit_bytes=2 << 20),
    )(e, f, q, p, v)


def last_kick_kernel(e_ref, f_ref, q_ref, v_ref, v_out):
    scale = slow_coupling * q_ref[pl.ds(position(), 1), :]
    for c in range(3):
        e = scale * jnp.sum(e_ref[:, c, :], axis=0, keepdims=True)
        v_out[c : c + 1, :] = (
            v_ref[c : c + 1, :] + 0.5 * inner_dt * f_ref[c : c + 1, :] + half_outer * e
        )


def last_kick(e, f, q, v):
    return pl.pallas_call(
        last_kick_kernel,
        out_shape=sds((3, LANES)),
        in_specs=[VMEM] * 4,
        out_specs=VMEM,
        name="last_kick",
        compiler_params=pltpu.CompilerParams(vmem_limit_bytes=2 << 20),
    )(e, f, q, v)


def slow_kernel(first, row0, nb_ref, tab_ref, vel_ref, *refs):
    earlier = (2 if first else 1) if row0 else 0
    results = 2 if first or row0 else 1
    before, refs = refs[:earlier], refs[earlier:]
    outs, scratch = refs[:results], refs[results:]
    totals = scratch[8]
    if first:
        fetch = pltpu.make_async_copy(vel_ref.at[:, row0 : outs[0].shape[1]], scratch[9], scratch[10])
        fetch.start()
    vel_out = outs[0]
    if first:
        cell_out = outs[1]
    elif row0:
        pos_out = outs[1]
    bufs = [tuple(scratch[0:4]), tuple(scratch[4:8])]
    cell_rows, cell_cols = vel_out.shape[1] - row0, vel_out.shape[2]
    slots = nb_ref.shape[1]
    count = cell_rows * cell_cols
    skip = row0 * cell_cols
    if row0:
        vel_out[:, :row0] = before[0][...]
        if first:
            cell_out[:skip] = before[1][...]
    row8 = lax.broadcasted_iota(jnp.int32, (8, CELL), 0)

    def place(n):
        return lax.shift_right_logical(n, cell_cols.bit_length() - 1), n & (cell_cols - 1)

    def load8(r, c):
        t = tab_ref[r, c]
        return jnp.concatenate([t, jnp.zeros_like(t)], axis=0)

    def distances(n, buf):
        feat, ys, dist, _ = buf
        r, c = place(n)
        left = jnp.transpose(left_rows(load8(r + (row0 + 2), c + 2))).astype(BF16)
        for k in range(slots):
            o = nb_ref[n + row0 * cell_cols, k]
            dr = lax.shift_right_logical(o * 13, 6)
            dc = o - 5 * dr
            y = load8(r + (dr + row0), c + dc)
            y = y + jnp.where(
                row8 == 0, (dr - 2).astype(F32), jnp.where(row8 == 1, (dc - 2).astype(F32), 0.0)
            )
            ys[8 * k : 8 * k + 8] = y
            feat[:, CELL * k : CELL * (k + 1)] = right_rows(y, 0.5).astype(BF16)
        dist[...] = jnp.dot(left, feat[...], preferred_element_type=F32)

    def pairs(buf):
        _, ys, dist, sums = buf
        for g in range(0, CELL // 8, 2):
            at = [slice(8 * (g + h), 8 * (g + h) + 8) for h in range(2)]
            acc = [None, None]
            for k in range(slots):
                y = [jnp.broadcast_to(ys[8 * k + x : 8 * k + x + 1], (8, CELL)) for x in range(4)]
                for h in range(2):
                    i = lax.rsqrt(dist[at[h], CELL * k : CELL * (k + 1)])
                    w = (y[3] * i) * (i * i)
                    f = [w * y[0], w * y[1], w * y[2], w]
                    acc[h] = f if acc[h] is None else [acc[h][x] + f[x] for x in range(4)]
            for h in range(2):
                for x in range(4):
                    sums[x, at[h], :] = acc[h][x]

    def finish(n, buf):
        sums = buf[3]
        for x in range(4):
            totals[n, x : x + 1, :] = jnp.sum(jnp.transpose(sums[x]), axis=0, keepdims=True)

    distances(0, bufs[0])

    def body(i, carry):
        n = 2 * i
        distances(n + 1, bufs[1])
        pairs(bufs[0])
        finish(jnp.maximum(n - 1, 0), bufs[1])
        distances(jnp.minimum(n + 2, count - 1), bufs[0])
        pairs(bufs[1])
        finish(n, bufs[0])
        return carry

    lax.fori_loop(0, count // 2, body, 0)
    finish(count - 1, bufs[1])
    if first:
        fetch.wait()
    rows = slice(row0, row0 + cell_rows)
    inner = (slice(row0 + 2, row0 + 2 + cell_rows), slice(2, 2 + cell_cols))
    charge = tab_ref[inner[0], inner[1], 3, :].reshape(count, CELL)
    for x in range(3):
        p = tab_ref[inner[0], inner[1], x, :].reshape(count, CELL)
        f = slow_coupling * charge * (p * totals[:, 3, :] - totals[:, x, :])
        v = (scratch[9][x] if first else vel_ref[x, rows]) + half_outer * f.reshape(cell_rows, cell_cols, CELL)
        vel_out[x, rows] = v
        if first:
            p = p + outer_dt * v.reshape(count, CELL)
            cell_out[skip:, x, :] = p
        elif row0:
            pos_out[x] = tab_ref[2 : 2 + row0 + cell_rows, inner[1], x, :]
    if first:
        cell_out[skip:, 3, :] = charge


def slow(first, row0, rows, nb, tab, vel, before=()):
    shape = (3, row0 + rows) + vel.shape[2:]
    own = rows * vel.shape[2]
    slots = nb.shape[1]
    out = (sds(shape),)
    if first:
        out += (sds(((row0 + rows) * vel.shape[2], 4, CELL)),)
    elif row0:
        out += (sds(shape),)
    pairs = own * slots * CELL * CELL
    return pl.pallas_call(
        functools.partial(slow_kernel, first, row0),
        out_shape=out,
        in_specs=[SMEM, VMEM, pl.BlockSpec(memory_space=pltpu.HBM) if first else VMEM]
        + [VMEM] * len(before),
        out_specs=(VMEM,) * len(out),
        scratch_shapes=[
            pltpu.VMEM((48, slots * CELL), BF16),
            pltpu.VMEM((8 * slots, CELL), F32),
            pltpu.VMEM((CELL, slots * CELL), F32),
            pltpu.VMEM((4, CELL, CELL), F32),
        ] * 2 + [pltpu.VMEM((own, 4, CELL), F32)]
        + ([pltpu.VMEM((3, rows) + vel.shape[2:], F32), pltpu.SemaphoreType.DMA] if first else []),
        compiler_params=pltpu.CompilerParams(vmem_limit_bytes=4 << 20),
        cost_estimate=pl.CostEstimate(
            flops=10 * pairs, transcendentals=pairs, bytes_accessed=1_000_000
        ),
        name="slow",
    )(nb, tab, in_hbm(vel) if first else vel, *before)


def with_halo(x, sides, width):
    for axis, dim in sides:
        count, length = (lax.axis_size(axis), x.shape[dim])
        up = [(i, (i + 1) % count) for i in range(count)]
        down = [(j, i) for i, j in up]
        last = lax.slice_in_dim(x, length - width, length, axis=dim)
        initial = lax.slice_in_dim(x, 0, width, axis=dim)
        before = lax.ppermute(last, axis, up)
        after = lax.ppermute(initial, axis, down)
        x = jnp.concatenate([before, x, after], axis=dim)
    return x


def exchange(x):
    return lax.all_to_all(x, BOTH, 0, 0)


def per_device(*args):
    return rows_of_lanes(*args)


def rows_of_lanes(
    fast_pos, fast_vel, fast_charge, fast_owner, exclusions,
    slow_pos, slow_vel, slow_charge, neighbours,
):
    row_count, col_count = lax.axis_size("row"), lax.axis_size("col")
    count = row_count * col_count
    piece = fast_pos.shape[1]
    cell_rows, cell_cols = slow_pos.shape[1], slow_pos.shape[2]
    total_cols = cell_cols * col_count

    g = exchange(jnp.broadcast_to(fast_pos[None], (count, 3, piece)))

    q = fast_charge.reshape(count, piece)
    members = fast_charge.shape[0] // GROUPS
    grid = (total_cols, cell_rows, cell_cols)
    table, exm, groups = prep(fast_owner, q, exclusions, members, grid)

    cells = jnp.concatenate([slow_pos, slow_charge[None]], axis=0).transpose(1, 2, 0, 3)
    sides = (("row", 0), ("col", 1))
    nb = neighbours.reshape(cell_rows * cell_cols, -1)
    half = cell_rows // 2
    tab = with_halo(cells, sides, 2)
    part = ()
    for r0 in (0, half):
        part = slow(True, r0, half, nb, tab, slow_vel, part)
    slow_vel, cells2 = part
    tab2 = with_halo(cells2.reshape(cells.shape), sides, 2)
    part = ()
    for r0 in (0, half):
        part = slow(False, r0, half, nb, tab2, slow_vel, part)
    slow_vel, slow_pos = part

    back = exchange(env(groups, g, cells.reshape(cells2.shape), grid))
    f = fast_only(g, table, exm)
    send, p, v = kick(back, f, q, fast_pos, fast_vel)
    for _ in range(INNER - 1):
        g = exchange(send)
        send, p, v = fast_step(g, table, exm, v)
    g = exchange(send)
    back = exchange(env(groups, g, cells2, grid))
    f = fast_only(g, table, exm)
    v = last_kick(back, f, q, v)
    return (p, v, slow_pos, slow_vel)


def owner_coords(owner, total_cols):
    grid_row = (owner // total_cols).astype(jnp.float32)
    grid_col = (owner % total_cols).astype(jnp.float32)
    return jnp.stack([grid_row, grid_col, jnp.zeros_like(grid_row)])


def pair_fast(pos_a, cell_a, charge_a, exclude_a, pos_b, cell_b, charge_b, index_b):
    delta = pos_a[:, :, None] - pos_b[:, None, :] + (cell_a[:, :, None] - cell_b[:, None, :])
    dist_sq = jnp.sum(delta * delta, axis=0) + 1.0
    inverse = 1.0 / (dist_sq * jnp.sqrt(dist_sq))
    barred = jnp.any(exclude_a[:, :, None] == index_b[None, None, :], axis=1)
    weight = jnp.where(barred, jnp.float32(0.0), charge_a[:, None] * charge_b[None, :] * inverse)
    return fast_coupling * jnp.sum(weight[None] * delta, axis=2)


def slow_cells(own, views, lists):
    force = jnp.zeros((3,) + own.shape[1:], jnp.float32)
    offsets = jnp.arange(25, dtype=jnp.int32)
    for slot in range(lists.shape[-1]):
        chosen = lists[..., slot]
        pick = (chosen[..., None] == offsets).astype(jnp.float32)
        other = jnp.einsum("abo,oxabn->xabn", pick, views, precision=lax.Precision.HIGHEST)
        shift_row = (chosen // 5 - 2).astype(jnp.float32)
        shift_col = (chosen % 5 - 2).astype(jnp.float32)
        shift = jnp.stack([shift_row, shift_col, jnp.zeros_like(shift_row)])
        delta = own[0:3, :, :, :, None] - (other[0:3, :, :, None, :] + shift[:, :, :, None, None])
        dist_sq = jnp.sum(delta * delta, axis=0) + 0.5
        inverse = 1.0 / (dist_sq * jnp.sqrt(dist_sq))
        weight = other[3][:, :, None, :] * inverse
        force = force + jnp.sum(weight[None] * delta, axis=-1)
    return slow_coupling * own[3][None] * force


def fast_from_cells(frac, charge, picked):
    delta = frac[:, :, None] - picked[0:3]
    dist_sq = jnp.sum(delta * delta, axis=0) + 0.5
    inverse = 1.0 / (dist_sq * jnp.sqrt(dist_sq))
    weight = picked[3] * inverse
    return slow_coupling * charge[None, :] * jnp.sum(weight[None] * delta, axis=-1)


def general(
    fast_pos,
    fast_vel,
    fast_charge,
    fast_owner,
    exclusions,
    slow_pos,
    slow_vel,
    slow_charge,
    neighbours,
):
    row_count = lax.axis_size("row")
    col_count = lax.axis_size("col")
    row_index = lax.axis_index("row")
    col_index = lax.axis_index("col")
    flat_index = row_index * col_count + col_index
    piece = fast_pos.shape[1]
    cell_rows = slow_pos.shape[1]
    cell_cols = slow_pos.shape[2]
    total_cols = cell_cols * col_count
    coords = owner_coords(fast_owner, total_cols)
    block_width = col_count * piece
    block_start = row_index * block_width
    rows_cells = lax.dynamic_slice_in_dim(coords, block_start, block_width, 1)
    rows_charge = lax.dynamic_slice_in_dim(fast_charge, block_start, block_width, 0)
    rows_exclude = lax.dynamic_slice_in_dim(exclusions, block_start, block_width, 0)
    column_atoms = (
        (jnp.arange(row_count, dtype=jnp.int32) * col_count + col_index)[:, None] * piece
        + jnp.arange(piece, dtype=jnp.int32)[None, :]
    ).reshape(-1)
    column_cells = jnp.take(coords, column_atoms, axis=1)
    column_charge = jnp.take(fast_charge, column_atoms, axis=0)

    def fast_force(frac):
        rows_pos = lax.all_gather(frac, "col", axis=1, tiled=True)
        cols_pos = lax.all_gather(frac, "row", axis=1, tiled=True)
        partial_force = pair_fast(
            rows_pos,
            rows_cells,
            rows_charge,
            rows_exclude,
            cols_pos,
            column_cells,
            column_charge,
            column_atoms,
        )
        return lax.psum_scatter(partial_force, "col", scatter_dimension=1, tiled=True)

    grid_row = fast_owner // total_cols - row_index * cell_rows
    grid_col = fast_owner % total_cols - col_index * cell_cols
    inside = (grid_row >= 0) & (grid_row < cell_rows) & (grid_col >= 0) & (grid_col < cell_cols)
    local_cell = grid_row * cell_cols + grid_col
    cell_ids = jnp.arange(cell_rows * cell_cols, dtype=jnp.int32)
    select = jnp.where(
        inside[:, None] & (local_cell[:, None] == cell_ids[None, :]),
        jnp.float32(1.0),
        jnp.float32(0.0),
    )

    def slow_both(spos, frac):
        data = jnp.concatenate([spos, slow_charge[None]], axis=0)
        padded = with_halo(data, (("row", 1), ("col", 2)), 2)
        views = jnp.stack(
            [padded[:, o // 5 : o // 5 + cell_rows, o % 5 : o % 5 + cell_cols] for o in range(25)]
        )
        cell_force = slow_cells(data, views, neighbours)
        everyone = lax.all_gather(frac, ("row", "col"), axis=1, tiled=True)
        table = jnp.transpose(data, (1, 2, 0, 3)).reshape(cell_rows * cell_cols, 4 * CELL)
        picked = jnp.dot(
            select, table, precision=lax.Precision.HIGHEST, preferred_element_type=jnp.float32
        )
        picked = jnp.transpose(picked.reshape(fast_charge.shape[0], 4, CELL), (1, 0, 2))
        partial_env = fast_from_cells(everyone, fast_charge, picked)
        summed = lax.psum(partial_env, ("row", "col"))
        own_env = lax.dynamic_slice_in_dim(summed, flat_index * piece, piece, 1)
        return (cell_force, own_env)

    half_outer = 0.5 * outer_dt
    inner_dt = outer_dt / INNER
    fast_acc = fast_force(fast_pos)
    slow_acc, env_acc = slow_both(slow_pos, fast_pos)
    slow_vel = slow_vel + half_outer * slow_acc
    fast_vel = fast_vel + half_outer * env_acc
    for _ in range(INNER):
        fast_vel = fast_vel + 0.5 * inner_dt * fast_acc
        fast_pos = fast_pos + inner_dt * fast_vel
        fast_acc = fast_force(fast_pos)
        fast_vel = fast_vel + 0.5 * inner_dt * fast_acc
    slow_pos = slow_pos + outer_dt * slow_vel
    slow_acc, env_acc = slow_both(slow_pos, fast_pos)
    slow_vel = slow_vel + half_outer * slow_acc
    fast_vel = fast_vel + half_outer * env_acc
    return (fast_pos, fast_vel, slow_pos, slow_vel)


def solution(mesh):
    both = P(None, ("row", "col"))

    def run(*args):
        rows, cols = args[5].shape[1:3]
        powers = all(n & (n - 1) == 0 for n in (rows, cols, *mesh.shape.values()))
        special = args[0].shape[1] == LANES * mesh.size and powers
        step = jax.shard_map(
            per_device if special else general,
            mesh=mesh,
            in_specs=(
                both, both, P(), P(), P(),
                P(None, "row", "col", None), P(None, "row", "col", None),
                P("row", "col", None), P("row", "col", None),
            ),
            out_specs=(both, both, P(None, "row", "col", None), P(None, "row", "col", None)),
            check_vma=False,
        )
        return step(*args)

    return run
```

```python
import functools

import jax
import jax.numpy as jnp
from jax import lax
from jax.experimental import pallas as pl
from jax.experimental.pallas import tpu as pltpu
from jax.sharding import PartitionSpec as P


CELL = 128
INNER = 4
GROUPS = 256

fast_coupling = 1.0
slow_coupling = 0.1
outer_dt = 0.2
half_outer = 0.5 * outer_dt
inner_dt = outer_dt / INNER

BOTH = ("row", "col")
F32 = jnp.float32
BF16 = jnp.bfloat16
LANES = 128
ENV_UNROLL = 12
PARTS = 4


def in_hbm(x):
    return pltpu.with_memory_space_constraint(x, pltpu.HBM)


def position():
    return lax.axis_index("row") * lax.axis_size("col") + lax.axis_index("col")


VMEM = pl.BlockSpec(memory_space=pltpu.VMEM)
SMEM = pl.BlockSpec(memory_space=pltpu.SMEM)


def sds(shape, dtype=F32):
    return jax.ShapeDtypeStruct(shape, dtype)


def split3(x):
    hi = x.astype(BF16).astype(F32)
    rest = x - hi
    mid = rest.astype(BF16).astype(F32)
    return hi, mid, rest - mid


def norm_rows(y):
    row = lax.broadcasted_iota(jnp.int32, y.shape, 0)
    pos = jnp.where(row < 3, y, 0.0)
    return row, pos, jnp.sum(pos * pos, axis=0, keepdims=True)


def left_rows(y):
    row, pos, norm = norm_rows(y)
    hi, mid, lo = split3(jnp.where(row == 3, norm, jnp.where(row == 4, 1.0, pos)))
    return jnp.concatenate([hi, hi, mid, hi, mid, lo], axis=0)


def right_rows(y, soft):
    row, pos, norm = norm_rows(y)
    hi, mid, lo = split3(
        jnp.where(row == 3, 1.0, jnp.where(row == 4, norm + soft, -2.0 * pos))
    )
    return jnp.concatenate([hi, mid, hi, lo, mid, hi], axis=0)


def fast_rows(g_ref, table_ref, exm_ref, own, atoms, feat, dist, sums):
    count = g_ref.shape[0]
    members = exm_ref.shape[0]
    zeros = jnp.zeros((5, LANES), F32)
    me = jnp.concatenate([g_ref[own], zeros], axis=0) + table_ref[own]
    left = jnp.transpose(left_rows(me)).astype(BF16)
    part = max(1, count // PARTS)
    for start in range(0, count, part):
        for b in range(start, start + part):
            y = jnp.concatenate([g_ref[b], zeros], axis=0) + table_ref[b]
            atoms[b] = y
            feat[:, LANES * b : LANES * (b + 1)] = right_rows(y, 1.0).astype(BF16)
        at = slice(LANES * start, LANES * (start + part))
        dist[:, at] = jnp.dot(left, feat[:, at], preferred_element_type=F32)
    unroll = 16

    def body(i, carry):
        at = [pl.ds(pl.multiple_of((i * unroll + u) * 8, 8), 8) for u in range(unroll)]
        acc = [None] * unroll
        for b in range(count):
            y = [jnp.broadcast_to(atoms[b, c : c + 1, :], (8, LANES)) for c in range(4)]
            for u in range(unroll):
                r = lax.rsqrt(dist[at[u], LANES * b : LANES * (b + 1)])
                w = (y[3] * r) * (r * r)
                f = [w * y[0], w * y[1], w * y[2], w]
                acc[u] = f if acc[u] is None else [acc[u][c] + f[c] for c in range(4)]
        for u in range(unroll):
            for c in range(4):
                sums[c, at[u], :] = acc[u][c]
        return carry

    lax.fori_loop(0, LANES // (8 * unroll), body, 0)
    step = GROUPS // LANES
    part = pl.ds(lax.rem(own, step), members, stride=step)
    d = [me[c : c + 1] - atoms[part, c, :] for c in range(3)]
    r = lax.rsqrt(d[0] * d[0] + d[1] * d[1] + d[2] * d[2] + 1.0)
    w = (exm_ref[...] * atoms[part, 3, :]) * (r * (r * r))
    scale = fast_coupling * me[3:4]
    total = [jnp.sum(jnp.transpose(sums[c]), axis=0, keepdims=True) for c in range(4)]
    return [
        scale
        * (me[c : c + 1] * total[3] - total[c] - jnp.sum(w * d[c], axis=0, keepdims=True))
        for c in range(3)
    ]


def fast_only_kernel(g_ref, table_ref, exm_ref, f_ref, *scratch):
    rows = fast_rows(g_ref, table_ref, exm_ref, position(), *scratch)
    for c in range(3):
        f_ref[c : c + 1, :] = rows[c]


def fast_step_kernel(
    g_ref, table_ref, exm_ref, v_ref, send_ref, p_out, v_out, *scratch
):
    own = position()
    rows = fast_rows(g_ref, table_ref, exm_ref, own, *scratch)
    count = send_ref.shape[0]
    for c in range(3):
        v = v_ref[c : c + 1, :] + inner_dt * rows[c]
        p = g_ref[pl.ds(own, 1), c, :] + inner_dt * v
        v_out[c : c + 1, :] = v
        p_out[c : c + 1, :] = p
        send_ref[:, c, :] = jnp.broadcast_to(p, (count, LANES))


def fast_cost(count):
    pairs = count * LANES * LANES
    return pl.CostEstimate(flops=10 * pairs, transcendentals=pairs, bytes_accessed=count * 4096)


def fast_scratch(count):
    return [
        pltpu.VMEM((count, 8, LANES), F32),
        pltpu.VMEM((48, count * LANES), BF16),
        pltpu.VMEM((LANES, count * LANES), F32),
        pltpu.VMEM((4, LANES, LANES), F32),
    ]


def fast_only(g, table, exm):
    count = g.shape[0]
    return pl.pallas_call(
        fast_only_kernel,
        out_shape=sds((3, LANES)),
        in_specs=[VMEM] * 3,
        out_specs=VMEM,
        scratch_shapes=fast_scratch(count),
        cost_estimate=fast_cost(count),
        name="fast_only",
        compiler_params=pltpu.CompilerParams(vmem_limit_bytes=4 << 20),
    )(g, table, exm)


def fast_step(g, table, exm, v):
    count = g.shape[0]
    return pl.pallas_call(
        fast_step_kernel,
        out_shape=(sds((count, 3, LANES)), sds((3, LANES)), sds((3, LANES))),
        in_specs=[VMEM] * 4,
        out_specs=(VMEM,) * 3,
        scratch_shapes=fast_scratch(count),
        cost_estimate=fast_cost(count),
        name="fast_step",
        compiler_params=pltpu.CompilerParams(vmem_limit_bytes=4 << 20),
    )(g, table, exm, v)


def prep_kernel(
    grid, owner_hbm, q_hbm, ex_hbm, table_ref, exm_ref, list_ref,
    heads, owner_ref, q_ref, ex_ref, sems,
):
    total_cols, cell_rows, cell_cols = grid
    mine = pl.ds(pl.multiple_of(position() * LANES, LANES), LANES)
    first = pltpu.make_async_copy(owner_hbm.at[0 : heads.shape[0]], heads, sems.at[3])
    first.start()
    copies = [
        pltpu.make_async_copy(owner_hbm, owner_ref, sems.at[0]),
        pltpu.make_async_copy(q_hbm, q_ref, sems.at[1]),
        pltpu.make_async_copy(ex_hbm.at[:, mine], ex_ref, sems.at[2]),
    ]
    for copy in copies:
        copy.start()
    table_ref[...] = jnp.zeros_like(table_ref)
    row_bit = total_cols * cell_rows
    keep = -row_bit | (total_cols - cell_cols)
    here = lax.axis_index("row") * row_bit + lax.axis_index("col") * cell_cols
    first.wait()
    n = jnp.int32(0)
    batch = 16
    for start in range(0, GROUPS, batch):
        found = []
        for i in range(start, start + batch):
            cell = heads[i // LANES, i % LANES]
            other = (cell & keep) ^ here
            found.append((cell * GROUPS + i, lax.shift_right_logical(other - 1, 31)))
        for entry, inside in found:
            list_ref[n] = entry
            n = n + inside
    for k in range(ENV_UNROLL):
        list_ref[n + k] = -1
    list_ref[GROUPS + ENV_UNROLL] = n
    for copy in copies:
        copy.wait()
    owner = owner_ref[...]
    shift = total_cols.bit_length() - 1
    table_ref[:, 0, :] = (lax.shift_right_logical(owner, shift) - total_cols // 2).astype(F32)
    table_ref[:, 1, :] = ((owner & (total_cols - 1)) - total_cols // 2).astype(F32)
    table_ref[:, 3, :] = q_ref[...]
    ex = lax.shift_right_logical(ex_ref[...], GROUPS.bit_length() - 1)
    member = lax.broadcasted_iota(jnp.int32, exm_ref.shape, 0)
    barred = jnp.zeros(exm_ref.shape, F32)
    for k in range(ex_ref.shape[0]):
        barred = jnp.where(member == ex[k : k + 1], 1.0, barred)
    exm_ref[...] = barred


def prep(owner, q, exclusions, members, grid):
    count = owner.shape[0] // LANES
    hbm = pl.BlockSpec(memory_space=pltpu.HBM)
    return pl.pallas_call(
        functools.partial(prep_kernel, grid),
        out_shape=(
            sds((count, 8, LANES)), sds((members, LANES)),
            sds((GROUPS + ENV_UNROLL + 1,), jnp.int32),
        ),
        in_specs=[hbm, hbm, hbm],
        out_specs=(VMEM, VMEM, SMEM),
        scratch_shapes=[
            pltpu.SMEM((8 * pl.cdiv(GROUPS, 8 * LANES), LANES), jnp.int32),
            pltpu.VMEM((count, LANES), jnp.int32),
            pltpu.VMEM((count, LANES), F32),
            pltpu.VMEM((exclusions.shape[1], LANES), jnp.int32),
            pltpu.SemaphoreType.DMA((4,)),
        ],
        name="prep",
        compiler_params=pltpu.CompilerParams(vmem_limit_bytes=2 << 20),
    )(*(in_hbm(x) for x in (owner.reshape(count, LANES), q, exclusions.T)))


def env_kernel(grid, list_ref, g_ref, cells_ref, out_ref, planes, sums):
    total_cols, cell_rows, cell_cols = grid
    step = GROUPS // LANES
    members = g_ref.shape[0] // step
    for c in range(3):
        for h in range(step):
            planes[c, h] = g_ref[pl.ds(h, members, stride=step), c, :]
    sums[...] = jnp.zeros_like(sums)
    lane = lax.broadcasted_iota(jnp.int32, (members, LANES), 1)

    def body(t, carry):
        for u in range(ENV_UNROLL):
            n = t * ENV_UNROLL + u
            entry = list_ref[n]
            group = entry & (GROUPS - 1)
            h = lax.shift_right_logical(group, LANES.bit_length() - 1)
            here = (lane == (group & (LANES - 1))) & (entry >= 0)
            number = jnp.maximum(lax.shift_right_arithmetic(entry, GROUPS.bit_length() - 1), 0)
            r = lax.div(number, total_cols) & (cell_rows - 1)
            cell = cells_ref[r * cell_cols + (number & (cell_cols - 1))]
            d = []
            for c in range(3):
                x = jnp.sum(jnp.where(here, planes[c, h], 0.0), axis=1, keepdims=True)
                d.append(x - cell[c : c + 1, :])
            r = lax.rsqrt(d[0] * d[0] + d[1] * d[1] + d[2] * d[2] + 0.5)
            w = (cell[3:4, :] * r) * (r * r)
            for c in range(3):
                f = jnp.sum(w * d[c], axis=1, keepdims=True)
                sums[c, h] = sums[c, h] + jnp.where(here, f, 0.0)
        return carry

    lax.fori_loop(0, lax.div(list_ref[GROUPS + ENV_UNROLL] + (ENV_UNROLL - 1), ENV_UNROLL), body, 0)
    for c in range(3):
        for h in range(step):
            out_ref[pl.ds(h, members, stride=step), c, :] = sums[c, h]


def env(groups, g, cells, grid):
    count = g.shape[0]
    step = GROUPS // LANES
    members = count // step
    return pl.pallas_call(
        functools.partial(env_kernel, grid),
        out_shape=sds((count, 3, LANES)),
        in_specs=[SMEM, VMEM, VMEM],
        out_specs=VMEM,
        scratch_shapes=[
            pltpu.VMEM((3, step, members, LANES), F32),
            pltpu.VMEM((3, step, members, LANES), F32),
        ],
        cost_estimate=pl.CostEstimate(flops=2_000_000, transcendentals=60000, bytes_accessed=200000),
        name="env",
        compiler_params=pltpu.CompilerParams(vmem_limit_bytes=2 << 20),
    )(groups, g, cells)


def kick_kernel(e_ref, f_ref, q_ref, p_ref, v_ref, send_ref, p_out, v_out):
    scale = slow_coupling * q_ref[pl.ds(position(), 1), :]
    count = send_ref.shape[0]
    for c in range(3):
        e = scale * jnp.sum(e_ref[:, c, :], axis=0, keepdims=True)
        v = v_ref[c : c + 1, :] + half_outer * e + 0.5 * inner_dt * f_ref[c : c + 1, :]
        p = p_ref[c : c + 1, :] + inner_dt * v
        v_out[c : c + 1, :] = v
        p_out[c : c + 1, :] = p
        send_ref[:, c, :] = jnp.broadcast_to(p, (count, LANES))


def kick(e, f, q, p, v):
    count = e.shape[0]
    return pl.pallas_call(
        kick_kernel,
        out_shape=(sds((count, 3, LANES)), sds((3, LANES)), sds((3, LANES))),
        in_specs=[VMEM] * 5,
        out_specs=(VMEM,) * 3,
        name="kick",
        compiler_params=pltpu.CompilerParams(vmem_limit_bytes=2 << 20),
    )(e, f, q, p, v)


def last_kick_kernel(e_ref, f_ref, q_ref, v_ref, v_out):
    scale = slow_coupling * q_ref[pl.ds(position(), 1), :]
    for c in range(3):
        e = scale * jnp.sum(e_ref[:, c, :], axis=0, keepdims=True)
        v_out[c : c + 1, :] = (
            v_ref[c : c + 1, :] + 0.5 * inner_dt * f_ref[c : c + 1, :] + half_outer * e
        )


def last_kick(e, f, q, v):
    return pl.pallas_call(
        last_kick_kernel,
        out_shape=sds((3, LANES)),
        in_specs=[VMEM] * 4,
        out_specs=VMEM,
        name="last_kick",
        compiler_params=pltpu.CompilerParams(vmem_limit_bytes=2 << 20),
    )(e, f, q, v)


def slow_kernel(first, row0, nb_ref, tab_ref, vel_ref, *refs):
    earlier = (2 if first else 1) if row0 else 0
    results = 2 if first or row0 else 1
    before, refs = refs[:earlier], refs[earlier:]
    outs, scratch = refs[:results], refs[results:]
    totals = scratch[8]
    if first:
        fetch = pltpu.make_async_copy(vel_ref.at[:, row0 : outs[0].shape[1]], scratch[9], scratch[10])
        fetch.start()
    vel_out = outs[0]
    if first:
        cell_out = outs[1]
    elif row0:
        pos_out = outs[1]
    bufs = [tuple(scratch[0:4]), tuple(scratch[4:8])]
    cell_rows, cell_cols = vel_out.shape[1] - row0, vel_out.shape[2]
    slots = nb_ref.shape[1]
    count = cell_rows * cell_cols
    skip = row0 * cell_cols
    if row0:
        vel_out[:, :row0] = before[0][...]
        if first:
            cell_out[:skip] = before[1][...]
    row8 = lax.broadcasted_iota(jnp.int32, (8, CELL), 0)

    def place(n):
        return lax.shift_right_logical(n, cell_cols.bit_length() - 1), n & (cell_cols - 1)

    def load8(r, c):
        t = tab_ref[r, c]
        return jnp.concatenate([t, jnp.zeros_like(t)], axis=0)

    def distances(n, buf):
        feat, ys, dist, _ = buf
        r, c = place(n)
        left = jnp.transpose(left_rows(load8(r + (row0 + 2), c + 2))).astype(BF16)
        for k in range(slots):
            o = nb_ref[n + row0 * cell_cols, k]
            dr = lax.shift_right_logical(o * 13, 6)
            dc = o - 5 * dr
            y = load8(r + (dr + row0), c + dc)
            y = y + jnp.where(
                row8 == 0, (dr - 2).astype(F32), jnp.where(row8 == 1, (dc - 2).astype(F32), 0.0)
            )
            ys[8 * k : 8 * k + 8] = y
            feat[:, CELL * k : CELL * (k + 1)] = right_rows(y, 0.5).astype(BF16)
        dist[...] = jnp.dot(left, feat[...], preferred_element_type=F32)

    def pairs(buf):
        _, ys, dist, sums = buf
        for g in range(0, CELL // 8, 2):
            at = [slice(8 * (g + h), 8 * (g + h) + 8) for h in range(2)]
            acc = [None, None]
            for k in range(slots):
                y = [jnp.broadcast_to(ys[8 * k + x : 8 * k + x + 1], (8, CELL)) for x in range(4)]
                for h in range(2):
                    i = lax.rsqrt(dist[at[h], CELL * k : CELL * (k + 1)])
                    w = (y[3] * i) * (i * i)
                    f = [w * y[0], w * y[1], w * y[2], w]
                    acc[h] = f if acc[h] is None else [acc[h][x] + f[x] for x in range(4)]
            for h in range(2):
                for x in range(4):
                    sums[x, at[h], :] = acc[h][x]

    def finish(n, buf):
        sums = buf[3]
        for x in range(4):
            totals[n, x : x + 1, :] = jnp.sum(jnp.transpose(sums[x]), axis=0, keepdims=True)

    distances(0, bufs[0])

    def body(i, carry):
        n = 2 * i
        distances(n + 1, bufs[1])
        pairs(bufs[0])
        finish(jnp.maximum(n - 1, 0), bufs[1])
        distances(jnp.minimum(n + 2, count - 1), bufs[0])
        pairs(bufs[1])
        finish(n, bufs[0])
        return carry

    lax.fori_loop(0, count // 2, body, 0)
    finish(count - 1, bufs[1])
    if first:
        fetch.wait()
    rows = slice(row0, row0 + cell_rows)
    inner = (slice(row0 + 2, row0 + 2 + cell_rows), slice(2, 2 + cell_cols))
    charge = tab_ref[inner[0], inner[1], 3, :].reshape(count, CELL)
    for x in range(3):
        p = tab_ref[inner[0], inner[1], x, :].reshape(count, CELL)
        f = slow_coupling * charge * (p * totals[:, 3, :] - totals[:, x, :])
        v = (scratch[9][x] if first else vel_ref[x, rows]) + half_outer * f.reshape(cell_rows, cell_cols, CELL)
        vel_out[x, rows] = v
        if first:
            p = p + outer_dt * v.reshape(count, CELL)
            cell_out[skip:, x, :] = p
        elif row0:
            pos_out[x] = tab_ref[2 : 2 + row0 + cell_rows, inner[1], x, :]
    if first:
        cell_out[skip:, 3, :] = charge


def slow(first, row0, rows, nb, tab, vel, before=()):
    shape = (3, row0 + rows) + vel.shape[2:]
    own = rows * vel.shape[2]
    slots = nb.shape[1]
    out = (sds(shape),)
    if first:
        out += (sds(((row0 + rows) * vel.shape[2], 4, CELL)),)
    elif row0:
        out += (sds(shape),)
    pairs = own * slots * CELL * CELL
    return pl.pallas_call(
        functools.partial(slow_kernel, first, row0),
        out_shape=out,
        in_specs=[SMEM, VMEM, pl.BlockSpec(memory_space=pltpu.HBM) if first else VMEM]
        + [VMEM] * len(before),
        out_specs=(VMEM,) * len(out),
        scratch_shapes=[
            pltpu.VMEM((48, slots * CELL), BF16),
            pltpu.VMEM((8 * slots, CELL), F32),
            pltpu.VMEM((CELL, slots * CELL), F32),
            pltpu.VMEM((4, CELL, CELL), F32),
        ] * 2 + [pltpu.VMEM((own, 4, CELL), F32)]
        + ([pltpu.VMEM((3, rows) + vel.shape[2:], F32), pltpu.SemaphoreType.DMA] if first else []),
        compiler_params=pltpu.CompilerParams(vmem_limit_bytes=4 << 20),
        cost_estimate=pl.CostEstimate(
            flops=10 * pairs, transcendentals=pairs, bytes_accessed=1_000_000
        ),
        name="slow",
    )(nb, tab, in_hbm(vel) if first else vel, *before)


def with_halo(x, sides, width):
    for axis, dim in sides:
        count, length = (lax.axis_size(axis), x.shape[dim])
        up = [(i, (i + 1) % count) for i in range(count)]
        down = [(j, i) for i, j in up]
        last = lax.slice_in_dim(x, length - width, length, axis=dim)
        initial = lax.slice_in_dim(x, 0, width, axis=dim)
        before = lax.ppermute(last, axis, up)
        after = lax.ppermute(initial, axis, down)
        x = jnp.concatenate([before, x, after], axis=dim)
    return x


def exchange(x):
    return lax.all_to_all(x, BOTH, 0, 0)


def per_device(*args):
    return rows_of_lanes(*args)


def rows_of_lanes(
    fast_pos, fast_vel, fast_charge, fast_owner, exclusions,
    slow_pos, slow_vel, slow_charge, neighbours,
):
    row_count, col_count = lax.axis_size("row"), lax.axis_size("col")
    count = row_count * col_count
    piece = fast_pos.shape[1]
    cell_rows, cell_cols = slow_pos.shape[1], slow_pos.shape[2]
    total_cols = cell_cols * col_count

    g = exchange(jnp.broadcast_to(fast_pos[None], (count, 3, piece)))

    q = fast_charge.reshape(count, piece)
    members = fast_charge.shape[0] // GROUPS
    grid = (total_cols, cell_rows, cell_cols)
    table, exm, groups = prep(fast_owner, q, exclusions, members, grid)

    slow_charge, exm = lax.optimization_barrier((slow_charge, exm))
    cells = jnp.concatenate([slow_pos, slow_charge[None]], axis=0).transpose(1, 2, 0, 3)
    sides = (("row", 0), ("col", 1))
    nb = neighbours.reshape(cell_rows * cell_cols, -1)
    half = cell_rows // 2
    tab = with_halo(cells, sides, 2)
    part = ()
    for r0 in (0, half):
        part = slow(True, r0, half, nb, tab, slow_vel, part)
    slow_vel, cells2 = part
    tab2 = with_halo(cells2.reshape(cells.shape), sides, 2)
    part = ()
    for r0 in (0, half):
        part = slow(False, r0, half, nb, tab2, slow_vel, part)
    slow_vel, slow_pos = part

    back = exchange(env(groups, g, cells.reshape(cells2.shape), grid))
    f = fast_only(g, table, exm)
    send, p, v = kick(back, f, q, fast_pos, fast_vel)
    for _ in range(INNER - 1):
        g = exchange(send)
        send, p, v = fast_step(g, table, exm, v)
    g = exchange(send)
    back = exchange(env(groups, g, cells2, grid))
    f = fast_only(g, table, exm)
    v = last_kick(back, f, q, v)
    return (p, v, slow_pos, slow_vel)


def owner_coords(owner, total_cols):
    grid_row = (owner // total_cols).astype(jnp.float32)
    grid_col = (owner % total_cols).astype(jnp.float32)
    return jnp.stack([grid_row, grid_col, jnp.zeros_like(grid_row)])


def pair_fast(pos_a, cell_a, charge_a, exclude_a, pos_b, cell_b, charge_b, index_b):
    delta = pos_a[:, :, None] - pos_b[:, None, :] + (cell_a[:, :, None] - cell_b[:, None, :])
    dist_sq = jnp.sum(delta * delta, axis=0) + 1.0
    inverse = 1.0 / (dist_sq * jnp.sqrt(dist_sq))
    barred = jnp.any(exclude_a[:, :, None] == index_b[None, None, :], axis=1)
    weight = jnp.where(barred, jnp.float32(0.0), charge_a[:, None] * charge_b[None, :] * inverse)
    return fast_coupling * jnp.sum(weight[None] * delta, axis=2)


def slow_cells(own, views, lists):
    force = jnp.zeros((3,) + own.shape[1:], jnp.float32)
    offsets = jnp.arange(25, dtype=jnp.int32)
    for slot in range(lists.shape[-1]):
        chosen = lists[..., slot]
        pick = (chosen[..., None] == offsets).astype(jnp.float32)
        other = jnp.einsum("abo,oxabn->xabn", pick, views, precision=lax.Precision.HIGHEST)
        shift_row = (chosen // 5 - 2).astype(jnp.float32)
        shift_col = (chosen % 5 - 2).astype(jnp.float32)
        shift = jnp.stack([shift_row, shift_col, jnp.zeros_like(shift_row)])
        delta = own[0:3, :, :, :, None] - (other[0:3, :, :, None, :] + shift[:, :, :, None, None])
        dist_sq = jnp.sum(delta * delta, axis=0) + 0.5
        inverse = 1.0 / (dist_sq * jnp.sqrt(dist_sq))
        weight = other[3][:, :, None, :] * inverse
        force = force + jnp.sum(weight[None] * delta, axis=-1)
    return slow_coupling * own[3][None] * force


def fast_from_cells(frac, charge, picked):
    delta = frac[:, :, None] - picked[0:3]
    dist_sq = jnp.sum(delta * delta, axis=0) + 0.5
    inverse = 1.0 / (dist_sq * jnp.sqrt(dist_sq))
    weight = picked[3] * inverse
    return slow_coupling * charge[None, :] * jnp.sum(weight[None] * delta, axis=-1)


def general(
    fast_pos,
    fast_vel,
    fast_charge,
    fast_owner,
    exclusions,
    slow_pos,
    slow_vel,
    slow_charge,
    neighbours,
):
    row_count = lax.axis_size("row")
    col_count = lax.axis_size("col")
    row_index = lax.axis_index("row")
    col_index = lax.axis_index("col")
    flat_index = row_index * col_count + col_index
    piece = fast_pos.shape[1]
    cell_rows = slow_pos.shape[1]
    cell_cols = slow_pos.shape[2]
    total_cols = cell_cols * col_count
    coords = owner_coords(fast_owner, total_cols)
    block_width = col_count * piece
    block_start = row_index * block_width
    rows_cells = lax.dynamic_slice_in_dim(coords, block_start, block_width, 1)
    rows_charge = lax.dynamic_slice_in_dim(fast_charge, block_start, block_width, 0)
    rows_exclude = lax.dynamic_slice_in_dim(exclusions, block_start, block_width, 0)
    column_atoms = (
        (jnp.arange(row_count, dtype=jnp.int32) * col_count + col_index)[:, None] * piece
        + jnp.arange(piece, dtype=jnp.int32)[None, :]
    ).reshape(-1)
    column_cells = jnp.take(coords, column_atoms, axis=1)
    column_charge = jnp.take(fast_charge, column_atoms, axis=0)

    def fast_force(frac):
        rows_pos = lax.all_gather(frac, "col", axis=1, tiled=True)
        cols_pos = lax.all_gather(frac, "row", axis=1, tiled=True)
        partial_force = pair_fast(
            rows_pos,
            rows_cells,
            rows_charge,
            rows_exclude,
            cols_pos,
            column_cells,
            column_charge,
            column_atoms,
        )
        return lax.psum_scatter(partial_force, "col", scatter_dimension=1, tiled=True)

    grid_row = fast_owner // total_cols - row_index * cell_rows
    grid_col = fast_owner % total_cols - col_index * cell_cols
    inside = (grid_row >= 0) & (grid_row < cell_rows) & (grid_col >= 0) & (grid_col < cell_cols)
    local_cell = grid_row * cell_cols + grid_col
    cell_ids = jnp.arange(cell_rows * cell_cols, dtype=jnp.int32)
    select = jnp.where(
        inside[:, None] & (local_cell[:, None] == cell_ids[None, :]),
        jnp.float32(1.0),
        jnp.float32(0.0),
    )

    def slow_both(spos, frac):
        data = jnp.concatenate([spos, slow_charge[None]], axis=0)
        padded = with_halo(data, (("row", 1), ("col", 2)), 2)
        views = jnp.stack(
            [padded[:, o // 5 : o // 5 + cell_rows, o % 5 : o % 5 + cell_cols] for o in range(25)]
        )
        cell_force = slow_cells(data, views, neighbours)
        everyone = lax.all_gather(frac, ("row", "col"), axis=1, tiled=True)
        table = jnp.transpose(data, (1, 2, 0, 3)).reshape(cell_rows * cell_cols, 4 * CELL)
        picked = jnp.dot(
            select, table, precision=lax.Precision.HIGHEST, preferred_element_type=jnp.float32
        )
        picked = jnp.transpose(picked.reshape(fast_charge.shape[0], 4, CELL), (1, 0, 2))
        partial_env = fast_from_cells(everyone, fast_charge, picked)
        summed = lax.psum(partial_env, ("row", "col"))
        own_env = lax.dynamic_slice_in_dim(summed, flat_index * piece, piece, 1)
        return (cell_force, own_env)

    half_outer = 0.5 * outer_dt
    inner_dt = outer_dt / INNER
    fast_acc = fast_force(fast_pos)
    slow_acc, env_acc = slow_both(slow_pos, fast_pos)
    slow_vel = slow_vel + half_outer * slow_acc
    fast_vel = fast_vel + half_outer * env_acc
    for _ in range(INNER):
        fast_vel = fast_vel + 0.5 * inner_dt * fast_acc
        fast_pos = fast_pos + inner_dt * fast_vel
        fast_acc = fast_force(fast_pos)
        fast_vel = fast_vel + 0.5 * inner_dt * fast_acc
    slow_pos = slow_pos + outer_dt * slow_vel
    slow_acc, env_acc = slow_both(slow_pos, fast_pos)
    slow_vel = slow_vel + half_outer * slow_acc
    fast_vel = fast_vel + half_outer * env_acc
    return (fast_pos, fast_vel, slow_pos, slow_vel)


def solution(mesh):
    both = P(None, ("row", "col"))

    def run(*args):
        rows, cols = args[5].shape[1:3]
        powers = all(n & (n - 1) == 0 for n in (rows, cols, *mesh.shape.values()))
        special = args[0].shape[1] == LANES * mesh.size and powers
        step = jax.shard_map(
            per_device if special else general,
            mesh=mesh,
            in_specs=(
                both, both, P(), P(), P(),
                P(None, "row", "col", None), P(None, "row", "col", None),
                P("row", "col", None), P("row", "col", None),
            ),
            out_specs=(both, both, P(None, "row", "col", None), P(None, "row", "col", None)),
            check_vma=False,
        )
        return step(*args)

    return run
```
